128 devices in a mesh: nodes: 16 (over x, z), cols: 8 (over y, core).
Axes of the slice: x: 4, y: 4, z: 4, core: 2. Of those that a mesh axis runs over, the one named last changes fastest.
Arguments:
- node_feats: bfloat16 [32768, 256], P(('nodes', 'cols')), may hold values from -6 to 6
- tile_row: int32 [16, 2816], P('nodes', 'cols'), may hold values from 0 to 15, as said below
- tile_col: int32 [16, 2816], P('nodes', 'cols'), may hold values from 0 to 31
- tile_bits: int32 [16, 2816, 16, 128], P('nodes', 'cols'), may hold values from 0 to 255, as said below
- w_self: bfloat16 [256, 256], replicated, may hold values from -0.375 to 0.375
- w_neigh: bfloat16 [256, 256], replicated, may hold values from -1.5 to 1.5
- bias: float32 [256], replicated, may hold values from -3 to 3
- cotangent: bfloat16 [32768, 256], P(('nodes', 'cols')), may hold values from -6 to 6
Outputs:
- layer_out: bfloat16 [32768, 256], P(('nodes', 'cols'))
- feat_grad: bfloat16 [32768, 256], P(('nodes', 'cols'))
- self_grad: float32 [256, 256], replicated
- neigh_grad: float32 [256, 256], replicated
- bias_grad: float32 [256], replicated
The draws below stay inside these ranges and needn't reach their ends.
Inputs may be any that keep to these rules, and one draw needn't show every extreme that they name: `tile_row`: destination row block of a tile within its nodes group; in every nodes group at least one block carries no tile. `tile_col`: source row block of a tile within its cols index; a block may carry several tiles. `tile_bits`: bit j of word (w, a) of a tile is its edge from destination row a to source column 8 w + j; bits above the eighth are zero; some destination rows have no edge in any tile.
All inputs are finite; a program needn't handle non-finite values.
Results may differ from the reference program's by a relative error of at most 0.0075.
Values may be sent and summed in bfloat16 or wider, within the bound.
No kernel may reach another device: no remote copies, remote signals or barrier semaphores. Data moves between devices by JAX's collectives and lax.ppermute only.
A program may use at most 64 MiB of HBM per device.

```python
import jax
import jax.numpy as jnp
from jax import lax

F = 256
H = 256
SPARSITY = 512
ROWS_DEV = 256
TILE_DEV = 352
NODES = 32768
TILES = 2816
DEST_BLOCKS = 16
SRC_BLOCKS = 32
N_NODES = 16
N_COLS = 8


def permute_blocks(group_key):
    return jax.random.permutation(group_key, DEST_BLOCKS)


def tile_layout(key):
    live_blocks = DEST_BLOCKS - max(1, DEST_BLOCKS // 8)
    first_rank = jax.random.randint(jax.random.fold_in(key, 101), (N_NODES, TILES), 0, live_blocks)
    second_rank = jax.random.randint(jax.random.fold_in(key, 102), (N_NODES, TILES), 0, live_blocks)
    block_rank = jnp.minimum(first_rank, second_rank).astype(jnp.int32)
    group_keys = jax.random.split(jax.random.fold_in(key, 103), N_NODES)
    labels = jax.vmap(permute_blocks)(group_keys).astype(jnp.int32)
    tile_row = jnp.take_along_axis(labels, block_rank, axis=1).astype(jnp.int32)
    isolated = (jax.random.randint(jax.random.fold_in(key, 104), (N_NODES, DEST_BLOCKS, 128), 0, 20) == 0).astype(jnp.int32)
    return (tile_row, isolated)


def draw_tile_row(key, part):
    return tile_layout(key)[0]


def draw_tile_bits(key, part):
    tile_row, isolated = tile_layout(key)
    group_index = jnp.arange(N_NODES, dtype=jnp.int32)[:, None]
    keep_rows = 1 - isolated[group_index, tile_row]
    packed = jnp.zeros((N_NODES, TILES, 16, 128), jnp.int32)
    for bit_index in range(8):
        edge_flags = (jax.random.randint(jax.random.fold_in(key, 200 + bit_index), (N_NODES, TILES, 16, 128), 0, SPARSITY) == 0).astype(jnp.int32)
        packed = packed + edge_flags * keep_rows[:, :, None, :] * 2 ** bit_index
    first_kept = jnp.argmax(keep_rows[:, 0, :], axis=1).astype(jnp.int32)
    row_ids = jnp.arange(128, dtype=jnp.int32)[None, :]
    dense_word = (row_ids == first_kept[:, None]) & (keep_rows[:, 0, :] == 1)
    packed = packed.at[:, 0, 0, :].set(jnp.where(dense_word, 255, packed[:, 0, 0, :]).astype(jnp.int32))
    return packed.astype(jnp.int32)


def touch_ends(entries, stream_key, smallest, largest):
    dims = entries.shape
    index_at = [jax.random.randint(jax.random.fold_in(stream_key, axis), (), 0, dims[axis]) for axis in range(len(dims))]
    entries = entries.at[tuple(index_at)].set(smallest)
    longest = dims.index(max(dims))
    index_at[longest] = (index_at[longest] + 1) % dims[longest]
    return entries.at[tuple(index_at)].set(largest)


def level_of(own_key, extent, cuts, least, high):
    level, own = 1.0, jax.random.fold_in(own_key, 6)
    for position, blocks in cuts:
        draws = jnp.exp(jax.random.uniform(jax.random.fold_in(own, position), (blocks,), jnp.float32, least / len(cuts), high / len(cuts)))
        level = level * jnp.repeat(draws, extent[position] // blocks).reshape([-1 if axis == position else 1 for axis in range(len(extent))])
    return level


def noise(own_key, shape, scale, reach, shards=(), kind=jnp.bfloat16):
    gain = level_of(own_key, shape, shards, -0.22, 0.18) if shards else 1.0
    array = jax.random.normal(own_key, shape, jnp.float32) * scale * gain
    return jnp.minimum(jnp.maximum(array, -reach), reach).astype(kind)


def setup_inputs(seed: int = 0) -> dict:
    arg_keys = jax.random.split(jax.random.key(seed), 9)
    node_feats = noise(arg_keys[0], (NODES, F), 1.0, 6.0, ((0, 128),))
    tile_row = draw_tile_row(jax.random.fold_in(arg_keys[8], 71), 0)
    tile_col = touch_ends(jax.random.randint(arg_keys[2], (N_NODES, TILES), 0, SRC_BLOCKS), jax.random.fold_in(arg_keys[2], 1), 0, SRC_BLOCKS - 1).astype(jnp.int32)
    tile_bits = draw_tile_bits(jax.random.fold_in(arg_keys[8], 71), 0)
    w_self = noise(arg_keys[4], (F, H), F ** -0.5, 0.375)
    w_neigh = noise(arg_keys[5], (F, H), (F // 16) ** -0.5, 1.5)
    bias = noise(arg_keys[6], (H,), 0.5, 3.0, (), jnp.float32)
    cotangent = noise(arg_keys[7], (NODES, H), 1.0, 6.0, ((0, 128),))
    return {"node_feats": node_feats, "tile_row": tile_row, "tile_col": tile_col, "tile_bits": tile_bits, "w_self": w_self, "w_neigh": w_neigh, "bias": bias, "cotangent": cotangent}


def unpack_tiles(packed):
    shifts = jnp.arange(8, dtype=jnp.int32)
    edge_flags = jnp.right_shift(packed[:, :, None, :], shifts[None, None, :, None]) & 1
    return edge_flags.reshape(packed.shape[0], 128, 128)


def reference(node_feats, tile_row, tile_col, tile_bits, w_self, w_neigh, bias, cotangent):
    per_dev = ROWS_DEV // 128
    total_blocks = NODES // 128
    feat_blocks = node_feats.reshape(total_blocks, 128, F)

    def tile_ids(device):
        node_idx = device // N_COLS
        col_idx = device % N_COLS
        first_tile = (col_idx * TILE_DEV).astype(jnp.int32)
        rows_here = lax.dynamic_slice_in_dim(tile_row[node_idx], first_tile, TILE_DEV, 0)
        cols_here = lax.dynamic_slice_in_dim(tile_col[node_idx], first_tile, TILE_DEV, 0)
        packed_here = lax.dynamic_slice_in_dim(tile_bits[node_idx], first_tile, TILE_DEV, 0)
        bits_here = unpack_tiles(packed_here).astype(jnp.float32)
        dest_block = (node_idx * DEST_BLOCKS + rows_here).astype(jnp.int32)
        source_block = (((cols_here // per_dev) * N_COLS + col_idx) * per_dev + cols_here % per_dev).astype(jnp.int32)
        return dest_block, source_block, bits_here

    def forward_step(totals, device):
        summed, degree = totals
        dest_block, source_block, bits_here = tile_ids(device)
        picked = feat_blocks[source_block].astype(jnp.float32)
        products = jnp.einsum('tba,tbf->taf', bits_here, picked)
        summed = summed.at[dest_block].add(products)
        degree = degree.at[dest_block].add(jnp.sum(bits_here, axis=1))
        return (summed, degree), None

    devices = jnp.arange(N_NODES * N_COLS, dtype=jnp.int32)
    initial = (jnp.zeros((total_blocks, 128, F), jnp.float32), jnp.zeros((total_blocks, 128), jnp.float32))
    (summed, degree), _ = lax.scan(forward_step, initial, devices)
    degree = jnp.maximum(degree.reshape(NODES), 1.0)
    neigh_mean = (summed.reshape(NODES, F) / degree[:, None]).astype(jnp.bfloat16)
    preact = jnp.dot(node_feats, w_self, preferred_element_type=jnp.float32) + jnp.dot(neigh_mean, w_neigh, preferred_element_type=jnp.float32) + bias
    sigmoid_pre = jax.nn.sigmoid(preact)
    layer_out = (preact * sigmoid_pre).astype(jnp.bfloat16)
    pre_grad = (cotangent.astype(jnp.float32) * sigmoid_pre * (1.0 + preact * (1.0 - sigmoid_pre))).astype(jnp.bfloat16)
    self_grad = jnp.dot(node_feats.T, pre_grad, preferred_element_type=jnp.float32)
    neigh_grad = jnp.dot(neigh_mean.T, pre_grad, preferred_element_type=jnp.float32)
    bias_grad = jnp.sum(pre_grad.astype(jnp.float32), axis=0)
    mean_grad = (jnp.dot(pre_grad, w_neigh.T, preferred_element_type=jnp.float32) / degree[:, None]).astype(jnp.bfloat16)
    grad_blocks = mean_grad.reshape(total_blocks, 128, F)

    def backward_step(src_grad, device):
        dest_block, source_block, bits_here = tile_ids(device)
        picked = grad_blocks[dest_block].astype(jnp.float32)
        products = jnp.einsum('tba,taf->tbf', bits_here, picked)
        return src_grad.at[source_block].add(products), None

    src_grad, _ = lax.scan(backward_step, jnp.zeros((total_blocks, 128, F), jnp.float32), devices)
    feat_grad = (jnp.dot(pre_grad, w_self.T, preferred_element_type=jnp.float32) + src_grad.reshape(NODES, F)).astype(jnp.bfloat16)
    return (layer_out, feat_grad, self_grad, neigh_grad, bias_grad)
```

```python
import jax
import jax.numpy as jnp
from jax import lax
from jax.experimental import pallas as pl
from jax.experimental.pallas import tpu as pltpu
from jax.sharding import PartitionSpec as P

BF = jnp.bfloat16
F32 = jnp.float32


def build_kernel(row_ref, col_ref, bits_ref, at_ref, deg_ref, acc):
    step = pl.program_id(0)
    tiles = bits_ref.shape[0]
    slots = acc.shape[0]
    dests = at_ref.shape[1] // 128

    @pl.when(step == 0)
    def _():
        deg_ref[...] = jnp.zeros_like(deg_ref)

        def clear(s, carry):
            acc[s] = jnp.zeros((128, 128), F32)
            return carry

        lax.fori_loop(0, slots, clear, 0)
        shifts = lax.broadcasted_iota(jnp.int32, (8, 128), 0)

        def add_tile(t, carry):
            slot = col_ref[t] * dests + row_ref[t]
            for w in range(16):
                word = jnp.broadcast_to(bits_ref[t, w : w + 1, :], (8, 128))
                flag = (jnp.right_shift(word, shifts) & 1).astype(F32)
                acc[slot, 8 * w : 8 * w + 8, :] += flag
            return carry

        lax.fori_loop(0, tiles, add_tile, 0)

    for r in range(dests):
        block = acc[step * dests + r]
        at_ref[:, r * 128 : (r + 1) * 128] = block.astype(BF)
        deg_ref[:, r * 128 : (r + 1) * 128] += jnp.sum(block, axis=0, keepdims=True)


def build(rows, cols, bits, source_blocks, dest_blocks):
    tiles = bits.shape[0]
    return pl.pallas_call(
        build_kernel,
        out_shape=(
            jax.ShapeDtypeStruct((source_blocks * 128, dest_blocks * 128), BF),
            jax.ShapeDtypeStruct((1, dest_blocks * 128), F32),
        ),
        grid_spec=pltpu.PrefetchScalarGridSpec(
            num_scalar_prefetch=2,
            grid=(source_blocks,),
            in_specs=[pl.BlockSpec((tiles, 16, 128), lambda i, *_: (0, 0, 0))],
            out_specs=(
                pl.BlockSpec((128, dest_blocks * 128), lambda i, *_: (i, 0)),
                pl.BlockSpec((1, dest_blocks * 128), lambda i, *_: (0, 0)),
            ),
            scratch_shapes=[pltpu.VMEM((source_blocks * dest_blocks, 128, 128), F32)],
        ),
        compiler_params=pltpu.CompilerParams(vmem_limit_bytes=56 << 20),
        cost_estimate=pl.CostEstimate(flops=0, bytes_accessed=60 << 20, transcendentals=0),
        name="build",
    )(rows, cols, bits)


def forward_kernel(place_ref, xt_ref, at_ref, keep_ref, give_ref, acc):
    step = pl.program_id(0)
    width = xt_ref.shape[2]
    part = jnp.dot(xt_ref[0], at_ref[0:width, :], preferred_element_type=F32)
    for k in range(1, xt_ref.shape[0]):
        part += jnp.dot(
            xt_ref[k], at_ref[k * width : (k + 1) * width, :], preferred_element_type=F32
        )

    @pl.when(step == 0)
    def _():
        acc[...] = part

    @pl.when(step > 0)
    def _():
        acc[...] += part

    @pl.when(step == pl.num_programs(0) - 1)
    def _():
        y = place_ref[0]
        core = place_ref[1]
        for k in range(4):
            chunk = 2 * lax.rem(y + k, 4)
            mine = pl.multiple_of((chunk + core) * width, width)
            other = pl.multiple_of((chunk + 1 - core) * width, width)
            keep_ref[k] = acc[:, pl.ds(mine, width)]
            give_ref[k] = acc[:, pl.ds(other, width)].astype(BF)


def forward(place, xt, at):
    nodes, width_in, rows = xt.shape
    dest = at.shape[1]
    per = 2
    return pl.pallas_call(
        forward_kernel,
        out_shape=(
            jax.ShapeDtypeStruct((4, width_in, rows), F32),
            jax.ShapeDtypeStruct((4, width_in, rows), BF),
        ),
        grid_spec=pltpu.PrefetchScalarGridSpec(
            num_scalar_prefetch=1,
            grid=(nodes // per,),
            in_specs=[
                pl.BlockSpec((per, width_in, rows), lambda i, *_: (i, 0, 0)),
                pl.BlockSpec((per * rows, dest), lambda i, *_: (i, 0)),
            ],
            out_specs=(
                pl.BlockSpec((4, width_in, rows), lambda i, *_: (0, 0, 0)),
                pl.BlockSpec((4, width_in, rows), lambda i, *_: (0, 0, 0)),
            ),
            scratch_shapes=[pltpu.VMEM((width_in, dest), F32)],
        ),
        cost_estimate=pl.CostEstimate(
            flops=2 * nodes * rows * dest * width_in, bytes_accessed=20 << 20, transcendentals=0
        ),
        name="forward",
    )(place, xt, at)


def backward_kernel(g_ref, at_ref, out_ref):
    out_ref[...] = jnp.dot(at_ref[...], g_ref[...], preferred_element_type=F32).astype(BF)


def backward(g, at):
    source, dest = at.shape
    width = g.shape[1]
    rows = 512
    return pl.pallas_call(
        backward_kernel,
        out_shape=jax.ShapeDtypeStruct((source, width), BF),
        grid=(source // rows,),
        in_specs=[
            pl.BlockSpec((dest, width), lambda i: (0, 0)),
            pl.BlockSpec((rows, dest), lambda i: (i, 0)),
        ],
        out_specs=pl.BlockSpec((rows, width), lambda i: (i, 0)),
        cost_estimate=pl.CostEstimate(
            flops=2 * source * dest * width, bytes_accessed=20 << 20, transcendentals=0
        ),
        name="backward",
    )(g, at)


def dot_on(a, b, da, db):
    return lax.dot_general(a, b, (((da,), (db,)), ((), ())), preferred_element_type=F32)


def middle_kernel(
    own_ref, r1_ref, r2_ref, r3_ref, deg_ref, x_ref, ws_ref, wn_ref, bias_ref, cot_ref,
    out_ref, pre_ref, mean_ref, grad_ref,
):
    degree = jnp.maximum(jnp.sum(deg_ref[...], axis=0, keepdims=True), 1.0)
    summed = own_ref[0] + r1_ref[...].astype(F32) + r2_ref[...].astype(F32)
    summed += r3_ref[...].astype(F32)
    mean_t = (summed / degree).astype(BF)
    mean_ref[...] = mean_t
    preact = (
        jnp.dot(x_ref[...], ws_ref[...], preferred_element_type=F32)
        + dot_on(mean_t, wn_ref[...], 0, 0)
        + bias_ref[...]
    )
    sig = 1.0 / (1.0 + jnp.exp(-preact))
    out_ref[...] = (preact * sig).astype(BF)
    pre_grad = (cot_ref[...].astype(F32) * sig * (1.0 + preact * (1.0 - sig))).astype(BF)
    pre_ref[...] = pre_grad
    grad_t = dot_on(wn_ref[...], pre_grad, 1, 1) / degree
    grad_ref[...] = grad_t.T.astype(BF)


def middle(own, r1, r2, r3, deg, x, ws, wn, bias, cot):
    n = x.shape[0]
    shape = jax.ShapeDtypeStruct((n, n), BF)
    return pl.pallas_call(
        middle_kernel,
        out_shape=(shape, shape, shape, shape),
        cost_estimate=pl.CostEstimate(
            flops=6 * n * n * n, bytes_accessed=2 << 20, transcendentals=n * n
        ),
        name="middle",
    )(own, r1, r2, r3, deg, x, ws, wn, bias, cot)


def weights_kernel(x_ref, pre_ref, mean_ref, ws_ref, part_ref, self_ref):
    pre_grad = pre_ref[...]
    self_grad = dot_on(x_ref[...], pre_grad, 0, 0)
    neigh_grad = jnp.dot(mean_ref[...], pre_grad, preferred_element_type=F32)
    bias_grad = jnp.sum(pre_grad.astype(F32), axis=0, keepdims=True)
    first = lax.broadcasted_iota(jnp.int32, (8, 1), 0) == 0
    bias_rows = jnp.where(first, bias_grad, 0.0)
    for c in range(8):
        grad = self_grad if c < 4 else neigh_grad
        part_ref[c, 0:64, :] = grad[(c % 4) * 64 : (c % 4) * 64 + 64, :]
        part_ref[c, 64:72, :] = bias_rows
    self_ref[...] = dot_on(pre_grad, ws_ref[...], 1, 1)


def weights(x, pre_grad, mean_t, ws):
    n = x.shape[0]
    return pl.pallas_call(
        weights_kernel,
        out_shape=(
            jax.ShapeDtypeStruct((8, 72, n), F32),
            jax.ShapeDtypeStruct((n, n), F32),
        ),
        cost_estimate=pl.CostEstimate(
            flops=6 * n * n * n, bytes_accessed=2 << 20, transcendentals=0
        ),
        name="weights",
    )(x, pre_grad, mean_t, ws)


def finish_kernel(parts_ref, self_ref, out_ref):
    total = self_ref[...]
    for k in range(parts_ref.shape[0]):
        total += parts_ref[k].astype(F32)
    out_ref[...] = total.astype(BF)


def finish(parts, self_part):
    return pl.pallas_call(
        finish_kernel,
        out_shape=jax.ShapeDtypeStruct(self_part.shape, BF),
        cost_estimate=pl.CostEstimate(flops=1 << 20, bytes_accessed=2 << 20, transcendentals=0),
        name="finish",
    )(parts, self_part)


def swap(x, axis):
    return lax.all_to_all(x, axis, 0, 0, tiled=True)


def spread(x, axis):
    count = lax.axis_size(axis)
    return swap(jnp.broadcast_to(x[None], (count, *x.shape)), axis)


def along_y(step):
    return [(2 * y + c, 2 * ((y + step) % 4) + c) for y in range(4) for c in range(2)]


def shards(node_feats, tile_row, tile_col, tile_bits, w_self, w_neigh, bias, cotangent):
    nodes = lax.axis_size("nodes")
    cols = lax.axis_size("cols")
    rows_dev, width = node_feats.shape
    me = lax.axis_index("cols")
    y, core = me // 2, me % 2
    place = jnp.stack([y, core]).astype(jnp.int32)
    partner = [(i, i ^ 1) for i in range(8)]

    xt_all = spread(node_feats.T, "nodes")
    at, degree = build(
        tile_row[0], tile_col[0], tile_bits[0], nodes * rows_dev // 128, cols * rows_dev // 128
    )
    degrees = swap(degree.reshape(cols, rows_dev), "cols")

    keep, give = forward(place, xt_all, at)
    taken = lax.ppermute(give, "cols", partner)
    both = keep + taken.astype(F32)
    send = both[1:].astype(BF)
    got = [lax.ppermute(send[k - 1], "cols", along_y(k)) for k in (1, 2, 3)]
    layer_out, pre_grad, mean_t, mean_grad = middle(
        both[:1], *got, degrees, node_feats, w_self, w_neigh, bias.reshape(1, -1), cotangent
    )
    others = [mean_grad] + [lax.ppermute(mean_grad, "cols", along_y(k)) for k in (1, 2, 3)]
    same_core = jnp.stack(others)
    other_core = lax.ppermute(same_core, "cols", partner)
    pair = jnp.where(core == 0, jnp.stack([same_core, other_core], 1), jnp.stack([other_core, same_core], 1))
    order = (y - jnp.arange(4)) % 4
    grads = pair[order].reshape(cols * rows_dev, width)

    part, self_part = weights(node_feats, pre_grad, mean_t, w_self)
    part = jnp.sum(swap(part, "cols"), axis=0)
    bias_sum = part[64:72]
    fine = jnp.concatenate(
        [part[:64].reshape(nodes, 4, width), jnp.broadcast_to(bias_sum[None, :4], (nodes, 4, width))], 1
    )
    fine = jnp.sum(swap(fine, "nodes"), axis=0)
    coarse = spread(fine, "nodes")
    bias_grad = coarse[0, 4]
    coarse = coarse[:, :4].reshape(64, width)
    whole = spread(coarse, "cols").reshape(2, width, width)

    src = backward(grads, at)
    parts = swap(src.reshape(nodes, rows_dev, width), "nodes")
    feat_grad = finish(parts, self_part)
    return (layer_out, feat_grad, whole[0], whole[1], bias_grad)


def solution(mesh):
    return jax.shard_map(
        shards,
        mesh=mesh,
        in_specs=(
            P(("nodes", "cols"), None),
            P("nodes", "cols"),
            P("nodes", "cols"),
            P("nodes", "cols", None, None),
            P(),
            P(),
            P(),
            P(("nodes", "cols"), None),
        ),
        out_specs=(P(("nodes", "cols"), None), P(("nodes", "cols"), None), P(), P(), P()),
        check_vma=False,
    )
```

```python
import jax
import jax.numpy as jnp
from jax import lax
from jax.experimental import pallas as pl
from jax.experimental.pallas import tpu as pltpu
from jax.sharding import PartitionSpec as P

BF = jnp.bfloat16
F32 = jnp.float32
EXACT = 256


def params(mib):
    return pltpu.CompilerParams(vmem_limit_bytes=mib << 20)


def in_hbm(shape, kind):
    return pltpu.HBM(shape, kind)


def cost(flops, moved, transcendentals=0):
    return pl.CostEstimate(flops=flops, bytes_accessed=moved, transcendentals=transcendentals)


def prepare_kernel(x_ref, out_ref, flipped):
    @pl.when(pl.program_id(0) == 0)
    def _():
        flipped[...] = x_ref[...].T

    for k in range(out_ref.shape[0]):
        out_ref[k] = flipped[...]


def prepare(x, copies):
    rows, width = x.shape
    per = 4
    return pl.pallas_call(
        prepare_kernel,
        out_shape=in_hbm((copies, width, rows), BF),
        grid=(copies // per,),
        in_specs=[pl.BlockSpec((rows, width), lambda i: (0, 0))],
        out_specs=pl.BlockSpec((per, width, rows), lambda i: (i, 0, 0)),
        scratch_shapes=[pltpu.VMEM((width, rows), BF)],
        compiler_params=params(8),
        cost_estimate=cost(0, 2 << 20),
        name="prepare",
    )(x)


def build_kernel(row_ref, col_ref, bits_ref, at_ref, deg_ref, deg8, count, spill):
    sources = at_ref.shape[0] - 1
    dests = at_ref.shape[1]
    tiles = bits_ref.shape[0]
    for r in range(dests):
        deg8[r] = jnp.zeros((8, 128), F32)

    def clear(k, carry):
        for r in range(dests):
            at_ref[k, r] = jnp.zeros((128, 128), BF)
            count[k * dests + r] = 0
        return carry

    lax.fori_loop(0, sources, clear, 0)
    at_ref[sources, 0] = jnp.zeros((128, 128), BF)
    spill[0] = -1
    shifts = lax.broadcasted_iota(jnp.int32, (8, 128), 0)

    def add_tile(t, carry):
        row = row_ref[0, t]
        col = col_ref[0, t]
        slot = col * dests + row
        seen = count[slot]
        count[slot] = seen + 1
        full = seen >= EXACT
        spill[0] = jnp.where(full, slot, spill[0])
        to_col = jnp.where(full, sources, col)
        to_row = jnp.where(full, 0, row)
        total = None
        for i in range(8):
            flags = []
            for w in (2 * i, 2 * i + 1):
                word = jnp.broadcast_to(bits_ref[t, w : w + 1, :], (8, 128))
                flags.append((jnp.right_shift(word, shifts) & 1).astype(F32))
            pair = flags[0] + flags[1]
            total = pair if total is None else total + pair
            at_ref[to_col, to_row, 16 * i : 16 * i + 16, :] += jnp.concatenate(flags, 0).astype(BF)
        deg8[row] += total
        return carry

    lax.fori_loop(0, tiles, add_tile, 0, unroll=2)

    @pl.when(spill[0] >= 0)
    def _():
        slot = spill[0]
        col = lax.div(slot, dests)
        row = lax.rem(slot, dests)
        whole = at_ref[col, row].astype(F32) + at_ref[sources, 0].astype(F32)
        at_ref[col, row] = whole.astype(BF)

    for r in range(dests):
        deg_ref[:, r * 128 : (r + 1) * 128] = jnp.sum(deg8[r], axis=0, keepdims=True)


def build(rows, cols, bits, sources, dests):
    assert bits.shape[0] <= 2 * EXACT
    smem = pl.BlockSpec(memory_space=pltpu.SMEM)
    vmem = pl.BlockSpec(memory_space=pltpu.VMEM)
    return pl.pallas_call(
        build_kernel,
        out_shape=(
            in_hbm((sources + 1, dests, 128, 128), BF),
            jax.ShapeDtypeStruct((1, dests * 128), F32),
        ),
        in_specs=[smem, smem, vmem],
        out_specs=(vmem, vmem),
        scratch_shapes=[
            pltpu.VMEM((dests, 8, 128), F32),
            pltpu.SMEM((sources * dests,), jnp.int32),
            pltpu.SMEM((1,), jnp.int32),
        ],
        compiler_params=params(24),
        cost_estimate=cost(0, 30 << 20),
        name="build",
    )(rows, cols, bits)


def forward_kernel(place_ref, xt_ref, at_ref, out_ref, joined):
    @pl.when(pl.program_id(0) == 0)
    def _():
        for n in range(xt_ref.shape[0]):
            rows = xt_ref.shape[2]
            joined[:, n * rows : (n + 1) * rows] = xt_ref[n]

    blocks = [
        jnp.concatenate([at_ref[k, r] for r in range(at_ref.shape[1])], axis=1)
        for k in range(at_ref.shape[0])
    ]
    part = jnp.dot(joined[...], jnp.concatenate(blocks, axis=0), preferred_element_type=F32)
    out_ref[0] = part.astype(out_ref.dtype)


def forward(place, xt, at, kind):
    nodes, width, rows = xt.shape
    sources = at.shape[0] - 1
    per = rows // 128

    def chunk(j, place):
        return (0, 2 * lax.rem(place[0] + j, 4) + place[1], 0, 0)

    return pl.pallas_call(
        forward_kernel,
        out_shape=jax.ShapeDtypeStruct((4, width, rows), kind),
        grid_spec=pltpu.PrefetchScalarGridSpec(
            num_scalar_prefetch=1,
            grid=(4,),
            in_specs=[
                pl.BlockSpec((nodes, width, rows), lambda j, *_: (0, 0, 0)),
                pl.BlockSpec((sources, per, 128, 128), chunk),
            ],
            out_specs=pl.BlockSpec((1, width, rows), lambda j, *_: (j, 0, 0)),
            scratch_shapes=[pltpu.VMEM((width, nodes * rows), BF)],
        ),
        compiler_params=params(50),
        cost_estimate=cost(8 * nodes * rows * rows * width, 10 << 20),
        name="forward",
    )(place, xt, at)


def backward_kernel(place_ref, *refs):
    parts, at_ref, out_ref, grads = refs[:8], refs[8], refs[9], refs[10]
    rows = parts[0].shape[0]

    @pl.when(pl.program_id(0) == 0)
    def _():
        for k in range(4):
            chunk = 2 * lax.rem(place_ref[0] + 4 - k, 4)
            own = pl.multiple_of((chunk + place_ref[1]) * rows, rows)
            other = pl.multiple_of((chunk + 1 - place_ref[1]) * rows, rows)
            grads[pl.ds(own, rows), :] = parts[k][...]
            grads[pl.ds(other, rows), :] = parts[4 + k][...]

    for k in range(at_ref.shape[0]):
        block = jnp.concatenate([at_ref[k, r] for r in range(at_ref.shape[1])], axis=1)
        got = jnp.dot(block, grads[...], preferred_element_type=F32)
        out_ref[k * 128 : (k + 1) * 128, :] = got.astype(BF)


def backward(place, parts, at):
    sources, dests = at.shape[0] - 1, at.shape[1]
    rows, width = parts[0].shape
    per = 8
    return pl.pallas_call(
        backward_kernel,
        out_shape=in_hbm((sources * 128, width), BF),
        grid_spec=pltpu.PrefetchScalarGridSpec(
            num_scalar_prefetch=1,
            grid=(sources // per,),
            in_specs=[pl.BlockSpec((rows, width), lambda i, *_: (0, 0))] * 8
            + [pl.BlockSpec((per, dests, 128, 128), lambda i, *_: (i, 0, 0, 0))],
            out_specs=pl.BlockSpec((per * 128, width), lambda i, *_: (i, 0)),
            scratch_shapes=[pltpu.VMEM((dests * 128, width), BF)],
        ),
        compiler_params=params(50),
        cost_estimate=cost(2 * sources * 128 * dests * 128 * width, 20 << 20),
        name="backward",
    )(place, *parts, at)


def dot_on(a, b, da, db):
    return lax.dot_general(a, b, (((da,), (db,)), ((), ())), preferred_element_type=F32)


def middle_kernel(
    keep_ref, taken_ref, r1_ref, r2_ref, r3_ref, deg_ref, x_ref, ws_ref, wn_ref, bias_ref, cot_ref,
    out_ref, pre_ref, mean_ref, grad_ref,
):
    degree = jnp.maximum(deg_ref[...], 1.0)
    summed = keep_ref[0] + taken_ref[0].astype(F32) + r1_ref[...].astype(F32)
    summed += r2_ref[...].astype(F32) + r3_ref[...].astype(F32)
    mean_t = (summed / degree).astype(BF)
    mean_ref[...] = mean_t
    preact = (
        jnp.dot(x_ref[...], ws_ref[...], preferred_element_type=F32)
        + dot_on(mean_t, wn_ref[...], 0, 0)
        + bias_ref[...]
    )
    sig = 1.0 / (1.0 + jnp.exp(-preact))
    out_ref[...] = (preact * sig).astype(BF)
    pre_grad = (cot_ref[...].astype(F32) * sig * (1.0 + preact * (1.0 - sig))).astype(BF)
    pre_ref[...] = pre_grad
    grad_t = dot_on(wn_ref[...], pre_grad, 1, 1) / degree
    grad_ref[...] = grad_t.T.astype(BF)


def middle(keep, taken, got, deg, x, ws, wn, bias, cot):
    n = x.shape[0]
    shape = jax.ShapeDtypeStruct((n, n), BF)
    whole = pl.BlockSpec((n, n), lambda i: (0, 0))
    first = pl.BlockSpec((1, n, n), lambda i: (0, 0, 0))
    return pl.pallas_call(
        middle_kernel,
        out_shape=(shape, shape, shape, shape),
        grid=(1,),
        in_specs=[first, first, whole, whole, whole]
        + [pl.BlockSpec(deg.shape, lambda i: (0, 0)), whole, whole, whole]
        + [pl.BlockSpec((1, n), lambda i: (0, 0)), whole],
        out_specs=(whole, whole, whole, whole),
        compiler_params=params(16),
        cost_estimate=cost(6 * n * n * n, 2 << 20, n * n),
        name="middle",
    )(keep, taken, *got, deg, x, ws, wn, bias, cot)


def weights_kernel(x_ref, pre_ref, mean_ref, ws_ref, part_ref, self_ref):
    pre_grad = pre_ref[...]
    self_grad = dot_on(x_ref[...], pre_grad, 0, 0)
    neigh_grad = jnp.dot(mean_ref[...], pre_grad, preferred_element_type=F32)
    bias_grad = jnp.sum(pre_grad.astype(F32), axis=0, keepdims=True)
    first = lax.broadcasted_iota(jnp.int32, (8, 1), 0) == 0
    bias_rows = jnp.where(first, bias_grad, 0.0)
    for c in range(16):
        grad = self_grad if c < 8 else neigh_grad
        part_ref[c, 0:32, :] = grad[(c % 8) * 32 : (c % 8) * 32 + 32, :]
        part_ref[c, 32:40, :] = bias_rows
    self_ref[...] = dot_on(pre_grad, ws_ref[...], 1, 1)


def weights(x, pre_grad, mean_t, ws):
    n = x.shape[0]
    return pl.pallas_call(
        weights_kernel,
        out_shape=(
            in_hbm((16, 40, n), F32),
            jax.ShapeDtypeStruct((n, n), F32),
        ),
        compiler_params=params(16),
        cost_estimate=cost(6 * n * n * n, 2 << 20),
        name="weights",
    )(x, pre_grad, mean_t, ws)


def finish_kernel(parts_ref, self_ref, out_ref):
    total = self_ref[...]
    for k in range(parts_ref.shape[0]):
        total += parts_ref[k].astype(F32)
    out_ref[...] = total.astype(BF)


def finish(parts, self_part):
    return pl.pallas_call(
        finish_kernel,
        out_shape=jax.ShapeDtypeStruct(self_part.shape, BF),
        compiler_params=params(16),
        cost_estimate=cost(1 << 20, 2 << 20),
        name="finish",
    )(parts, self_part)


def assemble_kernel(spot_ref, *refs):
    planes, outs = refs[:4], refs[4:]
    rows = 2 * outs[0].shape[0] // 16
    for kx in range(4):
        x = lax.rem(spot_ref[0] + 4 - kx, 4)
        for kz in range(4):
            z = lax.rem(spot_ref[1] + 4 - kz, 4)
            place = pl.multiple_of((4 * lax.rem(x, 2) + z) * rows, rows)
            for half in range(2):

                @pl.when(lax.div(x, 2) == half)
                def _():
                    outs[half][pl.ds(place, rows), :] = planes[kx][kz, 0:rows, :]


def assemble(spot, planes):
    width = planes[0].shape[2]
    shape = jax.ShapeDtypeStruct((width, width), F32)
    vmem = pl.BlockSpec(memory_space=pltpu.VMEM)
    return pl.pallas_call(
        assemble_kernel,
        out_shape=(shape, shape),
        in_specs=[pl.BlockSpec(memory_space=pltpu.SMEM)] + [vmem] * 4,
        out_specs=(vmem, vmem),
        compiler_params=params(16),
        cost_estimate=cost(0, 2 << 20),
        name="assemble",
    )(spot, *planes)


def swap(x, axis):
    return lax.all_to_all(x, axis, 0, 0, tiled=True)


def along_y(step):
    return [(2 * y + c, 2 * ((y + step) % 4) + c) for y in range(4) for c in range(2)]


def send_node(x, dx, dz):
    moves = [
        (4 * i + j, 4 * ((i + dx) % 4) + (j + dz) % 4) for i in range(4) for j in range(4)
    ]
    return lax.ppermute(x, "nodes", moves)


PARTNER = [(i, i ^ 1) for i in range(8)]


def send_y(x, step):
    return lax.ppermute(x, "cols", along_y(step))


def send_core(x):
    return lax.ppermute(x, "cols", PARTNER)


def shards(node_feats, tile_row, tile_col, tile_bits, w_self, w_neigh, bias, cotangent):
    nodes = lax.axis_size("nodes")
    cols = lax.axis_size("cols")
    rows_dev, width = node_feats.shape
    me = lax.axis_index("cols")
    y, core = me // 2, me % 2
    mine = jnp.stack([y, core]).astype(jnp.int32)
    theirs = jnp.stack([y, 1 - core]).astype(jnp.int32)
    node = lax.axis_index("nodes")
    spot = jnp.stack([node // 4, node % 4]).astype(jnp.int32)

    ready = prepare(node_feats, nodes)
    tile_row, tile_col, ready = lax.optimization_barrier((tile_row, tile_col, ready))
    xt_all = swap(ready, "nodes")
    at, degree = build(
        tile_row, tile_col, tile_bits[0], nodes * rows_dev // 128, cols * rows_dev // 128
    )
    degree = degree + send_core(degree)
    degree = degree + send_y(degree, 1) + send_y(degree, 2) + send_y(degree, 3)
    degree = lax.dynamic_slice_in_dim(degree, me * rows_dev, rows_dev, 1)
    xt_all, degree, mine, theirs = lax.optimization_barrier((xt_all, degree, mine, theirs))

    give = forward(theirs, xt_all, at, BF)
    taken = send_core(give)
    keep = forward(mine, xt_all, at, F32)
    both = (keep[1:] + taken[1:].astype(F32)).astype(BF)
    got = [send_y(both[k - 1], k) for k in (1, 2, 3)]
    layer_out, pre_grad, mean_t, mean_grad = middle(
        keep, taken, got, degree, node_feats, w_self, w_neigh, bias.reshape(1, -1), cotangent
    )
    same_core = [mean_grad] + [send_y(mean_grad, k) for k in (1, 2, 3)]
    other_core = [send_core(g) for g in same_core]

    part, self_part = weights(node_feats, pre_grad, mean_t, w_self)
    part = jnp.sum(swap(part, "nodes"), axis=0)

    src = backward(mine, same_core + other_core, at)
    src, part = lax.optimization_barrier((src, part))
    parts = swap(src.reshape(nodes, rows_dev, width), "nodes")

    part = part + send_core(part)
    part = part + send_y(part, 1) + send_y(part, 2) + send_y(part, 3)
    line = jnp.stack([part] + [send_node(part, 0, k) for k in (1, 2, 3)])
    plane = [line] + [send_node(line, k, 0) for k in (1, 2, 3)]
    self_grad, neigh_grad = assemble(spot, plane)
    bias_grad = part[32]

    feat_grad = finish(parts, self_part)
    return (layer_out, feat_grad, self_grad, neigh_grad, bias_grad)


def solution(mesh):
    return jax.shard_map(
        shards,
        mesh=mesh,
        in_specs=(
            P(("nodes", "cols"), None),
            P("nodes", "cols"),
            P("nodes", "cols"),
            P("nodes", "cols", None, None),
            P(),
            P(),
            P(),
            P(("nodes", "cols"), None),
        ),
        out_specs=(P(("nodes", "cols"), None), P(("nodes", "cols"), None), P(), P(), P()),
        check_vma=False,
    )
```

```python
import jax
import jax.numpy as jnp
from jax import lax
from jax.experimental import pallas as pl
from jax.experimental.pallas import tpu as pltpu
from jax.sharding import PartitionSpec as P

BF = jnp.bfloat16
F32 = jnp.float32
EXACT = 256


def params(mib):
    return pltpu.CompilerParams(vmem_limit_bytes=mib << 20)


def in_hbm(shape, kind):
    return pltpu.HBM(shape, kind)


def cost(flops, moved, transcendentals=0):
    return pl.CostEstimate(flops=flops, bytes_accessed=moved, transcendentals=transcendentals)


def prepare_kernel(x_ref, out_ref):
    out_ref[...] = x_ref[...].T


def prepare(x):
    return pl.pallas_call(
        prepare_kernel,
        out_shape=jax.ShapeDtypeStruct(x.shape[::-1], BF),
        compiler_params=params(8),
        cost_estimate=cost(0, 1 << 18),
        name="prepare",
    )(x)


def build_kernel(row_ref, col_ref, bits_ref, at_ref, deg_ref, deg8, count, spill):
    sources = at_ref.shape[0] - 1
    dests = at_ref.shape[1]
    tiles = bits_ref.shape[0]
    for r in range(dests):
        deg8[r] = jnp.zeros((8, 128), F32)

    def clear(k, carry):
        for r in range(dests):
            at_ref[k, r] = jnp.zeros((128, 128), BF)
            count[k * dests + r] = 0
        return carry

    lax.fori_loop(0, sources, clear, 0)
    at_ref[sources, 0] = jnp.zeros((128, 128), BF)
    spill[0] = -1
    shifts = lax.broadcasted_iota(jnp.int32, (8, 128), 0)

    def add_tile(t, carry):
        row = row_ref[0, t]
        col = col_ref[0, t]
        slot = col * dests + row
        seen = count[slot]
        count[slot] = seen + 1
        full = seen >= EXACT
        spill[0] = jnp.where(full, slot, spill[0])
        to_col = jnp.where(full, sources, col)
        to_row = jnp.where(full, 0, row)
        total = None
        for i in range(8):
            flags = []
            for w in (2 * i, 2 * i + 1):
                word = jnp.broadcast_to(bits_ref[t, w : w + 1, :], (8, 128))
                flags.append((jnp.right_shift(word, shifts) & 1).astype(F32))
            pair = flags[0] + flags[1]
            total = pair if total is None else total + pair
            at_ref[to_col, to_row, 16 * i : 16 * i + 16, :] += jnp.concatenate(flags, 0).astype(BF)
        deg8[row] += total
        return carry

    lax.fori_loop(0, tiles, add_tile, 0, unroll=2)

    @pl.when(spill[0] >= 0)
    def _():
        slot = spill[0]
        col = lax.div(slot, dests)
        row = lax.rem(slot, dests)
        whole = at_ref[col, row].astype(F32) + at_ref[sources, 0].astype(F32)
        at_ref[col, row] = whole.astype(BF)

    for r in range(dests):
        deg_ref[:, r * 128 : (r + 1) * 128] = jnp.sum(deg8[r], axis=0, keepdims=True)


def build(rows, cols, bits, sources, dests):
    assert bits.shape[0] <= 2 * EXACT
    smem = pl.BlockSpec(memory_space=pltpu.SMEM)
    vmem = pl.BlockSpec(memory_space=pltpu.VMEM)
    return pl.pallas_call(
        build_kernel,
        out_shape=(
            jax.ShapeDtypeStruct((sources + 1, dests, 128, 128), BF),
            jax.ShapeDtypeStruct((1, dests * 128), F32),
        ),
        in_specs=[smem, smem, vmem],
        out_specs=(vmem, vmem),
        scratch_shapes=[
            pltpu.VMEM((dests, 8, 128), F32),
            pltpu.SMEM((sources * dests,), jnp.int32),
            pltpu.SMEM((1,), jnp.int32),
        ],
        compiler_params=params(24),
        cost_estimate=cost(0, 30 << 20),
        name="build",
    )(rows, cols, bits)


def forward_kernel(place_ref, *refs):
    planes, at_ref, out_ref, joined = refs[:4], refs[4], refs[5], refs[6]
    rows = planes[0].shape[2]

    @pl.when(pl.program_id(0) == 0)
    def _():
        for kx in range(4):
            x = lax.rem(place_ref[2] + 4 - kx, 4)
            for kz in range(4):
                n = 4 * x + lax.rem(place_ref[3] + 4 - kz, 4)
                joined[:, pl.ds(pl.multiple_of(n * rows, rows), rows)] = planes[kz][kx]

    blocks = [
        jnp.concatenate([at_ref[k, r] for r in range(at_ref.shape[1])], axis=1)
        for k in range(at_ref.shape[0])
    ]
    part = jnp.dot(joined[...], jnp.concatenate(blocks, axis=0), preferred_element_type=F32)
    out_ref[0] = part.astype(out_ref.dtype)


def forward(place, planes, at, kind):
    lines, width, rows = planes[0].shape
    sources = at.shape[0] - 1
    per = rows // 128

    def chunk(j, place):
        return (0, 2 * lax.rem(place[0] + j, 4) + place[1], 0, 0)

    return pl.pallas_call(
        forward_kernel,
        out_shape=jax.ShapeDtypeStruct((4, width, rows), kind),
        grid_spec=pltpu.PrefetchScalarGridSpec(
            num_scalar_prefetch=1,
            grid=(4,),
            in_specs=[pl.BlockSpec((lines, width, rows), lambda j, *_: (0, 0, 0))] * 4
            + [pl.BlockSpec((sources, per, 128, 128), chunk)],
            out_specs=pl.BlockSpec((1, width, rows), lambda j, *_: (j, 0, 0)),
            scratch_shapes=[pltpu.VMEM((width, sources * 128), BF)],
        ),
        compiler_params=params(20),
        cost_estimate=cost(8 * sources * 128 * rows * width, 10 << 20),
        name="forward",
    )(place, *planes, at)


def backward_kernel(place_ref, *refs):
    parts, at_ref, out_ref, grads = refs[:8], refs[8], refs[9], refs[10]
    rows = parts[0].shape[0]

    @pl.when(pl.program_id(0) == 0)
    def _():
        for k in range(4):
            chunk = 2 * lax.rem(place_ref[0] + 4 - k, 4)
            own = pl.multiple_of((chunk + place_ref[1]) * rows, rows)
            other = pl.multiple_of((chunk + 1 - place_ref[1]) * rows, rows)
            grads[pl.ds(own, rows), :] = parts[k][...]
            grads[pl.ds(other, rows), :] = parts[4 + k][...]

    for k in range(at_ref.shape[0]):
        block = jnp.concatenate([at_ref[k, r] for r in range(at_ref.shape[1])], axis=1)
        got = jnp.dot(block, grads[...], preferred_element_type=F32)
        out_ref[k * 128 : (k + 1) * 128, :] = got.astype(BF)


def backward(place, parts, at):
    sources, dests = at.shape[0] - 1, at.shape[1]
    rows, width = parts[0].shape
    per = 8
    return pl.pallas_call(
        backward_kernel,
        out_shape=in_hbm((sources * 128, width), BF),
        grid_spec=pltpu.PrefetchScalarGridSpec(
            num_scalar_prefetch=1,
            grid=(sources // per,),
            in_specs=[pl.BlockSpec((rows, width), lambda i, *_: (0, 0))] * 8
            + [pl.BlockSpec((per, dests, 128, 128), lambda i, *_: (i, 0, 0, 0))],
            out_specs=pl.BlockSpec((per * 128, width), lambda i, *_: (i, 0)),
            scratch_shapes=[pltpu.VMEM((dests * 128, width), BF)],
        ),
        compiler_params=params(20),
        cost_estimate=cost(2 * sources * 128 * dests * 128 * width, 20 << 20),
        name="backward",
    )(place, *parts, at)


def dot_on(a, b, da, db):
    return lax.dot_general(a, b, (((da,), (db,)), ((), ())), preferred_element_type=F32)


def middle_kernel(
    place_ref, keep_ref, taken_ref, r1_ref, r2_ref, r3_ref, deg_ref, x_ref, ws_ref, wn_ref, bias_ref, cot_ref,
    out_ref, pre_ref, mean_ref, grad_ref,
):
    degree = jnp.maximum(deg_ref[...], 1.0)
    summed = keep_ref[0] + taken_ref[0].astype(F32) + r1_ref[...].astype(F32)
    summed += r2_ref[...].astype(F32) + r3_ref[...].astype(F32)
    mean_t = (summed / degree).astype(BF)
    mean_ref[...] = mean_t
    preact = (
        jnp.dot(x_ref[...], ws_ref[...], preferred_element_type=F32)
        + dot_on(mean_t, wn_ref[...], 0, 0)
        + bias_ref[...]
    )
    sig = 1.0 / (1.0 + jnp.exp(-preact))
    out_ref[...] = (preact * sig).astype(BF)
    pre_grad = (cot_ref[...].astype(F32) * sig * (1.0 + preact * (1.0 - sig))).astype(BF)
    pre_ref[...] = pre_grad
    grad_t = dot_on(wn_ref[...], pre_grad, 1, 1) / degree
    grad_ref[...] = grad_t.T.astype(BF)


def middle(place, keep, taken, got, deg, x, ws, wn, bias, cot):
    n = x.shape[0]
    shape = jax.ShapeDtypeStruct((n, n), BF)
    whole = pl.BlockSpec((n, n), lambda i, *_: (0, 0))
    first = pl.BlockSpec((1, n, n), lambda i, *_: (0, 0, 0))
    return pl.pallas_call(
        middle_kernel,
        out_shape=(shape, shape, shape, shape),
        grid_spec=pltpu.PrefetchScalarGridSpec(
            num_scalar_prefetch=1,
            grid=(1,),
            in_specs=[first, first, whole, whole, whole]
            + [pl.BlockSpec((1, n), lambda i, place: (0, 2 * place[0] + place[1]))]
            + [whole, whole, whole, pl.BlockSpec((1, n), lambda i, *_: (0, 0)), whole],
            out_specs=(whole, whole, whole, whole),
        ),
        compiler_params=params(16),
        cost_estimate=cost(6 * n * n * n, 2 << 20, n * n),
        name="middle",
    )(place, keep, taken, *got, deg, x, ws, wn, bias, cot)


def weights_kernel(place_ref, x_ref, pre_ref, mean_ref, ws_ref, keep_ref, give_ref, self_ref):
    n = x_ref.shape[0]
    pre_grad = pre_ref[...]
    grads = (
        dot_on(x_ref[...], pre_grad, 0, 0),
        jnp.dot(mean_ref[...], pre_grad, preferred_element_type=F32),
    )
    bias_grad = jnp.sum(pre_grad.astype(F32), axis=0, keepdims=True)
    first = lax.broadcasted_iota(jnp.int32, (16, 1), 0) == 0
    bias_rows = jnp.where(first, bias_grad, 0.0)
    for core in range(2):

        @pl.when(place_ref[1] == core)
        def _():
            keep_ref[0:n, :] = grads[core]
            give_ref[0:n, :] = grads[1 - core]

    keep_ref[n : n + 16, :] = bias_rows
    give_ref[n : n + 16, :] = bias_rows
    self_ref[...] = dot_on(pre_grad, ws_ref[...], 1, 1)


def weights(place, x, pre_grad, mean_t, ws):
    n = x.shape[0]
    half = jax.ShapeDtypeStruct((n + 16, n), F32)
    vmem = pl.BlockSpec(memory_space=pltpu.VMEM)
    return pl.pallas_call(
        weights_kernel,
        out_shape=(half, half, jax.ShapeDtypeStruct((n, n), F32)),
        in_specs=[pl.BlockSpec(memory_space=pltpu.SMEM)] + [vmem] * 4,
        out_specs=(vmem, vmem, vmem),
        compiler_params=params(16),
        cost_estimate=cost(6 * n * n * n, 2 << 20),
        name="weights",
    )(place, x, pre_grad, mean_t, ws)


def finish_kernel(parts_ref, self_ref, out_ref):
    total = self_ref[...]
    for k in range(parts_ref.shape[0]):
        total += parts_ref[k].astype(F32)
    out_ref[...] = total.astype(BF)


def finish(parts, self_part):
    return pl.pallas_call(
        finish_kernel,
        out_shape=jax.ShapeDtypeStruct(self_part.shape, BF),
        compiler_params=params(16),
        cost_estimate=cost(1 << 20, 2 << 20),
        name="finish",
    )(parts, self_part)


def swap(x, axis):
    return lax.all_to_all(x, axis, 0, 0, tiled=True)


def along_y(step):
    return [(2 * y + c, 2 * ((y + step) % 4) + c) for y in range(4) for c in range(2)]


def send_node(x, dx, dz):
    moves = [
        (4 * i + j, 4 * ((i + dx) % 4) + (j + dz) % 4) for i in range(4) for j in range(4)
    ]
    return lax.ppermute(x, "nodes", moves)


PARTNER = [(i, i ^ 1) for i in range(8)]


def send_y(x, step):
    return lax.ppermute(x, "cols", along_y(step))


def send_core(x):
    return lax.ppermute(x, "cols", PARTNER)


def total(x, send):
    x = x.astype(BF)
    one, two, three = (send(x, k).astype(F32) for k in (1, 2, 3))
    return (x.astype(F32) + two) + (one + three)


def send_x(x, step):
    return send_node(x, step, 0)


def send_z(x, step):
    return send_node(x, 0, step)


def shards(node_feats, tile_row, tile_col, tile_bits, w_self, w_neigh, bias, cotangent):
    nodes = lax.axis_size("nodes")
    cols = lax.axis_size("cols")
    rows_dev, width = node_feats.shape
    me, node = lax.axis_index("cols"), lax.axis_index("nodes")
    y, core = me // 2, me % 2
    mine = jnp.stack([y, core, node // 4, node % 4]).astype(jnp.int32)
    theirs = jnp.stack([y, 1 - core, node // 4, node % 4]).astype(jnp.int32)

    ready = prepare(node_feats)
    line = jnp.stack([ready] + [send_x(ready, k) for k in (1, 2, 3)])
    tile_row, tile_col, line, mine, theirs = lax.optimization_barrier(
        (tile_row, tile_col, line, mine, theirs)
    )
    planes = [line] + [send_z(line, k) for k in (1, 2, 3)]
    at, degree = build(
        tile_row, tile_col, tile_bits[0], nodes * rows_dev // 128, cols * rows_dev // 128
    )
    degree = degree + send_core(degree)
    degree = degree + send_y(degree, 1) + send_y(degree, 2) + send_y(degree, 3)
    *planes, degree = lax.optimization_barrier((*planes, degree))

    give = forward(theirs, planes, at, BF)
    taken = send_core(give)
    keep = forward(mine, planes, at, F32)
    both = (keep[1:] + taken[1:].astype(F32)).astype(BF)
    got = [send_y(both[k - 1], k) for k in (1, 2, 3)]
    layer_out, pre_grad, mean_t, mean_grad = middle(
        mine, keep, taken, got, degree, node_feats, w_self, w_neigh, bias.reshape(1, -1), cotangent
    )
    same_core = [mean_grad] + [send_y(mean_grad, k) for k in (1, 2, 3)]
    other_core = [send_core(g) for g in same_core]

    part, give_part, self_part = weights(mine, node_feats, pre_grad, mean_t, w_self)
    part = total(part + send_core(give_part), send_x)

    src = backward(mine, same_core + other_core, at)
    src, part = lax.optimization_barrier((src, part))
    parts = swap(src.reshape(nodes, rows_dev, width), "nodes")

    part = total(total(part, send_z), send_y)
    other = send_core(part)
    bias_grad = part[width]
    self_grad = jnp.where(core == 0, part[:width], other[:width])
    neigh_grad = jnp.where(core == 0, other[:width], part[:width])

    feat_grad = finish(parts, self_part)
    return (layer_out, feat_grad, self_grad, neigh_grad, bias_grad)


def solution(mesh):
    return jax.shard_map(
        shards,
        mesh=mesh,
        in_specs=(
            P(("nodes", "cols"), None),
            P("nodes", "cols"),
            P("nodes", "cols"),
            P("nodes", "cols", None, None),
            P(),
            P(),
            P(),
            P(("nodes", "cols"), None),
        ),
        out_specs=(P(("nodes", "cols"), None), P(("nodes", "cols"), None), P(), P(), P()),
        check_vma=False,
    )
```

```python
import jax
import jax.numpy as jnp
from jax import lax
from jax.experimental import pallas as pl
from jax.experimental.pallas import tpu as pltpu
from jax.sharding import PartitionSpec as P

BF = jnp.bfloat16
F32 = jnp.float32
EXACT = 256
EXTRA = 16


def params(mib):
    return pltpu.CompilerParams(vmem_limit_bytes=mib << 20)


def in_hbm(shape, kind):
    return pltpu.HBM(shape, kind)


def cost(flops, moved, transcendentals=0):
    return pl.CostEstimate(flops=flops, bytes_accessed=moved, transcendentals=transcendentals)


def prepare_kernel(x_ref, out_ref):
    out_ref[...] = x_ref[...].T


def prepare(x):
    return pl.pallas_call(
        prepare_kernel,
        out_shape=jax.ShapeDtypeStruct(x.shape[::-1], BF),
        compiler_params=params(8),
        cost_estimate=cost(0, 1 << 18),
        name="prepare",
    )(x)


def build_kernel(
    rows_ref, cols_ref, bits_all, gate_ref, at_ref, deg_ref,
    deg8, count, spill, row_ref, col_ref, bits_ref, sems,
):
    sources = at_ref.shape[0] - 1
    dests = at_ref.shape[1]
    tiles = bits_ref.shape[0]
    pieces = 4
    each = tiles // pieces

    def fetch(k):
        part = pl.ds(k * each, each)
        return pltpu.make_async_copy(bits_all.at[0, part], bits_ref.at[part], sems.at[2 + k])

    copies = [
        pltpu.make_async_copy(rows_ref, row_ref, sems.at[0]),
        pltpu.make_async_copy(cols_ref, col_ref, sems.at[1]),
    ] + [fetch(k) for k in range(pieces)]
    for copy in copies:
        copy.start()
    for r in range(dests):
        deg8[r] = jnp.zeros((8, 128), F32)

    def clear(k, carry):
        for r in range(dests):
            at_ref[k, r] = jnp.zeros((128, 128), BF)
            count[k * dests + r] = 0
        return carry

    lax.fori_loop(0, sources, clear, 0)
    at_ref[sources, 0] = jnp.zeros((128, 128), BF)
    spill[0] = -1
    shifts = lax.broadcasted_iota(jnp.int32, (8, 128), 0)

    def add_tile(t, carry):
        row = row_ref[0, t]
        col = col_ref[0, t]
        slot = col * dests + row
        seen = count[slot]
        count[slot] = seen + 1
        full = seen >= EXACT
        spill[0] = jnp.where(full, slot, spill[0])
        to_col = jnp.where(full, sources, col)
        to_row = jnp.where(full, 0, row)
        total = None
        for i in range(8):
            flags = []
            for w in (2 * i, 2 * i + 1):
                word = jnp.broadcast_to(bits_ref[t, w : w + 1, :], (8, 128))
                flags.append((jnp.right_shift(word, shifts) & 1).astype(F32))
            pair = flags[0] + flags[1]
            total = pair if total is None else total + pair
            at_ref[to_col, to_row, 16 * i : 16 * i + 16, :] += jnp.concatenate(flags, 0).astype(BF)
        deg8[row] += total
        return carry

    copies[0].wait()
    copies[1].wait()
    for k in range(pieces):
        copies[2 + k].wait()
        lax.fori_loop(k * each, (k + 1) * each, add_tile, 0, unroll=2)

    @pl.when(spill[0] >= 0)
    def _():
        slot = spill[0]
        col = lax.div(slot, dests)
        row = lax.rem(slot, dests)
        whole = at_ref[col, row].astype(F32) + at_ref[sources, 0].astype(F32)
        at_ref[col, row] = whole.astype(BF)

    for r in range(dests):
        deg_ref[:, r * 128 : (r + 1) * 128] = jnp.sum(deg8[r], axis=0, keepdims=True)


def build(rows, cols, bits, gate, sources, dests):
    tiles = bits.shape[1]
    assert tiles <= 2 * EXACT and tiles % 8 == 0
    hbm = pl.BlockSpec(memory_space=pltpu.HBM)
    vmem = pl.BlockSpec(memory_space=pltpu.VMEM)
    return pl.pallas_call(
        build_kernel,
        out_shape=(
            jax.ShapeDtypeStruct((sources + 1, dests, 128, 128), BF),
            jax.ShapeDtypeStruct((1, dests * 128), F32),
        ),
        in_specs=[hbm, hbm, hbm, pl.BlockSpec(memory_space=pl.ANY)],
        out_specs=(vmem, vmem),
        scratch_shapes=[
            pltpu.VMEM((dests, 8, 128), F32),
            pltpu.SMEM((sources * dests,), jnp.int32),
            pltpu.SMEM((1,), jnp.int32),
            pltpu.SMEM((1, tiles), jnp.int32),
            pltpu.SMEM((1, tiles), jnp.int32),
            pltpu.VMEM((tiles, 16, 128), jnp.int32),
            pltpu.SemaphoreType.DMA((6,)),
        ],
        compiler_params=params(24),
        cost_estimate=cost(0, 30 << 20),
        name="build",
    )(rows, cols, bits, gate)


def forward_kernel(place_ref, *refs):
    planes, at_ref, deg_ref, out_ref, joined = refs[:4], refs[4], refs[5], refs[6], refs[7]
    rows = planes[0].shape[2]
    width = planes[0].shape[1]

    @pl.when(pl.program_id(0) == 0)
    def _():
        for kx in range(4):
            x = lax.rem(place_ref[2] + 4 - kx, 4)
            for kz in range(4):
                n = 4 * x + lax.rem(place_ref[3] + 4 - kz, 4)
                joined[:, pl.ds(pl.multiple_of(n * rows, rows), rows)] = planes[kz][kx]

    blocks = [
        jnp.concatenate([at_ref[k, r] for r in range(at_ref.shape[1])], axis=1)
        for k in range(at_ref.shape[0])
    ]
    part = jnp.dot(joined[...], jnp.concatenate(blocks, axis=0), preferred_element_type=F32)
    out_ref[0, 0:width, :] = part.astype(out_ref.dtype)
    degree = deg_ref[...] if out_ref.dtype == F32 else two_rows(deg_ref[...])
    out_ref[0, width:, :] = spaced(degree, out_ref.dtype)


def two_rows(whole):
    high = whole.astype(BF).astype(F32)
    first = lax.broadcasted_iota(jnp.int32, (2, 1), 0) == 0
    return jnp.where(first, high, whole - high)


def spaced(rows, kind):
    count, width = rows.shape
    place = lax.broadcasted_iota(jnp.int32, (EXTRA, 1), 0)
    out = jnp.zeros((EXTRA, width), F32)
    for k in range(count):
        out = jnp.where(place == k, rows[k : k + 1, :], out)
    return out.astype(kind)


def forward(place, planes, at, degree, kind):
    lines, width, rows = planes[0].shape
    sources = at.shape[0] - 1
    per = rows // 128

    def chunk(j, place):
        return (0, 2 * lax.rem(place[0] + j, 4) + place[1], 0, 0)

    return pl.pallas_call(
        forward_kernel,
        out_shape=jax.ShapeDtypeStruct((4, width + EXTRA, rows), kind),
        grid_spec=pltpu.PrefetchScalarGridSpec(
            num_scalar_prefetch=1,
            grid=(4,),
            in_specs=[pl.BlockSpec((lines, width, rows), lambda j, *_: (0, 0, 0))] * 4
            + [pl.BlockSpec((sources, per, 128, 128), chunk)]
            + [pl.BlockSpec((1, rows), lambda j, place: chunk(j, place)[:2])],
            out_specs=pl.BlockSpec((1, width + EXTRA, rows), lambda j, *_: (j, 0, 0)),
            scratch_shapes=[pltpu.VMEM((width, sources * 128), BF)],
        ),
        compiler_params=params(20),
        cost_estimate=cost(8 * sources * 128 * rows * width, 10 << 20),
        name="forward",
    )(place, *planes, at, degree)


def backward_kernel(place_ref, *refs):
    parts, at_ref, out_ref, grads = refs[:8], refs[8], refs[9], refs[10]
    rows = parts[0].shape[0]

    @pl.when(pl.program_id(0) == 0)
    def _():
        for k in range(4):
            chunk = 2 * lax.rem(place_ref[0] + 4 - k, 4)
            own = pl.multiple_of((chunk + place_ref[1]) * rows, rows)
            other = pl.multiple_of((chunk + 1 - place_ref[1]) * rows, rows)
            grads[pl.ds(own, rows), :] = parts[k][...]
            grads[pl.ds(other, rows), :] = parts[4 + k][...]

    for k in range(at_ref.shape[0]):
        block = jnp.concatenate([at_ref[k, r] for r in range(at_ref.shape[1])], axis=1)
        got = jnp.dot(block, grads[...], preferred_element_type=F32)
        out_ref[k * 128 : (k + 1) * 128, :] = got.astype(BF)


def backward(place, parts, at):
    sources, dests = at.shape[0] - 1, at.shape[1]
    rows, width = parts[0].shape
    per = 8
    return pl.pallas_call(
        backward_kernel,
        out_shape=in_hbm((sources * 128, width), BF),
        grid_spec=pltpu.PrefetchScalarGridSpec(
            num_scalar_prefetch=1,
            grid=(sources // per,),
            in_specs=[pl.BlockSpec((rows, width), lambda i, *_: (0, 0))] * 8
            + [pl.BlockSpec((per, dests, 128, 128), lambda i, *_: (i, 0, 0, 0))],
            out_specs=pl.BlockSpec((per * 128, width), lambda i, *_: (i, 0)),
            scratch_shapes=[pltpu.VMEM((dests * 128, width), BF)],
        ),
        compiler_params=params(20),
        cost_estimate=cost(2 * sources * 128 * dests * 128 * width, 20 << 20),
        name="backward",
    )(place, *parts, at)


def dot_on(a, b, da, db):
    return lax.dot_general(a, b, (((da,), (db,)), ((), ())), preferred_element_type=F32)


def mix_kernel(keep_ref, taken_ref, own_ref, *outs):
    width = own_ref.shape[0] - EXTRA
    own_ref[...] = keep_ref[0] + taken_ref[0].astype(F32)
    for k, out_ref in enumerate(outs):
        both = keep_ref[k + 1] + taken_ref[k + 1].astype(F32)
        out_ref[0:width, :] = both[0:width].astype(BF)
        degree = both[width : width + 1] + both[width + 1 : width + 2]
        out_ref[width:, :] = spaced(two_rows(degree), BF)


def mix(keep, taken):
    shape = keep.shape[1:]
    return pl.pallas_call(
        mix_kernel,
        out_shape=(jax.ShapeDtypeStruct(shape, F32),) + (jax.ShapeDtypeStruct(shape, BF),) * 3,
        compiler_params=params(16),
        cost_estimate=cost(1 << 18, 2 << 20),
        name="mix",
    )(keep, taken)


def middle_kernel(
    own_ref, r1_ref, r2_ref, r3_ref, x_ref, ws_ref, wn_ref, bias_ref, cot_ref,
    out_ref, pre_ref, mean_ref, grad_ref,
):
    width = x_ref.shape[1]
    summed = (own_ref[...] + r2_ref[...].astype(F32)) + (
        r1_ref[...].astype(F32) + r3_ref[...].astype(F32)
    )
    degree = jnp.maximum(summed[width : width + 1] + summed[width + 1 : width + 2], 1.0)
    summed = summed[0:width]
    mean_t = (summed / degree).astype(BF)
    mean_ref[...] = mean_t
    preact = (
        jnp.dot(x_ref[...], ws_ref[...], preferred_element_type=F32)
        + dot_on(mean_t, wn_ref[...], 0, 0)
        + bias_ref[...]
    )
    sig = 1.0 / (1.0 + jnp.exp(-preact))
    out_ref[...] = (preact * sig).astype(BF)
    pre_grad = (cot_ref[...].astype(F32) * sig * (1.0 + preact * (1.0 - sig))).astype(BF)
    pre_ref[...] = pre_grad
    grad_t = dot_on(wn_ref[...], pre_grad, 1, 1) / degree
    grad_ref[...] = grad_t.T.astype(BF)


def middle(own, got, x, ws, wn, bias, cot):
    n = x.shape[0]
    shape = jax.ShapeDtypeStruct((n, n), BF)
    return pl.pallas_call(
        middle_kernel,
        out_shape=(shape, shape, shape, shape),
        compiler_params=params(16),
        cost_estimate=cost(6 * n * n * n, 2 << 20, n * n),
        name="middle",
    )(own, *got, x, ws, wn, bias, cot)


def weights_kernel(place_ref, x_ref, pre_ref, mean_ref, ws_ref, keep_ref, give_ref, self_ref):
    n = x_ref.shape[0]
    pre_grad = pre_ref[...]
    grads = (
        dot_on(x_ref[...], pre_grad, 0, 0),
        jnp.dot(mean_ref[...], pre_grad, preferred_element_type=F32),
    )
    bias_grad = jnp.sum(pre_grad.astype(F32), axis=0, keepdims=True)
    first = lax.broadcasted_iota(jnp.int32, (16, 1), 0) == 0
    bias_rows = jnp.where(first, bias_grad, 0.0)
    for core in range(2):

        @pl.when(place_ref[1] == core)
        def _():
            keep_ref[0:n, :] = grads[core]
            give_ref[0:n, :] = grads[1 - core]

    keep_ref[n : n + 16, :] = bias_rows
    give_ref[n : n + 16, :] = bias_rows
    self_ref[...] = dot_on(pre_grad, ws_ref[...], 1, 1)


def weights(place, x, pre_grad, mean_t, ws):
    n = x.shape[0]
    half = jax.ShapeDtypeStruct((n + 16, n), F32)
    vmem = pl.BlockSpec(memory_space=pltpu.VMEM)
    return pl.pallas_call(
        weights_kernel,
        out_shape=(half, half, jax.ShapeDtypeStruct((n, n), F32)),
        in_specs=[pl.BlockSpec(memory_space=pltpu.SMEM)] + [vmem] * 4,
        out_specs=(vmem, vmem, vmem),
        compiler_params=params(16),
        cost_estimate=cost(6 * n * n * n, 2 << 20),
        name="weights",
    )(place, x, pre_grad, mean_t, ws)


def finish_kernel(parts_ref, self_ref, out_ref):
    total = self_ref[...]
    for k in range(parts_ref.shape[0]):
        total += parts_ref[k].astype(F32)
    out_ref[...] = total.astype(BF)


def finish(parts, self_part):
    return pl.pallas_call(
        finish_kernel,
        out_shape=jax.ShapeDtypeStruct(self_part.shape, BF),
        compiler_params=params(16),
        cost_estimate=cost(1 << 20, 2 << 20),
        name="finish",
    )(parts, self_part)


def swap(x, axis):
    return lax.all_to_all(x, axis, 0, 0, tiled=True)


def along_y(step):
    return [(2 * y + c, 2 * ((y + step) % 4) + c) for y in range(4) for c in range(2)]


def send_node(x, dx, dz):
    moves = [
        (4 * i + j, 4 * ((i + dx) % 4) + (j + dz) % 4) for i in range(4) for j in range(4)
    ]
    return lax.ppermute(x, "nodes", moves)


PARTNER = [(i, i ^ 1) for i in range(8)]


def send_y(x, step):
    return lax.ppermute(x, "cols", along_y(step))


def send_core(x):
    return lax.ppermute(x, "cols", PARTNER)


def add_terms(terms):
    own, one, two, three = (x.astype(F32) for x in terms)
    return (own + two) + (one + three)


def send_x(x, step):
    return send_node(x, step, 0)


def send_z(x, step):
    return send_node(x, 0, step)


def shards(node_feats, tile_row, tile_col, tile_bits, w_self, w_neigh, bias, cotangent):
    nodes = lax.axis_size("nodes")
    cols = lax.axis_size("cols")
    rows_dev, width = node_feats.shape
    me, node = lax.axis_index("cols"), lax.axis_index("nodes")
    y, core = me // 2, me % 2
    mine = jnp.stack([y, core, node // 4, node % 4]).astype(jnp.int32)
    theirs = jnp.stack([y, 1 - core, node // 4, node % 4]).astype(jnp.int32)

    ready = prepare(node_feats)
    line = jnp.stack([ready] + [send_x(ready, k) for k in (1, 2, 3)])
    line, mine, theirs = lax.optimization_barrier((line, mine, theirs))
    planes = [line] + [send_z(line, k) for k in (1, 2, 3)]
    at, degree = build(
        *(pltpu.with_memory_space_constraint(t, pltpu.HBM) for t in (tile_row, tile_col, tile_bits)),
        line,
        nodes * rows_dev // 128, cols * rows_dev // 128
    )

    give = forward(theirs, planes, at, degree, BF)
    taken = send_core(give)
    keep = forward(mine, planes, at, degree, F32)
    own, *sent = mix(keep, taken)
    got = [send_y(sent[k - 1], k) for k in (1, 2, 3)]
    layer_out, pre_grad, mean_t, mean_grad = middle(
        own, got, node_feats, w_self, w_neigh, bias.reshape(1, -1), cotangent
    )
    same_core = [mean_grad] + [send_y(mean_grad, k) for k in (1, 2, 3)]

    part, give_part, self_part = weights(mine, node_feats, pre_grad, mean_t, w_self)
    part = (part + send_core(give_part)).astype(BF)
    terms = [part] + [send_x(part, k) for k in (1, 2, 3)]
    far, terms = lax.optimization_barrier((same_core[2], terms))
    other_core = [send_core(g) for g in (same_core[0], same_core[1], far, same_core[3])]

    grads, terms = lax.optimization_barrier((same_core + other_core, terms))
    part = add_terms(terms).astype(BF)
    terms = [part] + [send_z(part, k) for k in (1, 2, 3)]
    src = backward(mine, grads, at)
    src, terms = lax.optimization_barrier((src, terms))
    parts = swap(src.reshape(nodes, rows_dev, width), "nodes")

    part = add_terms(terms).astype(BF)
    part = add_terms([part] + [send_y(part, k) for k in (1, 2, 3)])
    other = send_core(part)
    bias_grad = part[width]
    self_grad = jnp.where(core == 0, part[:width], other[:width])
    neigh_grad = jnp.where(core == 0, other[:width], part[:width])

    feat_grad = finish(parts, self_part)
    return (layer_out, feat_grad, self_grad, neigh_grad, bias_grad)


def solution(mesh):
    return jax.shard_map(
        shards,
        mesh=mesh,
        in_specs=(
            P(("nodes", "cols"), None),
            P("nodes", "cols"),
            P("nodes", "cols"),
            P("nodes", "cols", None, None),
            P(),
            P(),
            P(),
            P(("nodes", "cols"), None),
        ),
        out_specs=(P(("nodes", "cols"), None), P(("nodes", "cols"), None), P(), P(), P()),
        check_vma=False,
    )
```

```python
import jax
import jax.numpy as jnp
from jax import lax
from jax.experimental import pallas as pl
from jax.experimental.pallas import tpu as pltpu
from jax.sharding import PartitionSpec as P

BF = jnp.bfloat16
F32 = jnp.float32
EXACT = 256
EXTRA = 16


def params(mib):
    return pltpu.CompilerParams(vmem_limit_bytes=mib << 20)


def in_hbm(shape, kind):
    return pltpu.HBM(shape, kind)


def cost(flops, moved, transcendentals=0):
    return pl.CostEstimate(flops=flops, bytes_accessed=moved, transcendentals=transcendentals)


def prepare_kernel(x_ref, top_ref, low_ref):
    half = top_ref.shape[0]
    flipped = x_ref[...].T
    top_ref[...] = flipped[:half]
    low_ref[...] = flipped[half:]


def prepare(x):
    rows, width = x.shape
    shape = jax.ShapeDtypeStruct((width // 2, rows), BF)
    return pl.pallas_call(
        prepare_kernel,
        out_shape=(shape, shape),
        compiler_params=params(8),
        cost_estimate=cost(0, 1 << 18),
        name="prepare",
    )(x)


def build_kernel(
    rows_ref, cols_ref, bits_all, gate_ref, at_ref, deg_ref,
    deg8, count, spill, row_ref, col_ref, bits_ref, sems,
):
    sources = at_ref.shape[0] - 1
    dests = at_ref.shape[1]
    tiles = bits_ref.shape[0]
    pieces = 4
    each = tiles // pieces

    def fetch(k):
        part = pl.ds(k * each, each)
        return pltpu.make_async_copy(bits_all.at[0, part], bits_ref.at[part], sems.at[2 + k])

    copies = [
        pltpu.make_async_copy(rows_ref, row_ref, sems.at[0]),
        pltpu.make_async_copy(cols_ref, col_ref, sems.at[1]),
    ] + [fetch(k) for k in range(pieces)]
    for copy in copies:
        copy.start()
    for r in range(dests):
        deg8[r] = jnp.zeros((8, 128), F32)

    def clear(k, carry):
        for r in range(dests):
            at_ref[k, r] = jnp.zeros((128, 128), BF)
            count[k * dests + r] = 0
        return carry

    lax.fori_loop(0, sources, clear, 0)
    at_ref[sources, 0] = jnp.zeros((128, 128), BF)
    spill[0] = -1
    shifts = lax.broadcasted_iota(jnp.int32, (8, 128), 0)

    def add_tile(t, carry):
        row = row_ref[0, t]
        col = col_ref[0, t]
        slot = col * dests + row
        seen = count[slot]
        count[slot] = seen + 1
        full = seen >= EXACT
        spill[0] = jnp.where(full, slot, spill[0])
        to_col = jnp.where(full, sources, col)
        to_row = jnp.where(full, 0, row)
        total = None
        for i in range(8):
            flags = []
            for w in (2 * i, 2 * i + 1):
                word = jnp.broadcast_to(bits_ref[t, w : w + 1, :], (8, 128))
                flags.append((jnp.right_shift(word, shifts) & 1).astype(F32))
            pair = flags[0] + flags[1]
            total = pair if total is None else total + pair
            at_ref[to_col, to_row, 16 * i : 16 * i + 16, :] += jnp.concatenate(flags, 0).astype(BF)
        deg8[row] += total
        return carry

    copies[0].wait()
    copies[1].wait()
    for k in range(pieces):
        copies[2 + k].wait()
        lax.fori_loop(k * each, (k + 1) * each, add_tile, 0, unroll=2)

    @pl.when(spill[0] >= 0)
    def _():
        slot = spill[0]
        col = lax.div(slot, dests)
        row = lax.rem(slot, dests)
        whole = at_ref[col, row].astype(F32) + at_ref[sources, 0].astype(F32)
        at_ref[col, row] = whole.astype(BF)

    for r in range(dests):
        deg_ref[:, r * 128 : (r + 1) * 128] = jnp.sum(deg8[r], axis=0, keepdims=True)


def build(rows, cols, bits, gate, sources, dests):
    tiles = bits.shape[1]
    assert tiles <= 2 * EXACT and tiles % 8 == 0
    hbm = pl.BlockSpec(memory_space=pltpu.HBM)
    vmem = pl.BlockSpec(memory_space=pltpu.VMEM)
    return pl.pallas_call(
        build_kernel,
        out_shape=(
            jax.ShapeDtypeStruct((sources + 1, dests, 128, 128), BF),
            jax.ShapeDtypeStruct((1, dests * 128), F32),
        ),
        in_specs=[hbm, hbm, hbm, pl.BlockSpec(memory_space=pl.ANY)],
        out_specs=(vmem, vmem),
        scratch_shapes=[
            pltpu.VMEM((dests, 8, 128), F32),
            pltpu.SMEM((sources * dests,), jnp.int32),
            pltpu.SMEM((1,), jnp.int32),
            pltpu.SMEM((1, tiles), jnp.int32),
            pltpu.SMEM((1, tiles), jnp.int32),
            pltpu.VMEM((tiles, 16, 128), jnp.int32),
            pltpu.SemaphoreType.DMA((6,)),
        ],
        compiler_params=params(24),
        cost_estimate=cost(0, 30 << 20),
        name="build",
    )(rows, cols, bits, gate)


def forward_kernel(place_ref, *refs):
    tops, lows = refs[:4], refs[4:8]
    at_ref, deg_ref, out_ref, joined = refs[8:]
    half, rows = tops[0].shape[1:]
    width = 2 * half

    @pl.when(pl.program_id(0) == 0)
    def _():
        for kx in range(4):
            x = lax.rem(place_ref[2] + 4 - kx, 4)
            for kz in range(4):
                n = 4 * x + lax.rem(place_ref[3] + 4 - kz, 4)
                lanes = pl.ds(pl.multiple_of(n * rows, rows), rows)
                joined[0:half, lanes] = tops[kz][kx]
                joined[half:width, lanes] = lows[kx][kz]

    blocks = [
        jnp.concatenate([at_ref[k, r] for r in range(at_ref.shape[1])], axis=1)
        for k in range(at_ref.shape[0])
    ]
    part = jnp.dot(joined[...], jnp.concatenate(blocks, axis=0), preferred_element_type=F32)
    out_ref[0, 0:width, :] = part.astype(out_ref.dtype)
    degree = deg_ref[...] if out_ref.dtype == F32 else two_rows(deg_ref[...])
    out_ref[0, width:, :] = spaced(degree, out_ref.dtype)


def two_rows(whole):
    high = whole.astype(BF).astype(F32)
    first = lax.broadcasted_iota(jnp.int32, (2, 1), 0) == 0
    return jnp.where(first, high, whole - high)


def spaced(rows, kind):
    count, width = rows.shape
    place = lax.broadcasted_iota(jnp.int32, (EXTRA, 1), 0)
    out = jnp.zeros((EXTRA, width), F32)
    for k in range(count):
        out = jnp.where(place == k, rows[k : k + 1, :], out)
    return out.astype(kind)


def forward(place, planes, at, degree, kind):
    lines, half, rows = planes[0].shape
    width = 2 * half
    sources = at.shape[0] - 1
    per = rows // 128

    def chunk(j, place):
        return (0, 2 * lax.rem(place[0] + j, 4) + place[1], 0, 0)

    return pl.pallas_call(
        forward_kernel,
        out_shape=jax.ShapeDtypeStruct((4, width + EXTRA, rows), kind),
        grid_spec=pltpu.PrefetchScalarGridSpec(
            num_scalar_prefetch=1,
            grid=(4,),
            in_specs=[pl.BlockSpec((lines, half, rows), lambda j, *_: (0, 0, 0))] * 8
            + [pl.BlockSpec((sources, per, 128, 128), chunk)]
            + [pl.BlockSpec((1, rows), lambda j, place: chunk(j, place)[:2])],
            out_specs=pl.BlockSpec((1, width + EXTRA, rows), lambda j, *_: (j, 0, 0)),
            scratch_shapes=[pltpu.VMEM((width, sources * 128), BF)],
        ),
        compiler_params=params(20),
        cost_estimate=cost(8 * sources * 128 * rows * width, 10 << 20),
        name="forward",
    )(place, *planes, at, degree)


def backward_kernel(place_ref, *refs):
    parts, at_ref, out_ref, grads = refs[:8], refs[8], refs[9], refs[10]
    rows = parts[0].shape[0]

    @pl.when(pl.program_id(0) == 0)
    def _():
        for k in range(4):
            chunk = 2 * lax.rem(place_ref[0] + 4 - k, 4)
            own = pl.multiple_of((chunk + place_ref[1]) * rows, rows)
            other = pl.multiple_of((chunk + 1 - place_ref[1]) * rows, rows)
            grads[pl.ds(own, rows), :] = parts[k][...]
            grads[pl.ds(other, rows), :] = parts[4 + k][...]

    for k in range(at_ref.shape[0]):
        block = jnp.concatenate([at_ref[k, r] for r in range(at_ref.shape[1])], axis=1)
        got = jnp.dot(block, grads[...], preferred_element_type=F32)
        out_ref[k * 128 : (k + 1) * 128, :] = got.astype(BF)


def backward(place, parts, at):
    sources, dests = at.shape[0] - 1, at.shape[1]
    rows, width = parts[0].shape
    per = 8
    return pl.pallas_call(
        backward_kernel,
        out_shape=in_hbm((sources * 128, width), BF),
        grid_spec=pltpu.PrefetchScalarGridSpec(
            num_scalar_prefetch=1,
            grid=(sources // per,),
            in_specs=[pl.BlockSpec((rows, width), lambda i, *_: (0, 0))] * 8
            + [pl.BlockSpec((per, dests, 128, 128), lambda i, *_: (i, 0, 0, 0))],
            out_specs=pl.BlockSpec((per * 128, width), lambda i, *_: (i, 0)),
            scratch_shapes=[pltpu.VMEM((dests * 128, width), BF)],
        ),
        compiler_params=params(20),
        cost_estimate=cost(2 * sources * 128 * dests * 128 * width, 20 << 20),
        name="backward",
    )(place, *parts, at)


def dot_on(a, b, da, db):
    return lax.dot_general(a, b, (((da,), (db,)), ((), ())), preferred_element_type=F32)


def mix_kernel(keep_ref, taken_ref, own_ref, *outs):
    width = own_ref.shape[0] - EXTRA
    own_ref[...] = keep_ref[0] + taken_ref[0].astype(F32)
    for k, out_ref in enumerate(outs):
        both = keep_ref[k + 1] + taken_ref[k + 1].astype(F32)
        out_ref[0:width, :] = both[0:width].astype(BF)
        degree = both[width : width + 1] + both[width + 1 : width + 2]
        out_ref[width:, :] = spaced(two_rows(degree), BF)


def mix(keep, taken):
    shape = keep.shape[1:]
    return pl.pallas_call(
        mix_kernel,
        out_shape=(jax.ShapeDtypeStruct(shape, F32),) + (jax.ShapeDtypeStruct(shape, BF),) * 3,
        compiler_params=params(16),
        cost_estimate=cost(1 << 18, 2 << 20),
        name="mix",
    )(keep, taken)


def middle_kernel(
    own_ref, r1_ref, r2_ref, r3_ref, x_ref, ws_ref, wn_ref, bias_ref, cot_ref,
    out_ref, pre_ref, mean_ref, grad_ref,
):
    width = x_ref.shape[1]
    summed = (own_ref[...] + r2_ref[...].astype(F32)) + (
        r1_ref[...].astype(F32) + r3_ref[...].astype(F32)
    )
    degree = jnp.maximum(summed[width : width + 1] + summed[width + 1 : width + 2], 1.0)
    summed = summed[0:width]
    mean_t = (summed / degree).astype(BF)
    mean_ref[...] = mean_t
    preact = (
        jnp.dot(x_ref[...], ws_ref[...], preferred_element_type=F32)
        + dot_on(mean_t, wn_ref[...], 0, 0)
        + bias_ref[...]
    )
    sig = 1.0 / (1.0 + jnp.exp(-preact))
    out_ref[...] = (preact * sig).astype(BF)
    pre_grad = (cot_ref[...].astype(F32) * sig * (1.0 + preact * (1.0 - sig))).astype(BF)
    pre_ref[...] = pre_grad
    grad_t = dot_on(wn_ref[...], pre_grad, 1, 1) / degree
    grad_ref[...] = grad_t.T.astype(BF)


def middle(own, got, x, ws, wn, bias, cot):
    n = x.shape[0]
    shape = jax.ShapeDtypeStruct((n, n), BF)
    return pl.pallas_call(
        middle_kernel,
        out_shape=(shape, shape, shape, shape),
        compiler_params=params(16),
        cost_estimate=cost(6 * n * n * n, 2 << 20, n * n),
        name="middle",
    )(own, *got, x, ws, wn, bias, cot)


def weights_kernel(place_ref, x_ref, pre_ref, mean_ref, ws_ref, keep_ref, give_ref, self_ref):
    n = x_ref.shape[0]
    pre_grad = pre_ref[...]
    grads = (
        dot_on(x_ref[...], pre_grad, 0, 0),
        jnp.dot(mean_ref[...], pre_grad, preferred_element_type=F32),
    )
    bias_grad = jnp.sum(pre_grad.astype(F32), axis=0, keepdims=True)
    first = lax.broadcasted_iota(jnp.int32, (16, 1), 0) == 0
    bias_rows = jnp.where(first, bias_grad, 0.0)
    for core in range(2):

        @pl.when(place_ref[1] == core)
        def _():
            keep_ref[0:n, :] = grads[core]
            give_ref[0:n, :] = grads[1 - core]

    keep_ref[n : n + 16, :] = bias_rows
    give_ref[n : n + 16, :] = bias_rows
    self_ref[...] = dot_on(pre_grad, ws_ref[...], 1, 1)


def weights(place, x, pre_grad, mean_t, ws):
    n = x.shape[0]
    half = jax.ShapeDtypeStruct((n + 16, n), F32)
    vmem = pl.BlockSpec(memory_space=pltpu.VMEM)
    return pl.pallas_call(
        weights_kernel,
        out_shape=(half, half, jax.ShapeDtypeStruct((n, n), F32)),
        in_specs=[pl.BlockSpec(memory_space=pltpu.SMEM)] + [vmem] * 4,
        out_specs=(vmem, vmem, vmem),
        compiler_params=params(16),
        cost_estimate=cost(6 * n * n * n, 2 << 20),
        name="weights",
    )(place, x, pre_grad, mean_t, ws)


def finish_kernel(parts_ref, self_ref, out_ref):
    total = self_ref[...]
    for k in range(parts_ref.shape[0]):
        total += parts_ref[k].astype(F32)
    out_ref[...] = total.astype(BF)


def finish(parts, self_part):
    return pl.pallas_call(
        finish_kernel,
        out_shape=jax.ShapeDtypeStruct(self_part.shape, BF),
        compiler_params=params(16),
        cost_estimate=cost(1 << 20, 2 << 20),
        name="finish",
    )(parts, self_part)


def swap(x, axis):
    return lax.all_to_all(x, axis, 0, 0, tiled=True)


def along_y(step):
    return [(2 * y + c, 2 * ((y + step) % 4) + c) for y in range(4) for c in range(2)]


def send_node(x, dx, dz):
    moves = [
        (4 * i + j, 4 * ((i + dx) % 4) + (j + dz) % 4) for i in range(4) for j in range(4)
    ]
    return lax.ppermute(x, "nodes", moves)


PARTNER = [(i, i ^ 1) for i in range(8)]


def send_y(x, step):
    return lax.ppermute(x, "cols", along_y(step))


def send_core(x):
    return lax.ppermute(x, "cols", PARTNER)


def add_terms(terms):
    own, one, two, three = (x.astype(F32) for x in terms)
    return (own + two) + (one + three)


def send_x(x, step):
    return send_node(x, step, 0)


def send_z(x, step):
    return send_node(x, 0, step)


def shards(node_feats, tile_row, tile_col, tile_bits, w_self, w_neigh, bias, cotangent):
    nodes = lax.axis_size("nodes")
    cols = lax.axis_size("cols")
    rows_dev, width = node_feats.shape
    me, node = lax.axis_index("cols"), lax.axis_index("nodes")
    y, core = me // 2, me % 2
    mine = jnp.stack([y, core, node // 4, node % 4]).astype(jnp.int32)
    theirs = jnp.stack([y, 1 - core, node // 4, node % 4]).astype(jnp.int32)

    top, low = prepare(node_feats)
    top = jnp.stack([top] + [send_x(top, k) for k in (1, 2, 3)])
    low = jnp.stack([low] + [send_z(low, k) for k in (1, 2, 3)])
    top, low, mine, theirs = lax.optimization_barrier((top, low, mine, theirs))
    planes = [top] + [send_z(top, k) for k in (1, 2, 3)]
    planes += [low] + [send_x(low, k) for k in (1, 2, 3)]
    at, degree = build(
        *(pltpu.with_memory_space_constraint(t, pltpu.HBM) for t in (tile_row, tile_col, tile_bits)),
        top,
        nodes * rows_dev // 128, cols * rows_dev // 128
    )

    give = forward(theirs, planes, at, degree, BF)
    taken = send_core(give)
    keep = forward(mine, planes, at, degree, F32)
    own, *sent = mix(keep, taken)
    got = [send_y(sent[k - 1], k) for k in (1, 2, 3)]
    layer_out, pre_grad, mean_t, mean_grad = middle(
        own, got, node_feats, w_self, w_neigh, bias.reshape(1, -1), cotangent
    )
    same_core = [mean_grad] + [send_y(mean_grad, k) for k in (1, 2, 3)]

    part, give_part, self_part = weights(mine, node_feats, pre_grad, mean_t, w_self)
    part = (part + send_core(give_part)).astype(BF)
    *same_core, part = lax.optimization_barrier((*same_core, part))
    other_core = [send_core(g) for g in same_core]
    terms = [part] + [send_x(part, k) for k in (1, 2, 3)]

    src = backward(mine, same_core + other_core, at)
    src, terms = lax.optimization_barrier((src, terms))
    parts = swap(src.reshape(nodes, rows_dev, width), "nodes")

    part = add_terms(terms).astype(BF)
    part = add_terms([part] + [send_y(part, k) for k in (1, 2, 3)]).astype(BF)
    part = add_terms([part] + [send_z(part, k) for k in (1, 2, 3)])
    other = send_core(part)
    bias_grad = part[width]
    self_grad = jnp.where(core == 0, part[:width], other[:width])
    neigh_grad = jnp.where(core == 0, other[:width], part[:width])

    feat_grad = finish(parts, self_part)
    return (layer_out, feat_grad, self_grad, neigh_grad, bias_grad)


def solution(mesh):
    return jax.shard_map(
        shards,
        mesh=mesh,
        in_specs=(
            P(("nodes", "cols"), None),
            P("nodes", "cols"),
            P("nodes", "cols"),
            P("nodes", "cols", None, None),
            P(),
            P(),
            P(),
            P(("nodes", "cols"), None),
        ),
        out_specs=(P(("nodes", "cols"), None), P(("nodes", "cols"), None), P(), P(), P()),
        check_vma=False,
    )
```

```python
import jax
import jax.numpy as jnp
from jax import lax
from jax.experimental import pallas as pl
from jax.experimental.pallas import tpu as pltpu
from jax.sharding import PartitionSpec as P

BF = jnp.bfloat16
F32 = jnp.float32
EXACT = 256
EXTRA = 16


def params(mib):
    return pltpu.CompilerParams(vmem_limit_bytes=mib << 20)


def in_hbm(shape, kind):
    return pltpu.HBM(shape, kind)


def cost(flops, moved, transcendentals=0):
    return pl.CostEstimate(flops=flops, bytes_accessed=moved, transcendentals=transcendentals)


def prepare_kernel(x_ref, top_ref, low_ref):
    half = top_ref.shape[0]
    flipped = x_ref[...].T
    top_ref[...] = flipped[:half]
    low_ref[...] = flipped[half:]


def prepare(x):
    rows, width = x.shape
    shape = jax.ShapeDtypeStruct((width // 2, rows), BF)
    return pl.pallas_call(
        prepare_kernel,
        out_shape=(shape, shape),
        compiler_params=params(8),
        cost_estimate=cost(0, 1 << 18),
        name="prepare",
    )(x)


def build_kernel(
    rows_ref, cols_ref, bits_all, gate_ref, at_ref, deg_ref,
    deg8, count, spill, row_ref, col_ref, bits_ref, sems,
):
    sources = at_ref.shape[0] - 1
    dests = at_ref.shape[1]
    tiles = bits_ref.shape[0]
    pieces = 4
    each = tiles // pieces

    def fetch(k):
        part = pl.ds(k * each, each)
        return pltpu.make_async_copy(bits_all.at[0, part], bits_ref.at[part], sems.at[2 + k])

    copies = [
        pltpu.make_async_copy(rows_ref, row_ref, sems.at[0]),
        pltpu.make_async_copy(cols_ref, col_ref, sems.at[1]),
    ] + [fetch(k) for k in range(pieces)]
    for copy in copies:
        copy.start()
    for r in range(dests):
        deg8[r] = jnp.zeros((8, 128), F32)

    def clear(k, carry):
        for r in range(dests):
            at_ref[k, r] = jnp.zeros((128, 128), BF)
            count[k * dests + r] = 0
        return carry

    lax.fori_loop(0, sources, clear, 0)
    at_ref[sources, 0] = jnp.zeros((128, 128), BF)
    spill[0] = -1
    shifts = lax.broadcasted_iota(jnp.int32, (8, 128), 0)

    def add_tile(t, carry):
        row = row_ref[0, t]
        col = col_ref[0, t]
        slot = col * dests + row
        seen = count[slot]
        count[slot] = seen + 1
        full = seen >= EXACT
        spill[0] = jnp.where(full, slot, spill[0])
        to_col = jnp.where(full, sources, col)
        to_row = jnp.where(full, 0, row)
        total = None
        for i in range(8):
            flags = []
            for w in (2 * i, 2 * i + 1):
                word = jnp.broadcast_to(bits_ref[t, w : w + 1, :], (8, 128))
                flags.append((jnp.right_shift(word, shifts) & 1).astype(F32))
            pair = flags[0] + flags[1]
            total = pair if total is None else total + pair
            at_ref[to_col, to_row, 16 * i : 16 * i + 16, :] += jnp.concatenate(flags, 0).astype(BF)
        deg8[row] += total
        return carry

    copies[0].wait()
    copies[1].wait()
    for k in range(pieces):
        copies[2 + k].wait()
        lax.fori_loop(k * each, (k + 1) * each, add_tile, 0, unroll=2)

    @pl.when(spill[0] >= 0)
    def _():
        slot = spill[0]
        col = lax.div(slot, dests)
        row = lax.rem(slot, dests)
        whole = at_ref[col, row].astype(F32) + at_ref[sources, 0].astype(F32)
        at_ref[col, row] = whole.astype(BF)

    for r in range(dests):
        deg_ref[:, r * 128 : (r + 1) * 128] = jnp.sum(deg8[r], axis=0, keepdims=True)


def build(rows, cols, bits, gate, sources, dests):
    tiles = bits.shape[1]
    assert tiles <= 2 * EXACT and tiles % 8 == 0
    hbm = pl.BlockSpec(memory_space=pltpu.HBM)
    vmem = pl.BlockSpec(memory_space=pltpu.VMEM)
    return pl.pallas_call(
        build_kernel,
        out_shape=(
            jax.ShapeDtypeStruct((sources + 1, dests, 128, 128), BF),
            jax.ShapeDtypeStruct((1, dests * 128), F32),
        ),
        in_specs=[hbm, hbm, hbm, pl.BlockSpec(memory_space=pl.ANY)],
        out_specs=(vmem, vmem),
        scratch_shapes=[
            pltpu.VMEM((dests, 8, 128), F32),
            pltpu.SMEM((sources * dests,), jnp.int32),
            pltpu.SMEM((1,), jnp.int32),
            pltpu.SMEM((1, tiles), jnp.int32),
            pltpu.SMEM((1, tiles), jnp.int32),
            pltpu.VMEM((tiles, 16, 128), jnp.int32),
            pltpu.SemaphoreType.DMA((6,)),
        ],
        compiler_params=params(24),
        cost_estimate=cost(0, 30 << 20),
        name="build",
    )(rows, cols, bits, gate)


def forward_kernel(place_ref, *refs):
    tops, lows = refs[:4], refs[4:8]
    at_ref, deg_ref, out_ref, joined = refs[8:]
    half, rows = tops[0].shape[1:]
    width = 2 * half

    @pl.when(pl.program_id(0) == 0)
    def _():
        for kx in range(4):
            x = lax.rem(place_ref[2] + 4 - kx, 4)
            for kz in range(4):
                n = 4 * x + lax.rem(place_ref[3] + 4 - kz, 4)
                lanes = pl.ds(pl.multiple_of(n * rows, rows), rows)
                joined[0:half, lanes] = tops[kz][kx]
                joined[half:width, lanes] = lows[kx][kz]

    blocks = [
        jnp.concatenate([at_ref[k, r] for r in range(at_ref.shape[1])], axis=1)
        for k in range(at_ref.shape[0])
    ]
    part = jnp.dot(joined[...], jnp.concatenate(blocks, axis=0), preferred_element_type=F32)
    out_ref[0, 0:width, :] = part.astype(out_ref.dtype)
    degree = deg_ref[...] if out_ref.dtype == F32 else two_rows(deg_ref[...])
    out_ref[0, width:, :] = spaced(degree, out_ref.dtype)


def two_rows(whole):
    high = whole.astype(BF).astype(F32)
    first = lax.broadcasted_iota(jnp.int32, (2, 1), 0) == 0
    return jnp.where(first, high, whole - high)


def spaced(rows, kind):
    count, width = rows.shape
    place = lax.broadcasted_iota(jnp.int32, (EXTRA, 1), 0)
    out = jnp.zeros((EXTRA, width), F32)
    for k in range(count):
        out = jnp.where(place == k, rows[k : k + 1, :], out)
    return out.astype(kind)


def forward(place, planes, at, degree, kind):
    lines, half, rows = planes[0].shape
    width = 2 * half
    sources = at.shape[0] - 1
    per = rows // 128

    def chunk(j, place):
        return (0, 2 * lax.rem(place[0] + j, 4) + place[1], 0, 0)

    return pl.pallas_call(
        forward_kernel,
        out_shape=jax.ShapeDtypeStruct((4, width + EXTRA, rows), kind),
        grid_spec=pltpu.PrefetchScalarGridSpec(
            num_scalar_prefetch=1,
            grid=(4,),
            in_specs=[pl.BlockSpec((lines, half, rows), lambda j, *_: (0, 0, 0))] * 8
            + [pl.BlockSpec((sources, per, 128, 128), chunk)]
            + [pl.BlockSpec((1, rows), lambda j, place: chunk(j, place)[:2])],
            out_specs=pl.BlockSpec((1, width + EXTRA, rows), lambda j, *_: (j, 0, 0)),
            scratch_shapes=[pltpu.VMEM((width, sources * 128), BF)],
        ),
        compiler_params=params(20),
        cost_estimate=cost(8 * sources * 128 * rows * width, 10 << 20),
        name="forward",
    )(place, *planes, at, degree)


def backward_kernel(place_ref, *refs):
    parts, at_ref, out_ref, grads = refs[:8], refs[8], refs[9], refs[10]
    rows = parts[0].shape[0]

    @pl.when(pl.program_id(0) == 0)
    def _():
        for k in range(4):
            chunk = 2 * lax.rem(place_ref[0] + 4 - k, 4)
            own = pl.multiple_of((chunk + place_ref[1]) * rows, rows)
            other = pl.multiple_of((chunk + 1 - place_ref[1]) * rows, rows)
            grads[pl.ds(own, rows), :] = parts[k][...]
            grads[pl.ds(other, rows), :] = parts[4 + k][...]

    for k in range(at_ref.shape[0]):
        block = jnp.concatenate([at_ref[k, r] for r in range(at_ref.shape[1])], axis=1)
        got = jnp.dot(block, grads[...], preferred_element_type=F32)
        out_ref[k * 128 : (k + 1) * 128, :] = got.astype(BF)


def backward(place, parts, at):
    sources, dests = at.shape[0] - 1, at.shape[1]
    rows, width = parts[0].shape
    per = 8
    return pl.pallas_call(
        backward_kernel,
        out_shape=in_hbm((sources * 128, width), BF),
        grid_spec=pltpu.PrefetchScalarGridSpec(
            num_scalar_prefetch=1,
            grid=(sources // per,),
            in_specs=[pl.BlockSpec((rows, width), lambda i, *_: (0, 0))] * 8
            + [pl.BlockSpec((per, dests, 128, 128), lambda i, *_: (i, 0, 0, 0))],
            out_specs=pl.BlockSpec((per * 128, width), lambda i, *_: (i, 0)),
            scratch_shapes=[pltpu.VMEM((dests * 128, width), BF)],
        ),
        compiler_params=params(20),
        cost_estimate=cost(2 * sources * 128 * dests * 128 * width, 20 << 20),
        name="backward",
    )(place, *parts, at)


def dot_on(a, b, da, db):
    return lax.dot_general(a, b, (((da,), (db,)), ((), ())), preferred_element_type=F32)


def mix_kernel(keep_ref, taken_ref, own_ref, *outs):
    width = own_ref.shape[0] - EXTRA
    own_ref[...] = keep_ref[0] + taken_ref[0].astype(F32)
    for k, out_ref in enumerate(outs):
        both = keep_ref[k + 1] + taken_ref[k + 1].astype(F32)
        out_ref[0:width, :] = both[0:width].astype(BF)
        degree = both[width : width + 1] + both[width + 1 : width + 2]
        out_ref[width:, :] = spaced(two_rows(degree), BF)


def mix(keep, taken):
    shape = keep.shape[1:]
    return pl.pallas_call(
        mix_kernel,
        out_shape=(jax.ShapeDtypeStruct(shape, F32),) + (jax.ShapeDtypeStruct(shape, BF),) * 3,
        compiler_params=params(16),
        cost_estimate=cost(1 << 18, 2 << 20),
        name="mix",
    )(keep, taken)


def middle_kernel(
    own_ref, r1_ref, r2_ref, r3_ref, x_ref, ws_ref, wn_ref, bias_ref, cot_ref,
    out_ref, pre_ref, mean_ref, grad_ref,
):
    width = x_ref.shape[1]
    summed = (own_ref[...] + r2_ref[...].astype(F32)) + (
        r1_ref[...].astype(F32) + r3_ref[...].astype(F32)
    )
    degree = jnp.maximum(summed[width : width + 1] + summed[width + 1 : width + 2], 1.0)
    summed = summed[0:width]
    mean_t = (summed / degree).astype(BF)
    mean_ref[...] = mean_t
    preact = (
        jnp.dot(x_ref[...], ws_ref[...], preferred_element_type=F32)
        + dot_on(mean_t, wn_ref[...], 0, 0)
        + bias_ref[...]
    )
    sig = 1.0 / (1.0 + jnp.exp(-preact))
    out_ref[...] = (preact * sig).astype(BF)
    pre_grad = (cot_ref[...].astype(F32) * sig * (1.0 + preact * (1.0 - sig))).astype(BF)
    pre_ref[...] = pre_grad
    grad_t = dot_on(wn_ref[...], pre_grad, 1, 1) / degree
    grad_ref[...] = grad_t.T.astype(BF)


def middle(own, got, x, ws, wn, bias, cot):
    n = x.shape[0]
    shape = jax.ShapeDtypeStruct((n, n), BF)
    return pl.pallas_call(
        middle_kernel,
        out_shape=(shape, shape, shape, shape),
        compiler_params=params(16),
        cost_estimate=cost(6 * n * n * n, 2 << 20, n * n),
        name="middle",
    )(own, *got, x, ws, wn, bias, cot)


def weights_kernel(x_ref, pre_ref, mean_ref, ws_ref, part_ref, self_ref):
    n = x_ref.shape[0]
    pre_grad = pre_ref[...]
    part_ref[0:n, :] = dot_on(x_ref[...], pre_grad, 0, 0).astype(BF)
    neigh_grad = jnp.dot(mean_ref[...], pre_grad, preferred_element_type=F32)
    part_ref[n : 2 * n, :] = neigh_grad.astype(BF)
    bias_grad = jnp.sum(pre_grad.astype(F32), axis=0, keepdims=True)
    part_ref[2 * n :, :] = spaced(bias_grad, BF)
    self_ref[...] = dot_on(pre_grad, ws_ref[...], 1, 1)


def weights(x, pre_grad, mean_t, ws):
    n = x.shape[0]
    return pl.pallas_call(
        weights_kernel,
        out_shape=(
            jax.ShapeDtypeStruct((2 * n + EXTRA, n), BF),
            jax.ShapeDtypeStruct((n, n), F32),
        ),
        compiler_params=params(16),
        cost_estimate=cost(6 * n * n * n, 2 << 20),
        name="weights",
    )(x, pre_grad, mean_t, ws)


def finish_kernel(parts_ref, self_ref, out_ref):
    total = self_ref[...]
    for k in range(parts_ref.shape[0]):
        total += parts_ref[k].astype(F32)
    out_ref[...] = total.astype(BF)


def finish(parts, self_part):
    return pl.pallas_call(
        finish_kernel,
        out_shape=jax.ShapeDtypeStruct(self_part.shape, BF),
        compiler_params=params(16),
        cost_estimate=cost(1 << 20, 2 << 20),
        name="finish",
    )(parts, self_part)


def swap(x, axis):
    return lax.all_to_all(x, axis, 0, 0, tiled=True)


def along_y(step):
    return [(2 * y + c, 2 * ((y + step) % 4) + c) for y in range(4) for c in range(2)]


def send_node(x, dx, dz):
    moves = [
        (4 * i + j, 4 * ((i + dx) % 4) + (j + dz) % 4) for i in range(4) for j in range(4)
    ]
    return lax.ppermute(x, "nodes", moves)


def send_flip(x, bit):
    moves = [(4 * i + j, 4 * (i ^ bit) + j) for i in range(4) for j in range(4)]
    return lax.ppermute(x, "nodes", moves)


PARTNER = [(i, i ^ 1) for i in range(8)]


def send_y(x, step):
    return lax.ppermute(x, "cols", along_y(step))


def send_core(x):
    return lax.ppermute(x, "cols", PARTNER)


def add_terms(terms):
    own, one, two, three = (x.astype(F32) for x in terms)
    return (own + two) + (one + three)


def send_x(x, step):
    return send_node(x, step, 0)


def send_z(x, step):
    return send_node(x, 0, step)


def shards(node_feats, tile_row, tile_col, tile_bits, w_self, w_neigh, bias, cotangent):
    nodes = lax.axis_size("nodes")
    cols = lax.axis_size("cols")
    rows_dev, width = node_feats.shape
    me, node = lax.axis_index("cols"), lax.axis_index("nodes")
    y, core = me // 2, me % 2
    mine = jnp.stack([y, core, node // 4, node % 4]).astype(jnp.int32)
    theirs = jnp.stack([y, 1 - core, node // 4, node % 4]).astype(jnp.int32)

    top, low = prepare(node_feats)
    top = jnp.stack([top] + [send_x(top, k) for k in (1, 2, 3)])
    low = jnp.stack([low] + [send_z(low, k) for k in (1, 2, 3)])
    top, low, mine, theirs, zero = lax.optimization_barrier((top, low, mine, theirs, core == 0))
    planes = [top] + [send_z(top, k) for k in (1, 2, 3)]
    planes += [low] + [send_x(low, k) for k in (1, 2, 3)]
    at, degree = build(
        *(pltpu.with_memory_space_constraint(t, pltpu.HBM) for t in (tile_row, tile_col, tile_bits)),
        top,
        nodes * rows_dev // 128, cols * rows_dev // 128
    )

    give = forward(theirs, planes, at, degree, BF)
    taken = send_core(give)
    keep = forward(mine, planes, at, degree, F32)
    own, *sent = mix(keep, taken)
    got = [send_y(sent[k - 1], k) for k in (1, 2, 3)]
    layer_out, pre_grad, mean_t, mean_grad = middle(
        own, got, node_feats, w_self, w_neigh, bias.reshape(1, -1), cotangent
    )
    same_core = [mean_grad] + [send_y(mean_grad, k) for k in (1, 2, 3)]

    part, self_part = weights(node_feats, pre_grad, mean_t, w_self)
    part = (part.astype(F32) + send_flip(part, 1).astype(F32)).astype(BF)
    other_core = [send_core(g) for g in same_core]
    flipped = send_flip(part, 2)

    src = backward(mine, same_core + other_core, at)
    src, part, flipped = lax.optimization_barrier((src, part, flipped))
    parts = swap(src.reshape(nodes, rows_dev, width), "nodes")

    part = (part.astype(F32) + flipped.astype(F32)).astype(BF)
    halves = (part[:width], part[width : 2 * width])
    kept = jnp.concatenate([jnp.where(zero, *halves), part[2 * width :]])
    given = jnp.concatenate([jnp.where(zero, *halves[::-1]), part[2 * width :]])
    part = (kept.astype(F32) + send_core(given).astype(F32)).astype(BF)
    part = add_terms([part] + [send_y(part, k) for k in (1, 2, 3)]).astype(BF)
    part = add_terms([part] + [send_z(part, k) for k in (1, 2, 3)])
    other = send_core(part)
    bias_grad = part[width]
    self_grad = jnp.where(zero, part[:width], other[:width])
    neigh_grad = jnp.where(zero, other[:width], part[:width])

    feat_grad = finish(parts, self_part)
    return (layer_out, feat_grad, self_grad, neigh_grad, bias_grad)


def solution(mesh):
    return jax.shard_map(
        shards,
        mesh=mesh,
        in_specs=(
            P(("nodes", "cols"), None),
            P("nodes", "cols"),
            P("nodes", "cols"),
            P("nodes", "cols", None, None),
            P(),
            P(),
            P(),
            P(("nodes", "cols"), None),
        ),
        out_specs=(P(("nodes", "cols"), None), P(("nodes", "cols"), None), P(), P(), P()),
        check_vma=False,
    )
```

```python
import jax
import jax.numpy as jnp
from jax import lax
from jax.experimental import pallas as pl
from jax.experimental.pallas import tpu as pltpu
from jax.sharding import PartitionSpec as P

BF = jnp.bfloat16
F32 = jnp.float32
EXACT = 256
EXTRA = 16


def params(mib):
    return pltpu.CompilerParams(vmem_limit_bytes=mib << 20)


def in_hbm(shape, kind):
    return pltpu.HBM(shape, kind)


def cost(flops, moved, transcendentals=0):
    return pl.CostEstimate(flops=flops, bytes_accessed=moved, transcendentals=transcendentals)


def prepare_kernel(x_ref, top_ref, low_ref):
    half = top_ref.shape[0]
    flipped = x_ref[...].T
    top_ref[...] = flipped[:half]
    low_ref[...] = flipped[half:]


def prepare(x):
    rows, width = x.shape
    shape = jax.ShapeDtypeStruct((width // 2, rows), BF)
    return pl.pallas_call(
        prepare_kernel,
        out_shape=(shape, shape),
        compiler_params=params(8),
        cost_estimate=cost(0, 1 << 18),
        name="prepare",
    )(x)


def build_kernel(
    rows_ref, cols_ref, bits_all, gate_ref, at_ref, deg_ref,
    deg8, count, spill, row_ref, col_ref, bits_ref, sems,
):
    sources = at_ref.shape[0] - 1
    dests = at_ref.shape[1]
    tiles = bits_ref.shape[0]
    pieces = 4
    each = tiles // pieces

    def fetch(k):
        part = pl.ds(k * each, each)
        return pltpu.make_async_copy(bits_all.at[0, part], bits_ref.at[part], sems.at[2 + k])

    copies = [
        pltpu.make_async_copy(rows_ref, row_ref, sems.at[0]),
        pltpu.make_async_copy(cols_ref, col_ref, sems.at[1]),
    ] + [fetch(k) for k in range(pieces)]
    for copy in copies:
        copy.start()
    for r in range(dests):
        deg8[r] = jnp.zeros((8, 128), F32)

    def clear(k, carry):
        for r in range(dests):
            at_ref[k, r] = jnp.zeros((128, 128), BF)
            count[k * dests + r] = 0
        return carry

    lax.fori_loop(0, sources, clear, 0)
    at_ref[sources, 0] = jnp.zeros((128, 128), BF)
    spill[0] = -1
    shifts = lax.broadcasted_iota(jnp.int32, (8, 128), 0)

    def add_tile(t, carry):
        row = row_ref[0, t]
        col = col_ref[0, t]
        slot = col * dests + row
        seen = count[slot]
        count[slot] = seen + 1
        full = seen >= EXACT
        spill[0] = jnp.where(full, slot, spill[0])
        to_col = jnp.where(full, sources, col)
        to_row = jnp.where(full, 0, row)
        total = None
        for i in range(8):
            flags = []
            for w in (2 * i, 2 * i + 1):
                word = jnp.broadcast_to(bits_ref[t, w : w + 1, :], (8, 128))
                flags.append((jnp.right_shift(word, shifts) & 1).astype(F32))
            pair = flags[0] + flags[1]
            total = pair if total is None else total + pair
            at_ref[to_col, to_row, 16 * i : 16 * i + 16, :] += jnp.concatenate(flags, 0).astype(BF)
        deg8[row] += total
        return carry

    copies[0].wait()
    copies[1].wait()
    for k in range(pieces):
        copies[2 + k].wait()
        lax.fori_loop(k * each, (k + 1) * each, add_tile, 0, unroll=2)

    @pl.when(spill[0] >= 0)
    def _():
        slot = spill[0]
        col = lax.div(slot, dests)
        row = lax.rem(slot, dests)
        whole = at_ref[col, row].astype(F32) + at_ref[sources, 0].astype(F32)
        at_ref[col, row] = whole.astype(BF)

    for r in range(dests):
        deg_ref[:, r * 128 : (r + 1) * 128] = jnp.sum(deg8[r], axis=0, keepdims=True)


def build(rows, cols, bits, gate, sources, dests):
    tiles = bits.shape[1]
    assert tiles <= 2 * EXACT and tiles % 8 == 0
    hbm = pl.BlockSpec(memory_space=pltpu.HBM)
    vmem = pl.BlockSpec(memory_space=pltpu.VMEM)
    return pl.pallas_call(
        build_kernel,
        out_shape=(
            jax.ShapeDtypeStruct((sources + 1, dests, 128, 128), BF),
            jax.ShapeDtypeStruct((1, dests * 128), F32),
        ),
        in_specs=[hbm, hbm, hbm, pl.BlockSpec(memory_space=pl.ANY)],
        out_specs=(vmem, vmem),
        scratch_shapes=[
            pltpu.VMEM((dests, 8, 128), F32),
            pltpu.SMEM((sources * dests,), jnp.int32),
            pltpu.SMEM((1,), jnp.int32),
            pltpu.SMEM((1, tiles), jnp.int32),
            pltpu.SMEM((1, tiles), jnp.int32),
            pltpu.VMEM((tiles, 16, 128), jnp.int32),
            pltpu.SemaphoreType.DMA((6,)),
        ],
        compiler_params=params(24),
        cost_estimate=cost(0, 30 << 20),
        name="build",
    )(rows, cols, bits, gate)


def forward_kernel(place_ref, *refs):
    tops, lows = refs[:4], refs[4:8]
    at_ref, deg_ref, out_ref, joined = refs[8:]
    half, rows = tops[0].shape[1:]
    width = 2 * half
    per = rows // 128
    for kx in range(4):
        x = lax.rem(place_ref[2] + 4 - kx, 4)
        for kz in range(4):
            n = 4 * x + lax.rem(place_ref[3] + 4 - kz, 4)
            lanes = pl.ds(pl.multiple_of(n * rows, rows), rows)
            joined[0:half, lanes] = tops[kz][kx]
            joined[half:width, lanes] = lows[kx][kz]

    def dest(j, carry):
        chunk = 2 * lax.rem(place_ref[0] + j, 4) + place_ref[1]
        blocks = [
            jnp.concatenate([at_ref[k, per * chunk + r] for r in range(per)], axis=1)
            for k in range(at_ref.shape[0] - 1)
        ]
        part = jnp.dot(joined[...], jnp.concatenate(blocks, axis=0), preferred_element_type=F32)
        out_ref[j, 0:width, :] = part.astype(out_ref.dtype)
        whole = deg_ref[:, pl.ds(pl.multiple_of(chunk * rows, rows), rows)]
        degree = whole if out_ref.dtype == F32 else two_rows(whole)
        out_ref[j, width:, :] = spaced(degree, out_ref.dtype)
        return carry

    lax.fori_loop(0, 4, dest, 0)


def two_rows(whole):
    high = whole.astype(BF).astype(F32)
    first = lax.broadcasted_iota(jnp.int32, (2, 1), 0) == 0
    return jnp.where(first, high, whole - high)


def spaced(rows, kind):
    count, width = rows.shape
    place = lax.broadcasted_iota(jnp.int32, (EXTRA, 1), 0)
    out = jnp.zeros((EXTRA, width), F32)
    for k in range(count):
        out = jnp.where(place == k, rows[k : k + 1, :], out)
    return out.astype(kind)


def forward(place, planes, at, degree, kind):
    _, half, rows = planes[0].shape
    width = 2 * half
    sources = at.shape[0] - 1
    vmem = pl.BlockSpec(memory_space=pltpu.VMEM)
    return pl.pallas_call(
        forward_kernel,
        out_shape=jax.ShapeDtypeStruct((4, width + EXTRA, rows), kind),
        in_specs=[pl.BlockSpec(memory_space=pltpu.SMEM)] + [vmem] * 10,
        out_specs=vmem,
        scratch_shapes=[pltpu.VMEM((width, sources * 128), BF)],
        compiler_params=params(20),
        cost_estimate=cost(8 * sources * 128 * rows * width, 10 << 20),
        name="forward",
    )(place, *planes, at, degree)


def backward_kernel(place_ref, *refs):
    parts, at_ref, out_ref, grads, held, sems = refs[:8], *refs[8:]
    rows = parts[0].shape[0]
    for k in range(4):
        chunk = 2 * lax.rem(place_ref[0] + 4 - k, 4)
        own = pl.multiple_of((chunk + place_ref[1]) * rows, rows)
        other = pl.multiple_of((chunk + 1 - place_ref[1]) * rows, rows)
        grads[pl.ds(own, rows), :] = parts[k][...]
        grads[pl.ds(other, rows), :] = parts[4 + k][...]
    pieces, each, _ = held.shape

    def copy(i):
        into = out_ref.at[pl.ds(pl.multiple_of(i * each, each), each)]
        return pltpu.make_async_copy(held.at[i], into, sems.at[i])

    def piece(i, carry):
        for k in range(each // 128):
            at = i * (each // 128) + k
            block = jnp.concatenate([at_ref[at, r] for r in range(at_ref.shape[1])], axis=1)
            got = jnp.dot(block, grads[...], preferred_element_type=F32)
            held[i, k * 128 : (k + 1) * 128, :] = got.astype(BF)
        copy(i).start()
        return carry

    lax.fori_loop(0, pieces, piece, 0)
    for i in range(pieces):
        copy(i).wait()


def backward(place, parts, at):
    sources, dests = at.shape[0] - 1, at.shape[1]
    _, width = parts[0].shape
    pieces = 8
    vmem = pl.BlockSpec(memory_space=pltpu.VMEM)
    return pl.pallas_call(
        backward_kernel,
        out_shape=in_hbm((sources * 128, width), BF),
        in_specs=[pl.BlockSpec(memory_space=pltpu.SMEM)] + [vmem] * 9,
        out_specs=pl.BlockSpec(memory_space=pltpu.HBM),
        scratch_shapes=[
            pltpu.VMEM((dests * 128, width), BF),
            pltpu.VMEM((pieces, sources * 128 // pieces, width), BF),
            pltpu.SemaphoreType.DMA((pieces,)),
        ],
        compiler_params=params(20),
        cost_estimate=cost(2 * sources * 128 * dests * 128 * width, 20 << 20),
        name="backward",
    )(place, *parts, at)


def dot_on(a, b, da, db):
    return lax.dot_general(a, b, (((da,), (db,)), ((), ())), preferred_element_type=F32)


def mix_kernel(keep_ref, taken_ref, own_ref, *outs):
    width = own_ref.shape[0] - EXTRA
    own_ref[...] = keep_ref[0] + taken_ref[0].astype(F32)
    for k, out_ref in enumerate(outs):
        both = keep_ref[k + 1] + taken_ref[k + 1].astype(F32)
        out_ref[0:width, :] = both[0:width].astype(BF)
        degree = both[width : width + 1] + both[width + 1 : width + 2]
        out_ref[width:, :] = spaced(two_rows(degree), BF)


def mix(keep, taken):
    shape = keep.shape[1:]
    return pl.pallas_call(
        mix_kernel,
        out_shape=(jax.ShapeDtypeStruct(shape, F32),) + (jax.ShapeDtypeStruct(shape, BF),) * 3,
        compiler_params=params(16),
        cost_estimate=cost(1 << 18, 2 << 20),
        name="mix",
    )(keep, taken)


def middle_kernel(
    own_ref, r1_ref, r2_ref, r3_ref, x_ref, ws_ref, wn_ref, bias_ref, cot_ref,
    out_ref, pre_ref, mean_ref, grad_ref,
):
    width = x_ref.shape[1]
    summed = (own_ref[...] + r2_ref[...].astype(F32)) + (
        r1_ref[...].astype(F32) + r3_ref[...].astype(F32)
    )
    degree = jnp.maximum(summed[width : width + 1] + summed[width + 1 : width + 2], 1.0)
    summed = summed[0:width]
    mean_t = (summed / degree).astype(BF)
    mean_ref[...] = mean_t
    preact = (
        jnp.dot(x_ref[...], ws_ref[...], preferred_element_type=F32)
        + dot_on(mean_t, wn_ref[...], 0, 0)
        + bias_ref[...]
    )
    sig = 1.0 / (1.0 + jnp.exp(-preact))
    out_ref[...] = (preact * sig).astype(BF)
    pre_grad = (cot_ref[...].astype(F32) * sig * (1.0 + preact * (1.0 - sig))).astype(BF)
    pre_ref[...] = pre_grad
    grad_t = dot_on(wn_ref[...], pre_grad, 1, 1) / degree
    grad_ref[...] = grad_t.T.astype(BF)


def middle(own, got, x, ws, wn, bias, cot):
    n = x.shape[0]
    shape = jax.ShapeDtypeStruct((n, n), BF)
    return pl.pallas_call(
        middle_kernel,
        out_shape=(shape, shape, shape, shape),
        compiler_params=params(16),
        cost_estimate=cost(6 * n * n * n, 2 << 20, n * n),
        name="middle",
    )(own, *got, x, ws, wn, bias, cot)


def weights_kernel(x_ref, pre_ref, mean_ref, ws_ref, part_ref, self_ref):
    n = x_ref.shape[0]
    pre_grad = pre_ref[...]
    part_ref[0:n, :] = dot_on(x_ref[...], pre_grad, 0, 0).astype(BF)
    neigh_grad = jnp.dot(mean_ref[...], pre_grad, preferred_element_type=F32)
    part_ref[n : 2 * n, :] = neigh_grad.astype(BF)
    bias_grad = jnp.sum(pre_grad.astype(F32), axis=0, keepdims=True)
    part_ref[2 * n :, :] = spaced(bias_grad, BF)
    self_ref[...] = dot_on(pre_grad, ws_ref[...], 1, 1)


def weights(x, pre_grad, mean_t, ws):
    n = x.shape[0]
    return pl.pallas_call(
        weights_kernel,
        out_shape=(
            jax.ShapeDtypeStruct((2 * n + EXTRA, n), BF),
            jax.ShapeDtypeStruct((n, n), F32),
        ),
        compiler_params=params(16),
        cost_estimate=cost(6 * n * n * n, 2 << 20),
        name="weights",
    )(x, pre_grad, mean_t, ws)


def finish_kernel(parts_ref, self_ref, out_ref):
    total = self_ref[...]
    for k in range(parts_ref.shape[0]):
        total += parts_ref[k].astype(F32)
    out_ref[...] = total.astype(BF)


def finish(parts, self_part):
    return pl.pallas_call(
        finish_kernel,
        out_shape=jax.ShapeDtypeStruct(self_part.shape, BF),
        compiler_params=params(16),
        cost_estimate=cost(1 << 20, 2 << 20),
        name="finish",
    )(parts, self_part)


def swap(x, axis):
    return lax.all_to_all(x, axis, 0, 0, tiled=True)


def along_y(step):
    return [(2 * y + c, 2 * ((y + step) % 4) + c) for y in range(4) for c in range(2)]


def send_node(x, dx, dz):
    moves = [
        (4 * i + j, 4 * ((i + dx) % 4) + (j + dz) % 4) for i in range(4) for j in range(4)
    ]
    return lax.ppermute(x, "nodes", moves)


def send_flip(x, bit):
    moves = [(4 * i + j, 4 * (i ^ bit) + j) for i in range(4) for j in range(4)]
    return lax.ppermute(x, "nodes", moves)


PARTNER = [(i, i ^ 1) for i in range(8)]


def send_y(x, step):
    return lax.ppermute(x, "cols", along_y(step))


def send_core(x):
    return lax.ppermute(x, "cols", PARTNER)


def add_terms(terms):
    own, one, two, three = (x.astype(F32) for x in terms)
    return (own + two) + (one + three)


def send_x(x, step):
    return send_node(x, step, 0)


def send_z(x, step):
    return send_node(x, 0, step)


def shards(node_feats, tile_row, tile_col, tile_bits, w_self, w_neigh, bias, cotangent):
    nodes = lax.axis_size("nodes")
    cols = lax.axis_size("cols")
    rows_dev, width = node_feats.shape
    me, node = lax.axis_index("cols"), lax.axis_index("nodes")
    y, core = me // 2, me % 2
    mine = jnp.stack([y, core, node // 4, node % 4]).astype(jnp.int32)
    theirs = jnp.stack([y, 1 - core, node // 4, node % 4]).astype(jnp.int32)

    top, low = prepare(node_feats)
    top = jnp.stack([top] + [send_x(top, k) for k in (1, 2, 3)])
    low = jnp.stack([low] + [send_z(low, k) for k in (1, 2, 3)])
    top, low, mine, theirs, zero = lax.optimization_barrier((top, low, mine, theirs, core == 0))
    planes = [top] + [send_z(top, k) for k in (1, 2, 3)]
    planes += [low] + [send_x(low, k) for k in (1, 2, 3)]
    at, degree = build(
        *(pltpu.with_memory_space_constraint(t, pltpu.HBM) for t in (tile_row, tile_col, tile_bits)),
        top,
        nodes * rows_dev // 128, cols * rows_dev // 128
    )

    give = forward(theirs, planes, at, degree, BF)
    taken = send_core(give)
    keep = forward(mine, planes, at, degree, F32)
    own, *sent = mix(keep, taken)
    far = send_y(sent[1], 2)
    got = [send_y(sent[0], 1), far, send_y(sent[2], 3)]
    layer_out, pre_grad, mean_t, mean_grad = middle(
        own, got, node_feats, w_self, w_neigh, bias.reshape(1, -1), cotangent
    )
    next_y, last_y = send_y(mean_grad, 1), send_y(mean_grad, 3)
    same_core = [mean_grad, next_y, send_y(mean_grad, 2), last_y]

    part, self_part = weights(node_feats, pre_grad, mean_t, w_self)
    part = (part.astype(F32) + send_flip(part, 1).astype(F32)).astype(BF)
    other_core = [send_core(g) for g in same_core]
    flipped = send_flip(part, 2)

    src = backward(mine, same_core + other_core, at)
    src, part, flipped = lax.optimization_barrier((src, part, flipped))
    parts = swap(src.reshape(nodes, rows_dev, width), "nodes")

    part = (part.astype(F32) + flipped.astype(F32)).astype(BF)
    halves = (part[:width], part[width : 2 * width])
    kept = jnp.concatenate([jnp.where(zero, *halves), part[2 * width :]])
    given = jnp.concatenate([jnp.where(zero, *halves[::-1]), part[2 * width :]])
    part = (kept.astype(F32) + send_core(given).astype(F32)).astype(BF)
    part = add_terms([part] + [send_y(part, k) for k in (1, 2, 3)]).astype(BF)
    part = add_terms([part] + [send_z(part, k) for k in (1, 2, 3)])
    other = send_core(part)
    bias_grad = part[width]
    self_grad = jnp.where(zero, part[:width], other[:width])
    neigh_grad = jnp.where(zero, other[:width], part[:width])

    feat_grad = finish(parts, self_part)
    return (layer_out, feat_grad, self_grad, neigh_grad, bias_grad)


def solution(mesh):
    return jax.shard_map(
        shards,
        mesh=mesh,
        in_specs=(
            P(("nodes", "cols"), None),
            P("nodes", "cols"),
            P("nodes", "cols"),
            P("nodes", "cols", None, None),
            P(),
            P(),
            P(),
            P(("nodes", "cols"), None),
        ),
        out_specs=(P(("nodes", "cols"), None), P(("nodes", "cols"), None), P(), P(), P()),
        check_vma=False,
    )
```

```python
import jax
import jax.numpy as jnp
from jax import lax
from jax.experimental import pallas as pl
from jax.experimental.pallas import tpu as pltpu
from jax.sharding import PartitionSpec as P

BF = jnp.bfloat16
F32 = jnp.float32
EXACT = 256
EXTRA = 16


def params(mib):
    return pltpu.CompilerParams(vmem_limit_bytes=mib << 20)


def in_hbm(shape, kind):
    return pltpu.HBM(shape, kind)


def cost(flops, moved, transcendentals=0):
    return pl.CostEstimate(flops=flops, bytes_accessed=moved, transcendentals=transcendentals)


def prepare_kernel(x_ref, top_ref, low_ref):
    half = top_ref.shape[0]
    flipped = x_ref[...].T
    top_ref[...] = flipped[:half]
    low_ref[...] = flipped[half:]


def prepare(x):
    rows, width = x.shape
    shape = jax.ShapeDtypeStruct((width // 2, rows), BF)
    return pl.pallas_call(
        prepare_kernel,
        out_shape=(shape, shape),
        compiler_params=params(8),
        cost_estimate=cost(0, 1 << 18),
        name="prepare",
    )(x)


def build_kernel(
    rows_ref, cols_ref, bits_all, gate_ref, at_ref, deg_ref,
    deg8, count, spill, row_ref, col_ref, bits_ref, sems,
):
    sources = at_ref.shape[0] - 1
    dests = at_ref.shape[1]
    tiles = bits_ref.shape[0]
    pieces = 4
    each = tiles // pieces

    def fetch(k):
        part = pl.ds(k * each, each)
        return pltpu.make_async_copy(bits_all.at[0, part], bits_ref.at[part], sems.at[2 + k])

    copies = [
        pltpu.make_async_copy(rows_ref, row_ref, sems.at[0]),
        pltpu.make_async_copy(cols_ref, col_ref, sems.at[1]),
    ] + [fetch(k) for k in range(pieces)]
    for copy in copies:
        copy.start()
    for r in range(dests):
        deg8[r] = jnp.zeros((8, 128), F32)

    def clear(k, carry):
        for r in range(dests):
            at_ref[k, r] = jnp.zeros((128, 128), BF)
            count[k * dests + r] = 0
        return carry

    lax.fori_loop(0, sources, clear, 0)
    at_ref[sources, 0] = jnp.zeros((128, 128), BF)
    spill[0] = -1
    shifts = lax.broadcasted_iota(jnp.int32, (8, 128), 0)

    def add_tile(t, carry):
        row = row_ref[0, t]
        col = col_ref[0, t]
        slot = col * dests + row
        seen = count[slot]
        count[slot] = seen + 1
        full = seen >= EXACT
        spill[0] = jnp.where(full, slot, spill[0])
        to_col = jnp.where(full, sources, col)
        to_row = jnp.where(full, 0, row)
        total = None
        for i in range(8):
            flags = []
            for w in (2 * i, 2 * i + 1):
                word = jnp.broadcast_to(bits_ref[t, w : w + 1, :], (8, 128))
                flags.append((jnp.right_shift(word, shifts) & 1).astype(F32))
            pair = flags[0] + flags[1]
            total = pair if total is None else total + pair
            at_ref[to_col, to_row, 16 * i : 16 * i + 16, :] += jnp.concatenate(flags, 0).astype(BF)
        deg8[row] += total
        return carry

    copies[0].wait()
    copies[1].wait()
    for k in range(pieces):
        copies[2 + k].wait()
        lax.fori_loop(k * each, (k + 1) * each, add_tile, 0, unroll=4)

    @pl.when(spill[0] >= 0)
    def _():
        slot = spill[0]
        col = lax.div(slot, dests)
        row = lax.rem(slot, dests)
        whole = at_ref[col, row].astype(F32) + at_ref[sources, 0].astype(F32)
        at_ref[col, row] = whole.astype(BF)

    for r in range(dests):
        deg_ref[:, r * 128 : (r + 1) * 128] = jnp.sum(deg8[r], axis=0, keepdims=True)


def build(rows, cols, bits, gate, sources, dests):
    tiles = bits.shape[1]
    assert tiles <= 2 * EXACT and tiles % 8 == 0
    hbm = pl.BlockSpec(memory_space=pltpu.HBM)
    vmem = pl.BlockSpec(memory_space=pltpu.VMEM)
    return pl.pallas_call(
        build_kernel,
        out_shape=(
            jax.ShapeDtypeStruct((sources + 1, dests, 128, 128), BF),
            jax.ShapeDtypeStruct((1, dests * 128), F32),
        ),
        in_specs=[hbm, hbm, hbm, pl.BlockSpec(memory_space=pl.ANY)],
        out_specs=(vmem, vmem),
        scratch_shapes=[
            pltpu.VMEM((dests, 8, 128), F32),
            pltpu.SMEM((sources * dests,), jnp.int32),
            pltpu.SMEM((1,), jnp.int32),
            pltpu.SMEM((1, tiles), jnp.int32),
            pltpu.SMEM((1, tiles), jnp.int32),
            pltpu.VMEM((tiles, 16, 128), jnp.int32),
            pltpu.SemaphoreType.DMA((6,)),
        ],
        compiler_params=params(24),
        cost_estimate=cost(0, 30 << 20),
        name="build",
    )(rows, cols, bits, gate)


def forward_kernel(place_ref, *refs):
    tops, lows = refs[:4], refs[4:8]
    at_ref, deg_ref, out_ref, joined = refs[8:]
    half, rows = tops[0].shape[1:]
    width = 2 * half
    per = rows // 128
    for kx in range(4):
        x = lax.rem(place_ref[2] + 4 - kx, 4)
        for kz in range(4):
            n = 4 * x + lax.rem(place_ref[3] + 4 - kz, 4)
            lanes = pl.ds(pl.multiple_of(n * rows, rows), rows)
            joined[0:half, lanes] = tops[kz][kx]
            joined[half:width, lanes] = lows[kx][kz]

    for j in range(4):
        chunk = 2 * lax.rem(place_ref[0] + j, 4) + place_ref[1]
        blocks = [
            jnp.concatenate([at_ref[k, per * chunk + r] for r in range(per)], axis=1)
            for k in range(at_ref.shape[0] - 1)
        ]
        part = jnp.dot(joined[...], jnp.concatenate(blocks, axis=0), preferred_element_type=F32)
        out_ref[j, 0:width, :] = part.astype(out_ref.dtype)
        whole = deg_ref[:, pl.ds(pl.multiple_of(chunk * rows, rows), rows)]
        degree = whole if out_ref.dtype == F32 else two_rows(whole)
        out_ref[j, width:, :] = spaced(degree, out_ref.dtype)


def two_rows(whole):
    high = whole.astype(BF).astype(F32)
    first = lax.broadcasted_iota(jnp.int32, (2, 1), 0) == 0
    return jnp.where(first, high, whole - high)


def spaced(rows, kind):
    count, width = rows.shape
    place = lax.broadcasted_iota(jnp.int32, (EXTRA, 1), 0)
    out = jnp.zeros((EXTRA, width), F32)
    for k in range(count):
        out = jnp.where(place == k, rows[k : k + 1, :], out)
    return out.astype(kind)


def forward(place, planes, at, degree, kind):
    _, half, rows = planes[0].shape
    width = 2 * half
    sources = at.shape[0] - 1
    vmem = pl.BlockSpec(memory_space=pltpu.VMEM)
    return pl.pallas_call(
        forward_kernel,
        out_shape=jax.ShapeDtypeStruct((4, width + EXTRA, rows), kind),
        in_specs=[pl.BlockSpec(memory_space=pltpu.SMEM)] + [vmem] * 10,
        out_specs=vmem,
        scratch_shapes=[pltpu.VMEM((width, sources * 128), BF)],
        compiler_params=params(20),
        cost_estimate=cost(8 * sources * 128 * rows * width, 10 << 20),
        name="forward",
    )(place, *planes, at, degree)


def backward_kernel(place_ref, *refs):
    parts, at_ref, out_ref, grads, held, sems = refs[:8], *refs[8:]
    rows = parts[0].shape[0]
    for k in range(4):
        chunk = 2 * lax.rem(place_ref[0] + 4 - k, 4)
        own = pl.multiple_of((chunk + place_ref[1]) * rows, rows)
        other = pl.multiple_of((chunk + 1 - place_ref[1]) * rows, rows)
        grads[pl.ds(own, rows), :] = parts[k][...]
        grads[pl.ds(other, rows), :] = parts[4 + k][...]
    pieces, each, _ = held.shape

    def copy(i):
        into = out_ref.at[pl.ds(pl.multiple_of(i * each, each), each)]
        return pltpu.make_async_copy(held.at[i], into, sems.at[i])

    def piece(i, carry):
        for k in range(each // 128):
            at = i * (each // 128) + k
            block = jnp.concatenate([at_ref[at, r] for r in range(at_ref.shape[1])], axis=1)
            got = jnp.dot(block, grads[...], preferred_element_type=F32)
            held[i, k * 128 : (k + 1) * 128, :] = got.astype(BF)
        copy(i).start()
        return carry

    lax.fori_loop(0, pieces, piece, 0)
    for i in range(pieces):
        copy(i).wait()


def backward(place, parts, at):
    sources, dests = at.shape[0] - 1, at.shape[1]
    _, width = parts[0].shape
    pieces = 4
    vmem = pl.BlockSpec(memory_space=pltpu.VMEM)
    return pl.pallas_call(
        backward_kernel,
        out_shape=in_hbm((sources * 128, width), BF),
        in_specs=[pl.BlockSpec(memory_space=pltpu.SMEM)] + [vmem] * 9,
        out_specs=pl.BlockSpec(memory_space=pltpu.HBM),
        scratch_shapes=[
            pltpu.VMEM((dests * 128, width), BF),
            pltpu.VMEM((pieces, sources * 128 // pieces, width), BF),
            pltpu.SemaphoreType.DMA((pieces,)),
        ],
        compiler_params=params(20),
        cost_estimate=cost(2 * sources * 128 * dests * 128 * width, 20 << 20),
        name="backward",
    )(place, *parts, at)


def dot_on(a, b, da, db):
    return lax.dot_general(a, b, (((da,), (db,)), ((), ())), preferred_element_type=F32)


def mix_kernel(keep_ref, taken_ref, own_ref, *outs):
    width = own_ref.shape[0] - EXTRA
    own_ref[...] = keep_ref[0] + taken_ref[0].astype(F32)
    for k, out_ref in enumerate(outs):
        both = keep_ref[k + 1] + taken_ref[k + 1].astype(F32)
        out_ref[0:width, :] = both[0:width].astype(BF)
        degree = both[width : width + 1] + both[width + 1 : width + 2]
        out_ref[width:, :] = spaced(two_rows(degree), BF)


def mix(keep, taken):
    shape = keep.shape[1:]
    return pl.pallas_call(
        mix_kernel,
        out_shape=(jax.ShapeDtypeStruct(shape, F32),) + (jax.ShapeDtypeStruct(shape, BF),) * 3,
        compiler_params=params(16),
        cost_estimate=cost(1 << 18, 2 << 20),
        name="mix",
    )(keep, taken)


def middle_kernel(
    own_ref, r1_ref, r2_ref, r3_ref, x_ref, ws_ref, wn_ref, bias_ref, cot_ref,
    out_ref, pre_ref, mean_ref, grad_ref,
):
    width = x_ref.shape[1]
    summed = (own_ref[...] + r2_ref[...].astype(F32)) + (
        r1_ref[...].astype(F32) + r3_ref[...].astype(F32)
    )
    degree = jnp.maximum(summed[width : width + 1] + summed[width + 1 : width + 2], 1.0)
    summed = summed[0:width]
    mean_t = (summed / degree).astype(BF)
    mean_ref[...] = mean_t
    preact = (
        jnp.dot(x_ref[...], ws_ref[...], preferred_element_type=F32)
        + dot_on(mean_t, wn_ref[...], 0, 0)
        + bias_ref[...]
    )
    sig = 1.0 / (1.0 + jnp.exp(-preact))
    out_ref[...] = (preact * sig).astype(BF)
    pre_grad = (cot_ref[...].astype(F32) * sig * (1.0 + preact * (1.0 - sig))).astype(BF)
    pre_ref[...] = pre_grad
    grad_t = dot_on(wn_ref[...], pre_grad, 1, 1) / degree
    grad_ref[...] = grad_t.T.astype(BF)


def middle(own, got, x, ws, wn, bias, cot):
    n = x.shape[0]
    shape = jax.ShapeDtypeStruct((n, n), BF)
    return pl.pallas_call(
        middle_kernel,
        out_shape=(shape, shape, shape, shape),
        compiler_params=params(16),
        cost_estimate=cost(6 * n * n * n, 2 << 20, n * n),
        name="middle",
    )(own, *got, x, ws, wn, bias, cot)


def weights_kernel(x_ref, pre_ref, mean_ref, ws_ref, part_ref, self_ref):
    n = x_ref.shape[0]
    pre_grad = pre_ref[...]
    part_ref[0:n, :] = dot_on(x_ref[...], pre_grad, 0, 0).astype(BF)
    neigh_grad = jnp.dot(mean_ref[...], pre_grad, preferred_element_type=F32)
    part_ref[n : 2 * n, :] = neigh_grad.astype(BF)
    bias_grad = jnp.sum(pre_grad.astype(F32), axis=0, keepdims=True)
    part_ref[2 * n :, :] = spaced(bias_grad, BF)
    self_ref[...] = dot_on(pre_grad, ws_ref[...], 1, 1)


def weights(x, pre_grad, mean_t, ws):
    n = x.shape[0]
    return pl.pallas_call(
        weights_kernel,
        out_shape=(
            jax.ShapeDtypeStruct((2 * n + EXTRA, n), BF),
            jax.ShapeDtypeStruct((n, n), F32),
        ),
        compiler_params=params(16),
        cost_estimate=cost(6 * n * n * n, 2 << 20),
        name="weights",
    )(x, pre_grad, mean_t, ws)


def finish_kernel(parts_ref, self_ref, out_ref):
    total = self_ref[...]
    for k in range(parts_ref.shape[0]):
        total += parts_ref[k].astype(F32)
    out_ref[...] = total.astype(BF)


def finish(parts, self_part):
    return pl.pallas_call(
        finish_kernel,
        out_shape=jax.ShapeDtypeStruct(self_part.shape, BF),
        compiler_params=params(16),
        cost_estimate=cost(1 << 20, 2 << 20),
        name="finish",
    )(parts, self_part)


def place_grads_kernel(place_ref, part_ref, other_ref, self_ref, neigh_ref, bias_ref):
    width = self_ref.shape[0]
    bias_ref[...] = part_ref[width : width + 1, :]
    for core, (first, second) in enumerate(((part_ref, other_ref), (other_ref, part_ref))):

        @pl.when(place_ref[1] == core)
        def _():
            self_ref[...] = first[0:width, :]
            neigh_ref[...] = second[0:width, :]


def place_grads(place, part, other):
    width = part.shape[1]
    vmem = pl.BlockSpec(memory_space=pltpu.VMEM)
    shape = jax.ShapeDtypeStruct((width, width), F32)
    return pl.pallas_call(
        place_grads_kernel,
        out_shape=(shape, shape, jax.ShapeDtypeStruct((1, width), F32)),
        in_specs=[pl.BlockSpec(memory_space=pltpu.SMEM), vmem, vmem],
        out_specs=(vmem, vmem, vmem),
        compiler_params=params(16),
        cost_estimate=cost(0, 1 << 20),
        name="place_grads",
    )(place, part, other)


def swap(x, axis):
    return lax.all_to_all(x, axis, 0, 0, tiled=True)


def along_y(step):
    return [(2 * y + c, 2 * ((y + step) % 4) + c) for y in range(4) for c in range(2)]


def send_node(x, dx, dz):
    moves = [
        (4 * i + j, 4 * ((i + dx) % 4) + (j + dz) % 4) for i in range(4) for j in range(4)
    ]
    return lax.ppermute(x, "nodes", moves)


def send_flip(x, bit):
    moves = [(4 * i + j, 4 * (i ^ bit) + j) for i in range(4) for j in range(4)]
    return lax.ppermute(x, "nodes", moves)


PARTNER = [(i, i ^ 1) for i in range(8)]


def send_y(x, step):
    return lax.ppermute(x, "cols", along_y(step))


def send_core(x):
    return lax.ppermute(x, "cols", PARTNER)


def add_terms(terms):
    own, one, two, three = (x.astype(F32) for x in terms)
    return (own + two) + (one + three)


def send_x(x, step):
    return send_node(x, step, 0)


def send_z(x, step):
    return send_node(x, 0, step)


def shards(node_feats, tile_row, tile_col, tile_bits, w_self, w_neigh, bias, cotangent):
    nodes = lax.axis_size("nodes")
    cols = lax.axis_size("cols")
    rows_dev, width = node_feats.shape
    me, node = lax.axis_index("cols"), lax.axis_index("nodes")
    y, core = me // 2, me % 2
    mine = jnp.stack([y, core, node // 4, node % 4]).astype(jnp.int32)
    theirs = jnp.stack([y, 1 - core, node // 4, node % 4]).astype(jnp.int32)

    top, low = prepare(node_feats)
    top = jnp.stack([top] + [send_x(top, k) for k in (1, 2, 3)])
    low = jnp.stack([low] + [send_z(low, k) for k in (1, 2, 3)])
    top, low, mine, theirs, zero = lax.optimization_barrier((top, low, mine, theirs, core == 0))
    planes = [top] + [send_z(top, k) for k in (1, 2, 3)]
    planes += [low] + [send_x(low, k) for k in (1, 2, 3)]
    at, degree = build(
        *(pltpu.with_memory_space_constraint(t, pltpu.HBM) for t in (tile_row, tile_col, tile_bits)),
        top,
        nodes * rows_dev // 128, cols * rows_dev // 128
    )

    give = forward(theirs, planes, at, degree, BF)
    taken = send_core(give)
    keep = forward(mine, planes, at, degree, F32)
    own, *sent = mix(keep, taken)
    far = send_y(sent[1], 2)
    got = [send_y(sent[0], 1), far, send_y(sent[2], 3)]
    layer_out, pre_grad, mean_t, mean_grad = middle(
        own, got, node_feats, w_self, w_neigh, bias.reshape(1, -1), cotangent
    )
    next_y, last_y = send_y(mean_grad, 1), send_y(mean_grad, 3)
    same_core = [mean_grad, next_y, send_y(mean_grad, 2), last_y]

    part, self_part = weights(node_feats, pre_grad, mean_t, w_self)
    part = (part.astype(F32) + send_flip(part, 1).astype(F32)).astype(BF)
    other_core = [send_core(g) for g in same_core]
    flipped = send_flip(part, 2)

    src = backward(mine, same_core + other_core, at)
    src, part, flipped = lax.optimization_barrier((src, part, flipped))
    parts = swap(src.reshape(nodes, rows_dev, width), "nodes")

    part = part.astype(F32) + flipped.astype(F32)
    halves = (part[:width], part[width : 2 * width])
    kept = jnp.concatenate([jnp.where(zero, *halves), part[2 * width :]])
    given = jnp.concatenate([jnp.where(zero, *halves[::-1]), part[2 * width :]])
    part = kept + send_core(given)
    part = add_terms([part] + [send_y(part, k) for k in (1, 2, 3)]).astype(BF)
    part = add_terms([part] + [send_z(part, k) for k in (1, 2, 3)])
    self_grad, neigh_grad, bias_grad = place_grads(mine, part, send_core(part))

    feat_grad = finish(parts, self_part)
    return (layer_out, feat_grad, self_grad, neigh_grad, bias_grad[0])


def solution(mesh):
    return jax.shard_map(
        shards,
        mesh=mesh,
        in_specs=(
            P(("nodes", "cols"), None),
            P("nodes", "cols"),
            P("nodes", "cols"),
            P("nodes", "cols", None, None),
            P(),
            P(),
            P(),
            P(("nodes", "cols"), None),
        ),
        out_specs=(P(("nodes", "cols"), None), P(("nodes", "cols"), None), P(), P(), P()),
        check_vma=False,
    )
```

```python
import jax
import jax.numpy as jnp
from jax import lax
from jax.experimental import pallas as pl
from jax.experimental.pallas import tpu as pltpu
from jax.sharding import PartitionSpec as P

BF = jnp.bfloat16
F32 = jnp.float32
EXACT = 256
EXTRA = 16


def params(mib):
    return pltpu.CompilerParams(vmem_limit_bytes=mib << 20)


def in_hbm(shape, kind):
    return pltpu.HBM(shape, kind)


def cost(flops, moved, transcendentals=0):
    return pl.CostEstimate(flops=flops, bytes_accessed=moved, transcendentals=transcendentals)


def prepare_kernel(x_ref, top_ref, low_ref):
    half = top_ref.shape[0]
    flipped = x_ref[...].T
    top_ref[...] = flipped[:half]
    low_ref[...] = flipped[half:]


def prepare(x):
    rows, width = x.shape
    shape = jax.ShapeDtypeStruct((width // 2, rows), BF)
    return pl.pallas_call(
        prepare_kernel,
        out_shape=(shape, shape),
        compiler_params=params(8),
        cost_estimate=cost(0, 1 << 18),
        name="prepare",
    )(x)


def build_kernel(
    rows_ref, cols_ref, bits_all, gate_ref, at_ref, deg_ref,
    deg8, count, spill, row_ref, col_ref, bits_ref, sems,
):
    sources = at_ref.shape[0] - 1
    dests = at_ref.shape[1]
    tiles = bits_ref.shape[0]
    pieces = 4
    each = tiles // pieces

    def fetch(k):
        part = pl.ds(k * each, each)
        return pltpu.make_async_copy(bits_all.at[0, part], bits_ref.at[part], sems.at[2 + k])

    copies = [
        pltpu.make_async_copy(rows_ref, row_ref, sems.at[0]),
        pltpu.make_async_copy(cols_ref, col_ref, sems.at[1]),
    ] + [fetch(k) for k in range(pieces)]
    for copy in copies:
        copy.start()
    for r in range(dests):
        deg8[r] = jnp.zeros((8, 128), F32)

    def clear(k, carry):
        for r in range(dests):
            at_ref[k, r] = jnp.zeros((128, 128), BF)
            count[k * dests + r] = 0
        return carry

    lax.fori_loop(0, sources, clear, 0)
    at_ref[sources, 0] = jnp.zeros((128, 128), BF)
    spill[0] = -1
    shifts = lax.broadcasted_iota(jnp.int32, (8, 128), 0)

    def add_tile(t, carry):
        row = row_ref[0, t]
        col = col_ref[0, t]
        slot = col * dests + row
        seen = count[slot]
        count[slot] = seen + 1
        full = seen >= EXACT
        spill[0] = jnp.where(full, slot, spill[0])
        to_col = jnp.where(full, sources, col)
        to_row = jnp.where(full, 0, row)
        total = None
        for i in range(8):
            flags = []
            for w in (2 * i, 2 * i + 1):
                word = jnp.broadcast_to(bits_ref[t, w : w + 1, :], (8, 128))
                flags.append((jnp.right_shift(word, shifts) & 1).astype(F32))
            pair = flags[0] + flags[1]
            total = pair if total is None else total + pair
            at_ref[to_col, to_row, 16 * i : 16 * i + 16, :] += jnp.concatenate(flags, 0).astype(BF)
        deg8[row] += total
        return carry

    copies[0].wait()
    copies[1].wait()
    for k in range(pieces):
        copies[2 + k].wait()
        lax.fori_loop(k * each, (k + 1) * each, add_tile, 0, unroll=4)

    @pl.when(spill[0] >= 0)
    def _():
        slot = spill[0]
        col = lax.div(slot, dests)
        row = lax.rem(slot, dests)
        whole = at_ref[col, row].astype(F32) + at_ref[sources, 0].astype(F32)
        at_ref[col, row] = whole.astype(BF)

    for r in range(dests):
        deg_ref[:, r * 128 : (r + 1) * 128] = jnp.sum(deg8[r], axis=0, keepdims=True)


def build(rows, cols, bits, gate, sources, dests):
    tiles = bits.shape[1]
    assert tiles <= 2 * EXACT and tiles % 8 == 0
    hbm = pl.BlockSpec(memory_space=pltpu.HBM)
    vmem = pl.BlockSpec(memory_space=pltpu.VMEM)
    return pl.pallas_call(
        build_kernel,
        out_shape=(
            jax.ShapeDtypeStruct((sources + 1, dests, 128, 128), BF),
            jax.ShapeDtypeStruct((1, dests * 128), F32),
        ),
        in_specs=[hbm, hbm, hbm, pl.BlockSpec(memory_space=pl.ANY)],
        out_specs=(vmem, vmem),
        scratch_shapes=[
            pltpu.VMEM((dests, 8, 128), F32),
            pltpu.SMEM((sources * dests,), jnp.int32),
            pltpu.SMEM((1,), jnp.int32),
            pltpu.SMEM((1, tiles), jnp.int32),
            pltpu.SMEM((1, tiles), jnp.int32),
            pltpu.VMEM((tiles, 16, 128), jnp.int32),
            pltpu.SemaphoreType.DMA((6,)),
        ],
        compiler_params=params(24),
        cost_estimate=cost(0, 30 << 20),
        name="build",
    )(rows, cols, bits, gate)


def forward_kernel(place_ref, *refs):
    tops, lows = refs[:4], refs[4:8]
    at_ref, deg_ref, out_ref, joined = refs[8:]
    half, rows = tops[0].shape[1:]
    width = 2 * half
    per = rows // 128
    for kx in range(4):
        x = lax.rem(place_ref[2] + 4 - kx, 4)
        for kz in range(4):
            n = 4 * x + lax.rem(place_ref[3] + 4 - kz, 4)
            lanes = pl.ds(pl.multiple_of(n * rows, rows), rows)
            joined[0:half, lanes] = tops[kz][kx]
            joined[half:width, lanes] = lows[kx][kz]

    for j in range(4):
        chunk = 2 * lax.rem(place_ref[0] + j, 4) + place_ref[1]
        blocks = [
            jnp.concatenate([at_ref[k, per * chunk + r] for r in range(per)], axis=1)
            for k in range(at_ref.shape[0] - 1)
        ]
        part = jnp.dot(joined[...], jnp.concatenate(blocks, axis=0), preferred_element_type=F32)
        out_ref[j, 0:width, :] = part.astype(out_ref.dtype)
        whole = deg_ref[:, pl.ds(pl.multiple_of(chunk * rows, rows), rows)]
        degree = whole if out_ref.dtype == F32 else two_rows(whole)
        out_ref[j, width:, :] = spaced(degree, out_ref.dtype)


def two_rows(whole):
    high = whole.astype(BF).astype(F32)
    first = lax.broadcasted_iota(jnp.int32, (2, 1), 0) == 0
    return jnp.where(first, high, whole - high)


def spaced(rows, kind):
    count, width = rows.shape
    place = lax.broadcasted_iota(jnp.int32, (EXTRA, 1), 0)
    out = jnp.zeros((EXTRA, width), F32)
    for k in range(count):
        out = jnp.where(place == k, rows[k : k + 1, :], out)
    return out.astype(kind)


def forward(place, planes, at, degree, kind):
    _, half, rows = planes[0].shape
    width = 2 * half
    sources = at.shape[0] - 1
    vmem = pl.BlockSpec(memory_space=pltpu.VMEM)
    return pl.pallas_call(
        forward_kernel,
        out_shape=jax.ShapeDtypeStruct((4, width + EXTRA, rows), kind),
        in_specs=[pl.BlockSpec(memory_space=pltpu.SMEM)] + [vmem] * 10,
        out_specs=vmem,
        scratch_shapes=[pltpu.VMEM((width, sources * 128), BF)],
        compiler_params=params(20),
        cost_estimate=cost(8 * sources * 128 * rows * width, 10 << 20),
        name="forward",
    )(place, *planes, at, degree)


def backward_kernel(place_ref, *refs):
    parts, at_ref, out_ref, grads, held, sems = refs[:8], *refs[8:]
    rows = parts[0].shape[0]
    for k in range(4):
        chunk = 2 * lax.rem(place_ref[0] + 4 - k, 4)
        own = pl.multiple_of((chunk + place_ref[1]) * rows, rows)
        other = pl.multiple_of((chunk + 1 - place_ref[1]) * rows, rows)
        grads[pl.ds(own, rows), :] = parts[k][...]
        grads[pl.ds(other, rows), :] = parts[4 + k][...]
    pieces, each, _ = held.shape

    def copy(i):
        into = out_ref.at[pl.ds(pl.multiple_of(i * each, each), each)]
        return pltpu.make_async_copy(held.at[i], into, sems.at[i])

    def piece(i, carry):
        for k in range(each // 128):
            at = i * (each // 128) + k
            block = jnp.concatenate([at_ref[at, r] for r in range(at_ref.shape[1])], axis=1)
            got = jnp.dot(block, grads[...], preferred_element_type=F32)
            held[i, k * 128 : (k + 1) * 128, :] = got.astype(BF)
        copy(i).start()
        return carry

    lax.fori_loop(0, pieces, piece, 0)
    for i in range(pieces):
        copy(i).wait()


def backward(place, parts, at):
    sources, dests = at.shape[0] - 1, at.shape[1]
    _, width = parts[0].shape
    pieces = 4
    vmem = pl.BlockSpec(memory_space=pltpu.VMEM)
    return pl.pallas_call(
        backward_kernel,
        out_shape=in_hbm((sources * 128, width), BF),
        in_specs=[pl.BlockSpec(memory_space=pltpu.SMEM)] + [vmem] * 9,
        out_specs=pl.BlockSpec(memory_space=pltpu.HBM),
        scratch_shapes=[
            pltpu.VMEM((dests * 128, width), BF),
            pltpu.VMEM((pieces, sources * 128 // pieces, width), BF),
            pltpu.SemaphoreType.DMA((pieces,)),
        ],
        compiler_params=params(20),
        cost_estimate=cost(2 * sources * 128 * dests * 128 * width, 20 << 20),
        name="backward",
    )(place, *parts, at)


def dot_on(a, b, da, db):
    return lax.dot_general(a, b, (((da,), (db,)), ((), ())), preferred_element_type=F32)


def mix_kernel(keep_ref, taken_ref, own_ref, *outs):
    width = own_ref.shape[0] - EXTRA
    own_ref[...] = keep_ref[0] + taken_ref[0].astype(F32)
    for k, out_ref in enumerate(outs):
        both = keep_ref[k + 1] + taken_ref[k + 1].astype(F32)
        out_ref[0:width, :] = both[0:width].astype(BF)
        degree = both[width : width + 1] + both[width + 1 : width + 2]
        out_ref[width:, :] = spaced(two_rows(degree), BF)


def mix(keep, taken):
    shape = keep.shape[1:]
    return pl.pallas_call(
        mix_kernel,
        out_shape=(jax.ShapeDtypeStruct(shape, F32),) + (jax.ShapeDtypeStruct(shape, BF),) * 3,
        compiler_params=params(16),
        cost_estimate=cost(1 << 18, 2 << 20),
        name="mix",
    )(keep, taken)


def middle_kernel(
    own_ref, r1_ref, r2_ref, r3_ref, x_ref, ws_ref, wn_ref, bias_ref, cot_ref,
    out_ref, pre_ref, mean_ref, grad_ref,
):
    width = x_ref.shape[1]
    summed = (own_ref[...] + r2_ref[...].astype(F32)) + (
        r1_ref[...].astype(F32) + r3_ref[...].astype(F32)
    )
    degree = jnp.maximum(summed[width : width + 1] + summed[width + 1 : width + 2], 1.0)
    summed = summed[0:width]
    mean_t = (summed / degree).astype(BF)
    mean_ref[...] = mean_t
    preact = (
        jnp.dot(x_ref[...], ws_ref[...], preferred_element_type=F32)
        + dot_on(mean_t, wn_ref[...], 0, 0)
        + bias_ref[...]
    )
    sig = 1.0 / (1.0 + jnp.exp(-preact))
    out_ref[...] = (preact * sig).astype(BF)
    pre_grad = (cot_ref[...].astype(F32) * sig * (1.0 + preact * (1.0 - sig))).astype(BF)
    pre_ref[...] = pre_grad
    grad_t = dot_on(wn_ref[...], pre_grad, 1, 1) / degree
    grad_ref[...] = grad_t.T.astype(BF)


def middle(own, got, x, ws, wn, bias, cot):
    n = x.shape[0]
    shape = jax.ShapeDtypeStruct((n, n), BF)
    return pl.pallas_call(
        middle_kernel,
        out_shape=(shape, shape, shape, shape),
        compiler_params=params(16),
        cost_estimate=cost(6 * n * n * n, 2 << 20, n * n),
        name="middle",
    )(own, *got, x, ws, wn, bias, cot)


def weights_kernel(x_ref, pre_ref, mean_ref, ws_ref, part_ref, self_ref):
    n = x_ref.shape[0]
    pre_grad = pre_ref[...]
    part_ref[0:n, :] = dot_on(x_ref[...], pre_grad, 0, 0).astype(BF)
    neigh_grad = jnp.dot(mean_ref[...], pre_grad, preferred_element_type=F32)
    part_ref[n : 2 * n, :] = neigh_grad.astype(BF)
    bias_grad = jnp.sum(pre_grad.astype(F32), axis=0, keepdims=True)
    part_ref[2 * n :, :] = spaced(bias_grad, BF)
    self_ref[...] = dot_on(pre_grad, ws_ref[...], 1, 1)


def weights(x, pre_grad, mean_t, ws):
    n = x.shape[0]
    return pl.pallas_call(
        weights_kernel,
        out_shape=(
            jax.ShapeDtypeStruct((2 * n + EXTRA, n), BF),
            jax.ShapeDtypeStruct((n, n), F32),
        ),
        compiler_params=params(16),
        cost_estimate=cost(6 * n * n * n, 2 << 20),
        name="weights",
    )(x, pre_grad, mean_t, ws)


def finish_kernel(parts_ref, self_ref, out_ref):
    total = self_ref[...]
    for k in range(parts_ref.shape[0]):
        total += parts_ref[k].astype(F32)
    out_ref[...] = total.astype(BF)


def finish(parts, self_part):
    return pl.pallas_call(
        finish_kernel,
        out_shape=jax.ShapeDtypeStruct(self_part.shape, BF),
        compiler_params=params(16),
        cost_estimate=cost(1 << 20, 2 << 20),
        name="finish",
    )(parts, self_part)


def swap(x, axis):
    return lax.all_to_all(x, axis, 0, 0, tiled=True)


def along_y(step):
    return [(2 * y + c, 2 * ((y + step) % 4) + c) for y in range(4) for c in range(2)]


def send_node(x, dx, dz):
    moves = [
        (4 * i + j, 4 * ((i + dx) % 4) + (j + dz) % 4) for i in range(4) for j in range(4)
    ]
    return lax.ppermute(x, "nodes", moves)


def send_x_flip(x, bit):
    moves = [(4 * i + j, 4 * (i ^ bit) + j) for i in range(4) for j in range(4)]
    return lax.ppermute(x, "nodes", moves)


def pair_sum(one, other):
    return one.astype(F32) + other.astype(F32)


PARTNER = [(i, i ^ 1) for i in range(8)]


def send_y(x, step):
    return lax.ppermute(x, "cols", along_y(step))


def send_core(x):
    return lax.ppermute(x, "cols", PARTNER)


def add_terms(terms):
    own, one, two, three = (x.astype(F32) for x in terms)
    return (own + two) + (one + three)


def send_x(x, step):
    return send_node(x, step, 0)


def send_z(x, step):
    return send_node(x, 0, step)


def shards(node_feats, tile_row, tile_col, tile_bits, w_self, w_neigh, bias, cotangent):
    nodes = lax.axis_size("nodes")
    cols = lax.axis_size("cols")
    rows_dev, width = node_feats.shape
    me, node = lax.axis_index("cols"), lax.axis_index("nodes")
    y, core = me // 2, me % 2
    mine = jnp.stack([y, core, node // 4, node % 4]).astype(jnp.int32)
    theirs = jnp.stack([y, 1 - core, node // 4, node % 4]).astype(jnp.int32)

    top, low = prepare(node_feats)
    top = jnp.stack([top] + [send_x(top, k) for k in (1, 2, 3)])
    low = jnp.stack([low] + [send_z(low, k) for k in (1, 2, 3)])
    top, low, mine, theirs, zero = lax.optimization_barrier((top, low, mine, theirs, core == 0))
    planes = [top] + [send_z(top, k) for k in (1, 2, 3)]
    planes += [low] + [send_x(low, k) for k in (1, 2, 3)]
    at, degree = build(
        *(pltpu.with_memory_space_constraint(t, pltpu.HBM) for t in (tile_row, tile_col, tile_bits)),
        top,
        nodes * rows_dev // 128, cols * rows_dev // 128
    )

    give = forward(theirs, planes, at, degree, BF)
    taken = send_core(give)
    keep = forward(mine, planes, at, degree, F32)
    own, *sent = mix(keep, taken)
    far = send_y(sent[1], 2)
    got = [send_y(sent[0], 1), far, send_y(sent[2], 3)]
    layer_out, pre_grad, mean_t, mean_grad = middle(
        own, got, node_feats, w_self, w_neigh, bias.reshape(1, -1), cotangent
    )
    next_y, last_y = send_y(mean_grad, 1), send_y(mean_grad, 3)
    same_core = [mean_grad, next_y, send_y(mean_grad, 2), last_y]

    part, self_part = weights(node_feats, pre_grad, mean_t, w_self)
    part = pair_sum(part, send_x_flip(part, 1)).astype(BF)
    other_core = [send_core(g) for g in same_core]
    flipped = send_x_flip(part, 2)

    src = backward(mine, same_core + other_core, at)
    src, part, flipped = lax.optimization_barrier((src, part, flipped))
    parts = swap(src.reshape(nodes, rows_dev, width), "nodes")

    part = pair_sum(part, flipped)
    halves = (part[:width], part[width : 2 * width])
    kept = jnp.concatenate([jnp.where(zero, *halves), part[2 * width :]])
    given = jnp.concatenate([jnp.where(zero, *halves[::-1]), part[2 * width :]])
    part = (kept + send_core(given)).astype(BF)
    part = add_terms([part] + [send_y(part, k) for k in (1, 2, 3)]).astype(BF)
    terms = [part] + [send_z(part, k) for k in (1, 2, 3)]

    feat_grad = finish(parts, self_part)
    feat_grad, terms = lax.optimization_barrier((feat_grad, terms))
    part = add_terms(terms)
    other = send_core(part)
    bias_grad = part[width]
    self_grad = jnp.where(zero, part[:width], other[:width])
    neigh_grad = jnp.where(zero, other[:width], part[:width])
    return (layer_out, feat_grad, self_grad, neigh_grad, bias_grad)


def solution(mesh):
    return jax.shard_map(
        shards,
        mesh=mesh,
        in_specs=(
            P(("nodes", "cols"), None),
            P("nodes", "cols"),
            P("nodes", "cols"),
            P("nodes", "cols", None, None),
            P(),
            P(),
            P(),
            P(("nodes", "cols"), None),
        ),
        out_specs=(P(("nodes", "cols"), None), P(("nodes", "cols"), None), P(), P(), P()),
        check_vma=False,
    )
```

```python
import jax
import jax.numpy as jnp
from jax import lax
from jax.experimental import pallas as pl
from jax.experimental.pallas import tpu as pltpu
from jax.sharding import PartitionSpec as P

BF = jnp.bfloat16
F32 = jnp.float32
EXACT = 256
EXTRA = 16


def params(mib):
    return pltpu.CompilerParams(vmem_limit_bytes=mib << 20)


def in_hbm(shape, kind):
    return pltpu.HBM(shape, kind)


def cost(flops, moved, transcendentals=0):
    return pl.CostEstimate(flops=flops, bytes_accessed=moved, transcendentals=transcendentals)


def prepare_kernel(x_ref, top_ref, low_ref):
    half = top_ref.shape[0]
    flipped = x_ref[...].T
    top_ref[...] = flipped[:half]
    low_ref[...] = flipped[half:]


def prepare(x):
    rows, width = x.shape
    shape = jax.ShapeDtypeStruct((width // 2, rows), BF)
    return pl.pallas_call(
        prepare_kernel,
        out_shape=(shape, shape),
        compiler_params=params(8),
        cost_estimate=cost(0, 1 << 18),
        name="prepare",
    )(x)


def build_kernel(
    rows_ref, cols_ref, bits_all, gate_ref, clear_ref, at_ref, deg_ref,
    deg8, count, spill, row_ref, col_ref, bits_ref, sems,
):
    sources = at_ref.shape[0] - 1
    dests = at_ref.shape[1]
    tiles = bits_ref.shape[0]
    pieces = 4
    each = tiles // pieces

    def fetch(k):
        part = pl.ds(k * each, each)
        return pltpu.make_async_copy(bits_all.at[0, part], bits_ref.at[part], sems.at[2 + k])

    copies = [
        pltpu.make_async_copy(rows_ref, row_ref, sems.at[0]),
        pltpu.make_async_copy(cols_ref, col_ref, sems.at[1]),
    ] + [fetch(k) for k in range(pieces)]
    for copy in copies:
        copy.start()
    for r in range(dests):
        deg8[r] = jnp.zeros((8, 128), F32)

    def clear(k, carry):
        for r in range(dests):
            count[k * dests + r] = 0
        return carry

    lax.fori_loop(0, sources, clear, 0)
    spill[0] = -1
    shifts = lax.broadcasted_iota(jnp.int32, (8, 128), 0)

    def add_tile(t, carry):
        row = row_ref[0, t]
        col = col_ref[0, t]
        slot = col * dests + row
        seen = count[slot]
        count[slot] = seen + 1
        full = seen >= EXACT
        spill[0] = jnp.where(full, slot, spill[0])
        to_col = jnp.where(full, sources, col)
        to_row = jnp.where(full, 0, row)
        total = None
        for i in range(8):
            flags = []
            for w in (2 * i, 2 * i + 1):
                word = jnp.broadcast_to(bits_ref[t, w : w + 1, :], (8, 128))
                flags.append((jnp.right_shift(word, shifts) & 1).astype(F32))
            pair = flags[0] + flags[1]
            total = pair if total is None else total + pair
            at_ref[to_col, to_row, 16 * i : 16 * i + 16, :] += jnp.concatenate(flags, 0).astype(BF)
        deg8[row] += total
        return carry

    copies[0].wait()
    copies[1].wait()
    for k in range(pieces):
        copies[2 + k].wait()
        lax.fori_loop(k * each, (k + 1) * each, add_tile, 0, unroll=4)

    @pl.when(spill[0] >= 0)
    def _():
        slot = spill[0]
        col = lax.div(slot, dests)
        row = lax.rem(slot, dests)
        whole = at_ref[col, row].astype(F32) + at_ref[sources, 0].astype(F32)
        at_ref[col, row] = whole.astype(BF)

    for r in range(dests):
        deg_ref[:, r * 128 : (r + 1) * 128] = jnp.sum(deg8[r], axis=0, keepdims=True)


def clear_kernel(gate_ref, at_ref):
    def clear(k, carry):
        for r in range(at_ref.shape[1]):
            at_ref[k, r] = jnp.zeros((128, 128), BF)
        return carry

    lax.fori_loop(0, at_ref.shape[0], clear, 0)


def cleared(gate, sources, dests):
    return pl.pallas_call(
        clear_kernel,
        out_shape=jax.ShapeDtypeStruct((sources + 1, dests, 128, 128), BF),
        in_specs=[pl.BlockSpec(memory_space=pl.ANY)],
        out_specs=pl.BlockSpec(memory_space=pltpu.VMEM),
        compiler_params=params(24),
        cost_estimate=cost(0, 8 << 20),
        name="clear",
    )(gate)


def build(rows, cols, bits, gate, at):
    sources, dests = at.shape[0] - 1, at.shape[1]
    tiles = bits.shape[1]
    assert tiles <= 2 * EXACT and tiles % 8 == 0
    hbm = pl.BlockSpec(memory_space=pltpu.HBM)
    vmem = pl.BlockSpec(memory_space=pltpu.VMEM)
    return pl.pallas_call(
        build_kernel,
        out_shape=(
            jax.ShapeDtypeStruct((sources + 1, dests, 128, 128), BF),
            jax.ShapeDtypeStruct((1, dests * 128), F32),
        ),
        in_specs=[hbm, hbm, hbm, pl.BlockSpec(memory_space=pl.ANY), vmem],
        out_specs=(vmem, vmem),
        scratch_shapes=[
            pltpu.VMEM((dests, 8, 128), F32),
            pltpu.SMEM((sources * dests,), jnp.int32),
            pltpu.SMEM((1,), jnp.int32),
            pltpu.SMEM((1, tiles), jnp.int32),
            pltpu.SMEM((1, tiles), jnp.int32),
            pltpu.VMEM((tiles, 16, 128), jnp.int32),
            pltpu.SemaphoreType.DMA((6,)),
        ],
        compiler_params=params(24),
        input_output_aliases={4: 0},
        cost_estimate=cost(0, 30 << 20),
        name="build",
    )(rows, cols, bits, gate, at)


def forward_kernel(place_ref, *refs):
    tops, lows = refs[:4], refs[4:8]
    at_ref, deg_ref, out_ref, joined = refs[8:]
    half, rows = tops[0].shape[1:]
    width = 2 * half
    per = rows // 128
    for kx in range(4):
        x = lax.rem(place_ref[2] + 4 - kx, 4)
        for kz in range(4):
            n = 4 * x + lax.rem(place_ref[3] + 4 - kz, 4)
            lanes = pl.ds(pl.multiple_of(n * rows, rows), rows)
            joined[0:half, lanes] = tops[kz][kx]
            joined[half:width, lanes] = lows[kx][kz]

    for j in range(4):
        chunk = 2 * lax.rem(place_ref[0] + j, 4) + place_ref[1]
        blocks = [
            jnp.concatenate([at_ref[k, per * chunk + r] for r in range(per)], axis=1)
            for k in range(at_ref.shape[0] - 1)
        ]
        part = jnp.dot(joined[...], jnp.concatenate(blocks, axis=0), preferred_element_type=F32)
        out_ref[j, 0:width, :] = part.astype(out_ref.dtype)
        whole = deg_ref[:, pl.ds(pl.multiple_of(chunk * rows, rows), rows)]
        degree = whole if out_ref.dtype == F32 else two_rows(whole)
        out_ref[j, width:, :] = spaced(degree, out_ref.dtype)


def two_rows(whole):
    high = whole.astype(BF).astype(F32)
    first = lax.broadcasted_iota(jnp.int32, (2, 1), 0) == 0
    return jnp.where(first, high, whole - high)


def spaced(rows, kind):
    count, width = rows.shape
    place = lax.broadcasted_iota(jnp.int32, (EXTRA, 1), 0)
    out = jnp.zeros((EXTRA, width), F32)
    for k in range(count):
        out = jnp.where(place == k, rows[k : k + 1, :], out)
    return out.astype(kind)


def forward(place, planes, at, degree, kind):
    _, half, rows = planes[0].shape
    width = 2 * half
    sources = at.shape[0] - 1
    vmem = pl.BlockSpec(memory_space=pltpu.VMEM)
    return pl.pallas_call(
        forward_kernel,
        out_shape=jax.ShapeDtypeStruct((4, width + EXTRA, rows), kind),
        in_specs=[pl.BlockSpec(memory_space=pltpu.SMEM)] + [vmem] * 10,
        out_specs=vmem,
        scratch_shapes=[pltpu.VMEM((width, sources * 128), BF)],
        compiler_params=params(20),
        cost_estimate=cost(8 * sources * 128 * rows * width, 10 << 20),
        name="forward",
    )(place, *planes, at, degree)


def backward_kernel(place_ref, *refs):
    parts, at_ref, out_ref, grads, held, sems = refs[:8], *refs[8:]
    rows = parts[0].shape[0]
    for k in range(4):
        chunk = 2 * lax.rem(place_ref[0] + 4 - k, 4)
        own = pl.multiple_of((chunk + place_ref[1]) * rows, rows)
        other = pl.multiple_of((chunk + 1 - place_ref[1]) * rows, rows)
        grads[pl.ds(own, rows), :] = parts[k][...]
        grads[pl.ds(other, rows), :] = parts[4 + k][...]
    pieces, each, _ = held.shape

    def copy(i):
        into = out_ref.at[pl.ds(pl.multiple_of(i * each, each), each)]
        return pltpu.make_async_copy(held.at[i], into, sems.at[i])

    def piece(i, carry):
        for k in range(each // 128):
            at = i * (each // 128) + k
            block = jnp.concatenate([at_ref[at, r] for r in range(at_ref.shape[1])], axis=1)
            got = jnp.dot(block, grads[...], preferred_element_type=F32)
            held[i, k * 128 : (k + 1) * 128, :] = got.astype(BF)
        copy(i).start()
        return carry

    lax.fori_loop(0, pieces, piece, 0)
    for i in range(pieces):
        copy(i).wait()


def backward(place, parts, at):
    sources, dests = at.shape[0] - 1, at.shape[1]
    _, width = parts[0].shape
    pieces = 4
    vmem = pl.BlockSpec(memory_space=pltpu.VMEM)
    return pl.pallas_call(
        backward_kernel,
        out_shape=in_hbm((sources * 128, width), BF),
        in_specs=[pl.BlockSpec(memory_space=pltpu.SMEM)] + [vmem] * 9,
        out_specs=pl.BlockSpec(memory_space=pltpu.HBM),
        scratch_shapes=[
            pltpu.VMEM((dests * 128, width), BF),
            pltpu.VMEM((pieces, sources * 128 // pieces, width), BF),
            pltpu.SemaphoreType.DMA((pieces,)),
        ],
        compiler_params=params(20),
        cost_estimate=cost(2 * sources * 128 * dests * 128 * width, 20 << 20),
        name="backward",
    )(place, *parts, at)


def dot_on(a, b, da, db):
    return lax.dot_general(a, b, (((da,), (db,)), ((), ())), preferred_element_type=F32)


def mix_kernel(keep_ref, taken_ref, own_ref, *outs):
    width = own_ref.shape[0] - EXTRA
    own_ref[...] = keep_ref[0] + taken_ref[0].astype(F32)
    for k, out_ref in enumerate(outs):
        both = keep_ref[k + 1] + taken_ref[k + 1].astype(F32)
        out_ref[0:width, :] = both[0:width].astype(BF)
        degree = both[width : width + 1] + both[width + 1 : width + 2]
        out_ref[width:, :] = spaced(two_rows(degree), BF)


def mix(keep, taken):
    shape = keep.shape[1:]
    return pl.pallas_call(
        mix_kernel,
        out_shape=(jax.ShapeDtypeStruct(shape, F32),) + (jax.ShapeDtypeStruct(shape, BF),) * 3,
        compiler_params=params(16),
        cost_estimate=cost(1 << 18, 2 << 20),
        name="mix",
    )(keep, taken)


def middle_kernel(
    own_ref, r1_ref, r2_ref, r3_ref, x_ref, ws_ref, wn_ref, bias_ref, cot_ref,
    out_ref, pre_ref, mean_ref, grad_ref,
):
    width = x_ref.shape[1]
    summed = (own_ref[...] + r2_ref[...].astype(F32)) + (
        r1_ref[...].astype(F32) + r3_ref[...].astype(F32)
    )
    degree = jnp.maximum(summed[width : width + 1] + summed[width + 1 : width + 2], 1.0)
    summed = summed[0:width]
    mean_t = (summed / degree).astype(BF)
    mean_ref[...] = mean_t
    preact = (
        jnp.dot(x_ref[...], ws_ref[...], preferred_element_type=F32)
        + dot_on(mean_t, wn_ref[...], 0, 0)
        + bias_ref[...]
    )
    sig = 1.0 / (1.0 + jnp.exp(-preact))
    out_ref[...] = (preact * sig).astype(BF)
    pre_grad = (cot_ref[...].astype(F32) * sig * (1.0 + preact * (1.0 - sig))).astype(BF)
    pre_ref[...] = pre_grad
    grad_t = dot_on(wn_ref[...], pre_grad, 1, 1) / degree
    grad_ref[...] = grad_t.T.astype(BF)


def middle(own, got, x, ws, wn, bias, cot):
    n = x.shape[0]
    shape = jax.ShapeDtypeStruct((n, n), BF)
    return pl.pallas_call(
        middle_kernel,
        out_shape=(shape, shape, shape, shape),
        compiler_params=params(16),
        cost_estimate=cost(6 * n * n * n, 2 << 20, n * n),
        name="middle",
    )(own, *got, x, ws, wn, bias, cot)


def weights_kernel(x_ref, pre_ref, mean_ref, ws_ref, part_ref, self_ref):
    n = x_ref.shape[0]
    pre_grad = pre_ref[...]
    part_ref[0:n, :] = dot_on(x_ref[...], pre_grad, 0, 0).astype(BF)
    neigh_grad = jnp.dot(mean_ref[...], pre_grad, preferred_element_type=F32)
    part_ref[n : 2 * n, :] = neigh_grad.astype(BF)
    bias_grad = jnp.sum(pre_grad.astype(F32), axis=0, keepdims=True)
    part_ref[2 * n :, :] = spaced(bias_grad, BF)
    self_ref[...] = dot_on(pre_grad, ws_ref[...], 1, 1)


def weights(x, pre_grad, mean_t, ws):
    n = x.shape[0]
    return pl.pallas_call(
        weights_kernel,
        out_shape=(
            jax.ShapeDtypeStruct((2 * n + EXTRA, n), BF),
            jax.ShapeDtypeStruct((n, n), F32),
        ),
        compiler_params=params(16),
        cost_estimate=cost(6 * n * n * n, 2 << 20),
        name="weights",
    )(x, pre_grad, mean_t, ws)


def finish_kernel(parts_ref, self_ref, out_ref):
    total = self_ref[...]
    for k in range(parts_ref.shape[0]):
        total += parts_ref[k].astype(F32)
    out_ref[...] = total.astype(BF)


def finish(parts, self_part):
    return pl.pallas_call(
        finish_kernel,
        out_shape=jax.ShapeDtypeStruct(self_part.shape, BF),
        compiler_params=params(16),
        cost_estimate=cost(1 << 20, 2 << 20),
        name="finish",
    )(parts, self_part)


def swap(x, axis):
    return lax.all_to_all(x, axis, 0, 0, tiled=True)


def along_y(step):
    return [(2 * y + c, 2 * ((y + step) % 4) + c) for y in range(4) for c in range(2)]


def send_node(x, dx, dz):
    moves = [
        (4 * i + j, 4 * ((i + dx) % 4) + (j + dz) % 4) for i in range(4) for j in range(4)
    ]
    return lax.ppermute(x, "nodes", moves)


def send_x_flip(x, bit):
    moves = [(4 * i + j, 4 * (i ^ bit) + j) for i in range(4) for j in range(4)]
    return lax.ppermute(x, "nodes", moves)


def pair_sum(one, other):
    return one.astype(F32) + other.astype(F32)


PARTNER = [(i, i ^ 1) for i in range(8)]


def send_y(x, step):
    return lax.ppermute(x, "cols", along_y(step))


def send_core(x):
    return lax.ppermute(x, "cols", PARTNER)


def add_terms(terms):
    own, one, two, three = (x.astype(F32) for x in terms)
    return (own + two) + (one + three)


def send_x(x, step):
    return send_node(x, step, 0)


def send_z(x, step):
    return send_node(x, 0, step)


def shards(node_feats, tile_row, tile_col, tile_bits, w_self, w_neigh, bias, cotangent):
    nodes = lax.axis_size("nodes")
    cols = lax.axis_size("cols")
    rows_dev, width = node_feats.shape
    me, node = lax.axis_index("cols"), lax.axis_index("nodes")
    y, core = me // 2, me % 2
    mine = jnp.stack([y, core, node // 4, node % 4]).astype(jnp.int32)
    theirs = jnp.stack([y, 1 - core, node // 4, node % 4]).astype(jnp.int32)

    top, low = prepare(node_feats)
    top = jnp.stack([top] + [send_x(top, k) for k in (1, 2, 3)])
    low = jnp.stack([low] + [send_z(low, k) for k in (1, 2, 3)])
    top, low, mine, theirs, zero = lax.optimization_barrier((top, low, mine, theirs, core == 0))
    planes = [top] + [send_z(top, k) for k in (1, 2, 3)]
    empty = cleared(low, nodes * rows_dev // 128, cols * rows_dev // 128)
    late, empty, third = lax.optimization_barrier((low, empty, send_x(low, 3)))
    planes += [low, send_x(late, 1), send_x(low, 2), third]
    fixed = [pltpu.with_memory_space_constraint(t, pltpu.HBM) for t in (tile_row, tile_col, tile_bits)]
    at, degree = build(*fixed, top, empty)

    give = forward(theirs, planes, at, degree, BF)
    taken = send_core(give)
    keep = forward(mine, planes, at, degree, F32)
    own, *sent = mix(keep, taken)
    far = send_y(sent[1], 2)
    got = [send_y(sent[0], 1), far, send_y(sent[2], 3)]
    layer_out, pre_grad, mean_t, mean_grad = middle(
        own, got, node_feats, w_self, w_neigh, bias.reshape(1, -1), cotangent
    )
    next_y, last_y = send_y(mean_grad, 1), send_y(mean_grad, 3)
    same_core = [mean_grad, next_y, send_y(mean_grad, 2), last_y]

    part, self_part = weights(node_feats, pre_grad, mean_t, w_self)
    part = pair_sum(part, send_x_flip(part, 1)).astype(BF)
    other_core = [send_core(g) for g in same_core]
    flipped = send_x_flip(part, 2)

    src = backward(mine, same_core + other_core, at)
    src, part, flipped = lax.optimization_barrier((src, part, flipped))
    parts = swap(src.reshape(nodes, rows_dev, width), "nodes")

    part = pair_sum(part, flipped)
    halves = (part[:width], part[width : 2 * width])
    kept = jnp.concatenate([jnp.where(zero, *halves), part[2 * width :]])
    given = jnp.concatenate([jnp.where(zero, *halves[::-1]), part[2 * width :]])
    part = (kept + send_core(given)).astype(BF)
    part = add_terms([part] + [send_y(part, k) for k in (1, 2, 3)]).astype(BF)
    terms = [part] + [send_z(part, k) for k in (1, 2, 3)]

    feat_grad = finish(parts, self_part)
    feat_grad, terms = lax.optimization_barrier((feat_grad, terms))
    part = add_terms(terms)
    other = send_core(part)
    bias_grad = part[width]
    self_grad = jnp.where(zero, part[:width], other[:width])
    neigh_grad = jnp.where(zero, other[:width], part[:width])
    return (layer_out, feat_grad, self_grad, neigh_grad, bias_grad)


def solution(mesh):
    return jax.shard_map(
        shards,
        mesh=mesh,
        in_specs=(
            P(("nodes", "cols"), None),
            P("nodes", "cols"),
            P("nodes", "cols"),
            P("nodes", "cols", None, None),
            P(),
            P(),
            P(),
            P(("nodes", "cols"), None),
        ),
        out_specs=(P(("nodes", "cols"), None), P(("nodes", "cols"), None), P(), P(), P()),
        check_vma=False,
    )
```

```python
import jax
import jax.numpy as jnp
from jax import lax
from jax.experimental import pallas as pl
from jax.experimental.pallas import tpu as pltpu
from jax.sharding import PartitionSpec as P

BF = jnp.bfloat16
F32 = jnp.float32
EXACT = 256
EXTRA = 16
FAR_FIRST = (0, 2, 1, 3)


def params(mib):
    return pltpu.CompilerParams(vmem_limit_bytes=mib << 20)


def in_hbm(shape, kind):
    return pltpu.HBM(shape, kind)


def cost(flops, moved, transcendentals=0):
    return pl.CostEstimate(flops=flops, bytes_accessed=moved, transcendentals=transcendentals)


def prepare_kernel(x_ref, top_ref, low_ref):
    half = top_ref.shape[0]
    flipped = x_ref[...].T
    top_ref[...] = flipped[:half]
    low_ref[...] = flipped[half:]


def prepare(x):
    rows, width = x.shape
    shape = jax.ShapeDtypeStruct((width // 2, rows), BF)
    return pl.pallas_call(
        prepare_kernel,
        out_shape=(shape, shape),
        compiler_params=params(8),
        cost_estimate=cost(0, 1 << 18),
        name="prepare",
    )(x)


def build_kernel(
    rows_ref, cols_ref, bits_all, gate_ref, clear_ref, at_ref, deg_ref,
    deg8, count, spill, row_ref, col_ref, bits_ref, sems,
):
    sources = at_ref.shape[0] - 1
    dests = at_ref.shape[1]
    tiles = bits_ref.shape[0]
    pieces = 4
    each = tiles // pieces

    def fetch(k):
        part = pl.ds(k * each, each)
        return pltpu.make_async_copy(bits_all.at[0, part], bits_ref.at[part], sems.at[2 + k])

    copies = [
        pltpu.make_async_copy(rows_ref, row_ref, sems.at[0]),
        pltpu.make_async_copy(cols_ref, col_ref, sems.at[1]),
    ] + [fetch(k) for k in range(pieces)]
    for copy in copies:
        copy.start()
    for r in range(dests):
        deg8[r] = jnp.zeros((8, 128), F32)

    def clear(k, carry):
        for r in range(dests):
            count[k * dests + r] = 0
        return carry

    lax.fori_loop(0, sources, clear, 0)
    spill[0] = -1
    shifts = lax.broadcasted_iota(jnp.int32, (8, 128), 0)

    def add_tile(t, carry):
        row = row_ref[0, t]
        col = col_ref[0, t]
        slot = col * dests + row
        seen = count[slot]
        count[slot] = seen + 1
        full = seen >= EXACT
        spill[0] = jnp.where(full, slot, spill[0])
        to_col = jnp.where(full, sources, col)
        to_row = jnp.where(full, 0, row)
        total = None
        for i in range(8):
            flags = []
            for w in (2 * i, 2 * i + 1):
                word = jnp.broadcast_to(bits_ref[t, w : w + 1, :], (8, 128))
                flags.append((jnp.right_shift(word, shifts) & 1).astype(F32))
            pair = flags[0] + flags[1]
            total = pair if total is None else total + pair
            at_ref[to_col, to_row, 16 * i : 16 * i + 16, :] += jnp.concatenate(flags, 0).astype(BF)
        deg8[row] += total
        return carry

    copies[0].wait()
    copies[1].wait()
    for k in range(pieces):
        copies[2 + k].wait()
        lax.fori_loop(k * each, (k + 1) * each, add_tile, 0, unroll=4)

    @pl.when(spill[0] >= 0)
    def _():
        slot = spill[0]
        col = lax.div(slot, dests)
        row = lax.rem(slot, dests)
        whole = at_ref[col, row].astype(F32) + at_ref[sources, 0].astype(F32)
        at_ref[col, row] = whole.astype(BF)

    for r in range(dests):
        deg_ref[:, r * 128 : (r + 1) * 128] = jnp.sum(deg8[r], axis=0, keepdims=True)


def clear_kernel(gate_ref, at_ref):
    def clear(k, carry):
        for r in range(at_ref.shape[1]):
            at_ref[k, r] = jnp.zeros((128, 128), BF)
        return carry

    lax.fori_loop(0, at_ref.shape[0], clear, 0)


def cleared(gate, sources, dests):
    return pl.pallas_call(
        clear_kernel,
        out_shape=jax.ShapeDtypeStruct((sources + 1, dests, 128, 128), BF),
        in_specs=[pl.BlockSpec(memory_space=pl.ANY)],
        out_specs=pl.BlockSpec(memory_space=pltpu.VMEM),
        compiler_params=params(24),
        cost_estimate=cost(0, 8 << 20),
        name="clear",
    )(gate)


def build(rows, cols, bits, gate, at):
    sources, dests = at.shape[0] - 1, at.shape[1]
    tiles = bits.shape[1]
    assert tiles <= 2 * EXACT and tiles % 8 == 0
    hbm = pl.BlockSpec(memory_space=pltpu.HBM)
    vmem = pl.BlockSpec(memory_space=pltpu.VMEM)
    return pl.pallas_call(
        build_kernel,
        out_shape=(
            jax.ShapeDtypeStruct((sources + 1, dests, 128, 128), BF),
            jax.ShapeDtypeStruct((1, dests * 128), F32),
        ),
        in_specs=[hbm, hbm, hbm, pl.BlockSpec(memory_space=pl.ANY), vmem],
        out_specs=(vmem, vmem),
        scratch_shapes=[
            pltpu.VMEM((dests, 8, 128), F32),
            pltpu.SMEM((sources * dests,), jnp.int32),
            pltpu.SMEM((1,), jnp.int32),
            pltpu.SMEM((1, tiles), jnp.int32),
            pltpu.SMEM((1, tiles), jnp.int32),
            pltpu.VMEM((tiles, 16, 128), jnp.int32),
            pltpu.SemaphoreType.DMA((6,)),
        ],
        compiler_params=params(24),
        input_output_aliases={4: 0},
        cost_estimate=cost(0, 30 << 20),
        name="build",
    )(rows, cols, bits, gate, at)


def forward_kernel(place_ref, *refs):
    tops, lows = refs[:4], refs[4:8]
    at_ref, deg_ref, out_ref, joined = refs[8:]
    half, rows = tops[0].shape[1:]
    width = 2 * half
    per = rows // 128
    for kx in range(4):
        x = lax.rem(place_ref[2] + 4 - kx, 4)
        for kz in range(4):
            n = 4 * x + lax.rem(place_ref[3] + 4 - kz, 4)
            lanes = pl.ds(pl.multiple_of(n * rows, rows), rows)
            joined[0:half, lanes] = tops[kz][kx]
            joined[half:width, lanes] = lows[kx][kz]

    for j in range(4):
        chunk = 2 * lax.rem(place_ref[0] + j, 4) + place_ref[1]
        blocks = [
            jnp.concatenate([at_ref[k, per * chunk + r] for r in range(per)], axis=1)
            for k in range(at_ref.shape[0] - 1)
        ]
        part = jnp.dot(joined[...], jnp.concatenate(blocks, axis=0), preferred_element_type=F32)
        out_ref[j, 0:width, :] = part.astype(out_ref.dtype)
        whole = deg_ref[:, pl.ds(pl.multiple_of(chunk * rows, rows), rows)]
        degree = whole if out_ref.dtype == F32 else two_rows(whole)
        out_ref[j, width:, :] = spaced(degree, out_ref.dtype)


def two_rows(whole):
    high = whole.astype(BF).astype(F32)
    first = lax.broadcasted_iota(jnp.int32, (2, 1), 0) == 0
    return jnp.where(first, high, whole - high)


def spaced(rows, kind):
    count, width = rows.shape
    place = lax.broadcasted_iota(jnp.int32, (EXTRA, 1), 0)
    out = jnp.zeros((EXTRA, width), F32)
    for k in range(count):
        out = jnp.where(place == k, rows[k : k + 1, :], out)
    return out.astype(kind)


def forward(place, planes, at, degree, kind):
    _, half, rows = planes[0].shape
    width = 2 * half
    sources = at.shape[0] - 1
    vmem = pl.BlockSpec(memory_space=pltpu.VMEM)
    return pl.pallas_call(
        forward_kernel,
        out_shape=jax.ShapeDtypeStruct((4, width + EXTRA, rows), kind),
        in_specs=[pl.BlockSpec(memory_space=pltpu.SMEM)] + [vmem] * 10,
        out_specs=vmem,
        scratch_shapes=[pltpu.VMEM((width, sources * 128), BF)],
        compiler_params=params(20),
        cost_estimate=cost(8 * sources * 128 * rows * width, 10 << 20),
        name="forward",
    )(place, *planes, at, degree)


def backward_kernel(place_ref, *refs):
    parts, at_ref, out_ref, grads, held, sems = refs[:8], *refs[8:]
    rows = parts[0].shape[0]
    for spot, k in enumerate(FAR_FIRST):
        chunk = 2 * lax.rem(place_ref[0] + 4 - k, 4)
        own = pl.multiple_of((chunk + place_ref[1]) * rows, rows)
        other = pl.multiple_of((chunk + 1 - place_ref[1]) * rows, rows)
        grads[pl.ds(own, rows), :] = parts[spot][...]
        grads[pl.ds(other, rows), :] = parts[4 + spot][...]
    pieces, each, _ = held.shape

    def copy(i):
        into = out_ref.at[pl.ds(pl.multiple_of(i * each, each), each)]
        return pltpu.make_async_copy(held.at[i], into, sems.at[i])

    def piece(i, carry):
        for k in range(each // 128):
            at = i * (each // 128) + k
            block = jnp.concatenate([at_ref[at, r] for r in range(at_ref.shape[1])], axis=1)
            got = jnp.dot(block, grads[...], preferred_element_type=F32)
            held[i, k * 128 : (k + 1) * 128, :] = got.astype(BF)
        copy(i).start()
        return carry

    lax.fori_loop(0, pieces, piece, 0)
    for i in range(pieces):
        copy(i).wait()


def backward(place, parts, at):
    sources, dests = at.shape[0] - 1, at.shape[1]
    _, width = parts[0].shape
    pieces = 4
    vmem = pl.BlockSpec(memory_space=pltpu.VMEM)
    return pl.pallas_call(
        backward_kernel,
        out_shape=in_hbm((sources * 128, width), BF),
        in_specs=[pl.BlockSpec(memory_space=pltpu.SMEM)] + [vmem] * 9,
        out_specs=pl.BlockSpec(memory_space=pltpu.HBM),
        scratch_shapes=[
            pltpu.VMEM((dests * 128, width), BF),
            pltpu.VMEM((pieces, sources * 128 // pieces, width), BF),
            pltpu.SemaphoreType.DMA((pieces,)),
        ],
        compiler_params=params(20),
        cost_estimate=cost(2 * sources * 128 * dests * 128 * width, 20 << 20),
        name="backward",
    )(place, *parts, at)


def dot_on(a, b, da, db):
    return lax.dot_general(a, b, (((da,), (db,)), ((), ())), preferred_element_type=F32)


def mix_kernel(keep_ref, taken_ref, own_ref, *outs):
    width = own_ref.shape[0] - EXTRA
    own_ref[...] = keep_ref[0] + taken_ref[0].astype(F32)
    for k, out_ref in enumerate(outs):
        both = keep_ref[k + 1] + taken_ref[k + 1].astype(F32)
        out_ref[0:width, :] = both[0:width].astype(BF)
        degree = both[width : width + 1] + both[width + 1 : width + 2]
        out_ref[width:, :] = spaced(two_rows(degree), BF)


def mix(keep, taken):
    shape = keep.shape[1:]
    return pl.pallas_call(
        mix_kernel,
        out_shape=(jax.ShapeDtypeStruct(shape, F32),) + (jax.ShapeDtypeStruct(shape, BF),) * 3,
        compiler_params=params(16),
        cost_estimate=cost(1 << 18, 2 << 20),
        name="mix",
    )(keep, taken)


def middle_kernel(
    own_ref, r2_ref, r1_ref, r3_ref, x_ref, ws_ref, wn_ref, bias_ref, cot_ref,
    out_ref, pre_ref, mean_ref, grad_ref,
):
    width = x_ref.shape[1]
    summed = (own_ref[...] + r2_ref[...].astype(F32)) + (
        r1_ref[...].astype(F32) + r3_ref[...].astype(F32)
    )
    degree = jnp.maximum(summed[width : width + 1] + summed[width + 1 : width + 2], 1.0)
    summed = summed[0:width]
    mean_t = (summed / degree).astype(BF)
    mean_ref[...] = mean_t
    preact = (
        jnp.dot(x_ref[...], ws_ref[...], preferred_element_type=F32)
        + dot_on(mean_t, wn_ref[...], 0, 0)
        + bias_ref[...]
    )
    sig = 1.0 / (1.0 + jnp.exp(-preact))
    out_ref[...] = (preact * sig).astype(BF)
    pre_grad = (cot_ref[...].astype(F32) * sig * (1.0 + preact * (1.0 - sig))).astype(BF)
    pre_ref[...] = pre_grad
    grad_t = dot_on(wn_ref[...], pre_grad, 1, 1) / degree
    grad_ref[...] = grad_t.T.astype(BF)


def middle(own, got, x, ws, wn, bias, cot):
    n = x.shape[0]
    shape = jax.ShapeDtypeStruct((n, n), BF)
    return pl.pallas_call(
        middle_kernel,
        out_shape=(shape, shape, shape, shape),
        compiler_params=params(16),
        cost_estimate=cost(6 * n * n * n, 2 << 20, n * n),
        name="middle",
    )(own, *got, x, ws, wn, bias, cot)


def weights_kernel(x_ref, pre_ref, mean_ref, ws_ref, part_ref, self_ref):
    n = x_ref.shape[0]
    pre_grad = pre_ref[...]
    part_ref[0:n, :] = dot_on(x_ref[...], pre_grad, 0, 0).astype(BF)
    neigh_grad = jnp.dot(mean_ref[...], pre_grad, preferred_element_type=F32)
    part_ref[n : 2 * n, :] = neigh_grad.astype(BF)
    bias_grad = jnp.sum(pre_grad.astype(F32), axis=0, keepdims=True)
    part_ref[2 * n :, :] = spaced(bias_grad, BF)
    self_ref[...] = dot_on(pre_grad, ws_ref[...], 1, 1)


def weights(x, pre_grad, mean_t, ws):
    n = x.shape[0]
    return pl.pallas_call(
        weights_kernel,
        out_shape=(
            jax.ShapeDtypeStruct((2 * n + EXTRA, n), BF),
            jax.ShapeDtypeStruct((n, n), F32),
        ),
        compiler_params=params(16),
        cost_estimate=cost(6 * n * n * n, 2 << 20),
        name="weights",
    )(x, pre_grad, mean_t, ws)


def finish_kernel(parts_ref, self_ref, out_ref):
    total = self_ref[...]
    for k in range(parts_ref.shape[0]):
        total += parts_ref[k].astype(F32)
    out_ref[...] = total.astype(BF)


def finish(parts, self_part):
    return pl.pallas_call(
        finish_kernel,
        out_shape=jax.ShapeDtypeStruct(self_part.shape, BF),
        compiler_params=params(16),
        cost_estimate=cost(1 << 20, 2 << 20),
        name="finish",
    )(parts, self_part)


def swap(x, axis):
    return lax.all_to_all(x, axis, 0, 0, tiled=True)


def along_y(step):
    return [(2 * y + c, 2 * ((y + step) % 4) + c) for y in range(4) for c in range(2)]


def send_node(x, dx, dz):
    moves = [
        (4 * i + j, 4 * ((i + dx) % 4) + (j + dz) % 4) for i in range(4) for j in range(4)
    ]
    return lax.ppermute(x, "nodes", moves)


def send_x_flip(x, bit):
    moves = [(4 * i + j, 4 * (i ^ bit) + j) for i in range(4) for j in range(4)]
    return lax.ppermute(x, "nodes", moves)


def pair_sum(one, other):
    return one.astype(F32) + other.astype(F32)


PARTNER = [(i, i ^ 1) for i in range(8)]


def send_y(x, step):
    return lax.ppermute(x, "cols", along_y(step))


def send_core(x):
    return lax.ppermute(x, "cols", PARTNER)


def add_terms(terms):
    own, one, two, three = (x.astype(F32) for x in terms)
    return (own + two) + (one + three)


def send_x(x, step):
    return send_node(x, step, 0)


def send_z(x, step):
    return send_node(x, 0, step)


def shards(node_feats, tile_row, tile_col, tile_bits, w_self, w_neigh, bias, cotangent):
    nodes = lax.axis_size("nodes")
    cols = lax.axis_size("cols")
    rows_dev, width = node_feats.shape
    me, node = lax.axis_index("cols"), lax.axis_index("nodes")
    y, core = me // 2, me % 2
    mine = jnp.stack([y, core, node // 4, node % 4]).astype(jnp.int32)
    theirs = jnp.stack([y, 1 - core, node // 4, node % 4]).astype(jnp.int32)

    top, low = prepare(node_feats)
    top = jnp.stack([top] + [send_x(top, k) for k in (1, 2, 3)])
    low = jnp.stack([low] + [send_z(low, k) for k in (1, 2, 3)])
    top, low, mine, theirs, zero = lax.optimization_barrier((top, low, mine, theirs, core == 0))
    planes = [top] + [send_z(top, k) for k in (1, 2, 3)]
    empty = cleared(low, nodes * rows_dev // 128, cols * rows_dev // 128)
    late, empty, third = lax.optimization_barrier((low, empty, send_x(low, 3)))
    planes += [low, send_x(late, 1), send_x(low, 2), third]
    fixed = [pltpu.with_memory_space_constraint(t, pltpu.HBM) for t in (tile_row, tile_col, tile_bits)]
    at, degree = build(*fixed, top, empty)

    give = forward(theirs, planes, at, degree, BF)
    taken = send_core(give)
    keep = forward(mine, planes, at, degree, F32)
    own, *sent = mix(keep, taken)
    far = send_y(sent[1], 2)
    got = [far, send_y(sent[0], 1), send_y(sent[2], 3)]
    layer_out, pre_grad, mean_t, mean_grad = middle(
        own, got, node_feats, w_self, w_neigh, bias.reshape(1, -1), cotangent
    )
    same_core = [mean_grad] + [send_y(mean_grad, k) for k in FAR_FIRST[1:]]

    part, self_part = weights(node_feats, pre_grad, mean_t, w_self)
    part = pair_sum(part, send_x_flip(part, 1)).astype(BF)
    other_core = [send_core(g) for g in same_core]
    flipped = send_x_flip(part, 2)

    src = backward(mine, same_core + other_core, at)
    src, part, flipped = lax.optimization_barrier((src, part, flipped))
    parts = swap(src.reshape(nodes, rows_dev, width), "nodes")

    part = pair_sum(part, flipped)
    halves = (part[:width], part[width : 2 * width])
    kept = jnp.concatenate([jnp.where(zero, *halves), part[2 * width :]])
    given = jnp.concatenate([jnp.where(zero, *halves[::-1]), part[2 * width :]])
    part = (kept + send_core(given)).astype(BF)
    part = add_terms([part] + [send_y(part, k) for k in (1, 2, 3)]).astype(BF)
    terms = [part] + [send_z(part, k) for k in (1, 2, 3)]

    feat_grad = finish(parts, self_part)
    feat_grad, terms = lax.optimization_barrier((feat_grad, terms))
    part = add_terms(terms)
    other = send_core(part)
    bias_grad = part[width]
    self_grad = jnp.where(zero, part[:width], other[:width])
    neigh_grad = jnp.where(zero, other[:width], part[:width])
    return (layer_out, feat_grad, self_grad, neigh_grad, bias_grad)


def solution(mesh):
    return jax.shard_map(
        shards,
        mesh=mesh,
        in_specs=(
            P(("nodes", "cols"), None),
            P("nodes", "cols"),
            P("nodes", "cols"),
            P("nodes", "cols", None, None),
            P(),
            P(),
            P(),
            P(("nodes", "cols"), None),
        ),
        out_specs=(P(("nodes", "cols"), None), P(("nodes", "cols"), None), P(), P(), P()),
        check_vma=False,
    )
```

```python
import jax
import jax.numpy as jnp
from jax import lax
from jax.experimental import pallas as pl
from jax.experimental.pallas import tpu as pltpu
from jax.sharding import PartitionSpec as P

BF = jnp.bfloat16
F32 = jnp.float32
EXACT = 256
EXTRA = 16
FAR_FIRST = (0, 2, 1, 3)


def params(mib):
    return pltpu.CompilerParams(vmem_limit_bytes=mib << 20)


def in_hbm(shape, kind):
    return pltpu.HBM(shape, kind)


def cost(flops, moved, transcendentals=0):
    return pl.CostEstimate(flops=flops, bytes_accessed=moved, transcendentals=transcendentals)


def prepare_kernel(x_ref, top_ref, low_ref):
    half = top_ref.shape[0]
    flipped = x_ref[...].T
    top_ref[...] = flipped[:half]
    low_ref[...] = flipped[half:]


def prepare(x):
    rows, width = x.shape
    shape = jax.ShapeDtypeStruct((width // 2, rows), BF)
    return pl.pallas_call(
        prepare_kernel,
        out_shape=(shape, shape),
        compiler_params=params(8),
        cost_estimate=cost(0, 1 << 18),
        name="prepare",
    )(x)


def build_kernel(
    rows_ref, cols_ref, bits_all, gate_ref, clear_ref, at_ref, deg_ref,
    deg8, count, spill, row_ref, col_ref, bits_ref, sems,
):
    sources = at_ref.shape[0] - 1
    dests = at_ref.shape[1]
    tiles = bits_ref.shape[0]
    pieces = 4
    each = tiles // pieces

    def fetch(k):
        part = pl.ds(k * each, each)
        return pltpu.make_async_copy(bits_all.at[0, part], bits_ref.at[part], sems.at[2 + k])

    copies = [
        pltpu.make_async_copy(rows_ref, row_ref, sems.at[0]),
        pltpu.make_async_copy(cols_ref, col_ref, sems.at[1]),
    ] + [fetch(k) for k in range(pieces)]
    for copy in copies:
        copy.start()
    for r in range(dests):
        deg8[r] = jnp.zeros((8, 128), F32)

    def clear(k, carry):
        for r in range(dests):
            count[k * dests + r] = 0
        return carry

    lax.fori_loop(0, sources, clear, 0)
    spill[0] = -1
    shifts = lax.broadcasted_iota(jnp.int32, (8, 128), 0)

    def add_tile(t, carry):
        row = row_ref[0, t]
        col = col_ref[0, t]
        slot = col * dests + row
        seen = count[slot]
        count[slot] = seen + 1
        full = seen >= EXACT
        spill[0] = jnp.where(full, slot, spill[0])
        to_col = jnp.where(full, sources, col)
        to_row = jnp.where(full, 0, row)
        total = None
        for i in range(8):
            flags = []
            for w in (2 * i, 2 * i + 1):
                word = jnp.broadcast_to(bits_ref[t, w : w + 1, :], (8, 128))
                flags.append((jnp.right_shift(word, shifts) & 1).astype(F32))
            pair = flags[0] + flags[1]
            total = pair if total is None else total + pair
            at_ref[to_col, to_row, 16 * i : 16 * i + 16, :] += jnp.concatenate(flags, 0).astype(BF)
        deg8[row] += total
        return carry

    copies[0].wait()
    copies[1].wait()
    for k in range(pieces):
        copies[2 + k].wait()
        lax.fori_loop(k * each, (k + 1) * each, add_tile, 0, unroll=4)

    @pl.when(spill[0] >= 0)
    def _():
        slot = spill[0]
        col = lax.div(slot, dests)
        row = lax.rem(slot, dests)
        whole = at_ref[col, row].astype(F32) + at_ref[sources, 0].astype(F32)
        at_ref[col, row] = whole.astype(BF)

    for r in range(dests):
        deg_ref[:, r * 128 : (r + 1) * 128] = jnp.sum(deg8[r], axis=0, keepdims=True)


def clear_kernel(gate_ref, at_ref):
    def clear(k, carry):
        for r in range(at_ref.shape[1]):
            at_ref[k, r] = jnp.zeros((128, 128), BF)
        return carry

    lax.fori_loop(0, at_ref.shape[0], clear, 0)


def cleared(gate, sources, dests):
    return pl.pallas_call(
        clear_kernel,
        out_shape=jax.ShapeDtypeStruct((sources + 1, dests, 128, 128), BF),
        in_specs=[pl.BlockSpec(memory_space=pl.ANY)],
        out_specs=pl.BlockSpec(memory_space=pltpu.VMEM),
        compiler_params=params(24),
        cost_estimate=cost(0, 8 << 20),
        name="clear",
    )(gate)


def build(rows, cols, bits, gate, at):
    sources, dests = at.shape[0] - 1, at.shape[1]
    tiles = bits.shape[1]
    assert tiles <= 2 * EXACT and tiles % 8 == 0
    hbm = pl.BlockSpec(memory_space=pltpu.HBM)
    vmem = pl.BlockSpec(memory_space=pltpu.VMEM)
    return pl.pallas_call(
        build_kernel,
        out_shape=(
            jax.ShapeDtypeStruct((sources + 1, dests, 128, 128), BF),
            jax.ShapeDtypeStruct((1, dests * 128), F32),
        ),
        in_specs=[hbm, hbm, hbm, pl.BlockSpec(memory_space=pl.ANY), vmem],
        out_specs=(vmem, vmem),
        scratch_shapes=[
            pltpu.VMEM((dests, 8, 128), F32),
            pltpu.SMEM((sources * dests,), jnp.int32),
            pltpu.SMEM((1,), jnp.int32),
            pltpu.SMEM((1, tiles), jnp.int32),
            pltpu.SMEM((1, tiles), jnp.int32),
            pltpu.VMEM((tiles, 16, 128), jnp.int32),
            pltpu.SemaphoreType.DMA((6,)),
        ],
        compiler_params=params(24),
        input_output_aliases={4: 0},
        cost_estimate=cost(0, 30 << 20),
        name="build",
    )(rows, cols, bits, gate, at)


def forward_kernel(place_ref, *refs):
    tops, lows = refs[:4], refs[4:8]
    at_ref, deg_ref, out_ref, joined = refs[8:]
    half, rows = tops[0].shape[1:]
    width = 2 * half
    per = rows // 128
    for kx in range(4):
        x = lax.rem(place_ref[2] + 4 - kx, 4)
        for kz in range(4):
            n = 4 * x + lax.rem(place_ref[3] + 4 - kz, 4)
            lanes = pl.ds(pl.multiple_of(n * rows, rows), rows)
            joined[0:half, lanes] = tops[kz][FAR_FIRST.index(kx)]
            joined[half:width, lanes] = lows[kx][FAR_FIRST.index(kz)]

    for j in range(4):
        chunk = 2 * lax.rem(place_ref[0] + j, 4) + place_ref[1]
        blocks = [
            jnp.concatenate([at_ref[k, per * chunk + r] for r in range(per)], axis=1)
            for k in range(at_ref.shape[0] - 1)
        ]
        part = jnp.dot(joined[...], jnp.concatenate(blocks, axis=0), preferred_element_type=F32)
        out_ref[j, 0:width, :] = part.astype(out_ref.dtype)
        whole = deg_ref[:, pl.ds(pl.multiple_of(chunk * rows, rows), rows)]
        degree = whole if out_ref.dtype == F32 else two_rows(whole)
        out_ref[j, width:, :] = spaced(degree, out_ref.dtype)


def two_rows(whole):
    high = whole.astype(BF).astype(F32)
    first = lax.broadcasted_iota(jnp.int32, (2, 1), 0) == 0
    return jnp.where(first, high, whole - high)


def spaced(rows, kind):
    count, width = rows.shape
    place = lax.broadcasted_iota(jnp.int32, (EXTRA, 1), 0)
    out = jnp.zeros((EXTRA, width), F32)
    for k in range(count):
        out = jnp.where(place == k, rows[k : k + 1, :], out)
    return out.astype(kind)


def forward(place, planes, at, degree, kind):
    _, half, rows = planes[0].shape
    width = 2 * half
    sources = at.shape[0] - 1
    vmem = pl.BlockSpec(memory_space=pltpu.VMEM)
    return pl.pallas_call(
        forward_kernel,
        out_shape=jax.ShapeDtypeStruct((4, width + EXTRA, rows), kind),
        in_specs=[pl.BlockSpec(memory_space=pltpu.SMEM)] + [vmem] * 10,
        out_specs=vmem,
        scratch_shapes=[pltpu.VMEM((width, sources * 128), BF)],
        compiler_params=params(20),
        cost_estimate=cost(8 * sources * 128 * rows * width, 10 << 20),
        name="forward",
    )(place, *planes, at, degree)


def backward_kernel(place_ref, *refs):
    parts, at_ref, out_ref, grads, held, sems = refs[:8], *refs[8:]
    rows = parts[0].shape[0]
    for spot, k in enumerate(FAR_FIRST):
        chunk = 2 * lax.rem(place_ref[0] + 4 - k, 4)
        own = pl.multiple_of((chunk + place_ref[1]) * rows, rows)
        other = pl.multiple_of((chunk + 1 - place_ref[1]) * rows, rows)
        grads[pl.ds(own, rows), :] = parts[spot][...]
        grads[pl.ds(other, rows), :] = parts[4 + spot][...]
    pieces, each, _ = held.shape

    def copy(i):
        into = out_ref.at[pl.ds(pl.multiple_of(i * each, each), each)]
        return pltpu.make_async_copy(held.at[i], into, sems.at[i])

    def piece(i, carry):
        for k in range(each // 128):
            at = i * (each // 128) + k
            block = jnp.concatenate([at_ref[at, r] for r in range(at_ref.shape[1])], axis=1)
            got = jnp.dot(block, grads[...], preferred_element_type=F32)
            held[i, k * 128 : (k + 1) * 128, :] = got.astype(BF)
        copy(i).start()
        return carry

    lax.fori_loop(0, pieces, piece, 0)
    for i in range(pieces):
        copy(i).wait()


def backward(place, parts, at):
    sources, dests = at.shape[0] - 1, at.shape[1]
    _, width = parts[0].shape
    pieces = 4
    vmem = pl.BlockSpec(memory_space=pltpu.VMEM)
    return pl.pallas_call(
        backward_kernel,
        out_shape=in_hbm((sources * 128, width), BF),
        in_specs=[pl.BlockSpec(memory_space=pltpu.SMEM)] + [vmem] * 9,
        out_specs=pl.BlockSpec(memory_space=pltpu.HBM),
        scratch_shapes=[
            pltpu.VMEM((dests * 128, width), BF),
            pltpu.VMEM((pieces, sources * 128 // pieces, width), BF),
            pltpu.SemaphoreType.DMA((pieces,)),
        ],
        compiler_params=params(20),
        cost_estimate=cost(2 * sources * 128 * dests * 128 * width, 20 << 20),
        name="backward",
    )(place, *parts, at)


def dot_on(a, b, da, db):
    return lax.dot_general(a, b, (((da,), (db,)), ((), ())), preferred_element_type=F32)


def mix_kernel(keep_ref, taken_ref, own_ref, *outs):
    width = own_ref.shape[0] - EXTRA
    own_ref[...] = keep_ref[0] + taken_ref[0].astype(F32)
    for k, out_ref in enumerate(outs):
        both = keep_ref[k + 1] + taken_ref[k + 1].astype(F32)
        out_ref[0:width, :] = both[0:width].astype(BF)
        degree = both[width : width + 1] + both[width + 1 : width + 2]
        out_ref[width:, :] = spaced(two_rows(degree), BF)


def mix(keep, taken):
    shape = keep.shape[1:]
    return pl.pallas_call(
        mix_kernel,
        out_shape=(jax.ShapeDtypeStruct(shape, F32),) + (jax.ShapeDtypeStruct(shape, BF),) * 3,
        compiler_params=params(16),
        cost_estimate=cost(1 << 18, 2 << 20),
        name="mix",
    )(keep, taken)


def middle_kernel(
    own_ref, r2_ref, r1_ref, r3_ref, x_ref, ws_ref, wn_ref, bias_ref, cot_ref,
    out_ref, pre_ref, mean_ref, grad_ref,
):
    width = x_ref.shape[1]
    summed = (own_ref[...] + r2_ref[...].astype(F32)) + (
        r1_ref[...].astype(F32) + r3_ref[...].astype(F32)
    )
    degree = jnp.maximum(summed[width : width + 1] + summed[width + 1 : width + 2], 1.0)
    summed = summed[0:width]
    mean_t = (summed / degree).astype(BF)
    mean_ref[...] = mean_t
    preact = (
        jnp.dot(x_ref[...], ws_ref[...], preferred_element_type=F32)
        + dot_on(mean_t, wn_ref[...], 0, 0)
        + bias_ref[...]
    )
    sig = 1.0 / (1.0 + jnp.exp(-preact))
    out_ref[...] = (preact * sig).astype(BF)
    pre_grad = (cot_ref[...].astype(F32) * sig * (1.0 + preact * (1.0 - sig))).astype(BF)
    pre_ref[...] = pre_grad
    grad_t = dot_on(wn_ref[...], pre_grad, 1, 1) / degree
    grad_ref[...] = grad_t.T.astype(BF)


def middle(own, got, x, ws, wn, bias, cot):
    n = x.shape[0]
    shape = jax.ShapeDtypeStruct((n, n), BF)
    return pl.pallas_call(
        middle_kernel,
        out_shape=(shape, shape, shape, shape),
        compiler_params=params(16),
        cost_estimate=cost(6 * n * n * n, 2 << 20, n * n),
        name="middle",
    )(own, *got, x, ws, wn, bias, cot)


def weights_kernel(x_ref, pre_ref, mean_ref, ws_ref, part_ref, self_ref):
    n = x_ref.shape[0]
    pre_grad = pre_ref[...]
    part_ref[0:n, :] = dot_on(x_ref[...], pre_grad, 0, 0).astype(BF)
    neigh_grad = jnp.dot(mean_ref[...], pre_grad, preferred_element_type=F32)
    part_ref[n : 2 * n, :] = neigh_grad.astype(BF)
    bias_grad = jnp.sum(pre_grad.astype(F32), axis=0, keepdims=True)
    part_ref[2 * n :, :] = spaced(bias_grad, BF)
    self_ref[...] = dot_on(pre_grad, ws_ref[...], 1, 1)


def weights(x, pre_grad, mean_t, ws):
    n = x.shape[0]
    return pl.pallas_call(
        weights_kernel,
        out_shape=(
            jax.ShapeDtypeStruct((2 * n + EXTRA, n), BF),
            jax.ShapeDtypeStruct((n, n), F32),
        ),
        compiler_params=params(16),
        cost_estimate=cost(6 * n * n * n, 2 << 20),
        name="weights",
    )(x, pre_grad, mean_t, ws)


def finish_kernel(parts_ref, self_ref, out_ref):
    total = self_ref[...]
    for k in range(parts_ref.shape[0]):
        total += parts_ref[k].astype(F32)
    out_ref[...] = total.astype(BF)


def finish(parts, self_part):
    return pl.pallas_call(
        finish_kernel,
        out_shape=jax.ShapeDtypeStruct(self_part.shape, BF),
        compiler_params=params(16),
        cost_estimate=cost(1 << 20, 2 << 20),
        name="finish",
    )(parts, self_part)


def swap(x, axis):
    return lax.all_to_all(x, axis, 0, 0, tiled=True)


def along_y(step):
    return [(2 * y + c, 2 * ((y + step) % 4) + c) for y in range(4) for c in range(2)]


def send_node(x, dx, dz):
    moves = [
        (4 * i + j, 4 * ((i + dx) % 4) + (j + dz) % 4) for i in range(4) for j in range(4)
    ]
    return lax.ppermute(x, "nodes", moves)


def send_x_flip(x, bit):
    moves = [(4 * i + j, 4 * (i ^ bit) + j) for i in range(4) for j in range(4)]
    return lax.ppermute(x, "nodes", moves)


def pair_sum(one, other):
    return one.astype(F32) + other.astype(F32)


PARTNER = [(i, i ^ 1) for i in range(8)]


def send_y(x, step):
    return lax.ppermute(x, "cols", along_y(step))


def send_core(x):
    return lax.ppermute(x, "cols", PARTNER)


def add_terms(terms):
    own, one, two, three = (x.astype(F32) for x in terms)
    return (own + two) + (one + three)


def send_x(x, step):
    return send_node(x, step, 0)


def send_z(x, step):
    return send_node(x, 0, step)


def shards(node_feats, tile_row, tile_col, tile_bits, w_self, w_neigh, bias, cotangent):
    nodes = lax.axis_size("nodes")
    cols = lax.axis_size("cols")
    rows_dev, width = node_feats.shape
    me, node = lax.axis_index("cols"), lax.axis_index("nodes")
    y, core = me // 2, me % 2
    mine = jnp.stack([y, core, node // 4, node % 4]).astype(jnp.int32)
    theirs = jnp.stack([y, 1 - core, node // 4, node % 4]).astype(jnp.int32)

    top, low = prepare(node_feats)
    top = jnp.stack([top] + [send_x(top, k) for k in FAR_FIRST[1:]])
    low = jnp.stack([low] + [send_z(low, k) for k in FAR_FIRST[1:]])
    top, low, mine, theirs, zero = lax.optimization_barrier((top, low, mine, theirs, core == 0))
    planes = [top] + [send_z(top, k) for k in (1, 2, 3)]
    empty = cleared(low, nodes * rows_dev // 128, cols * rows_dev // 128)
    late, empty, third = lax.optimization_barrier((low, empty, send_x(low, 3)))
    planes += [low, send_x(late, 1), send_x(low, 2), third]
    fixed = [pltpu.with_memory_space_constraint(t, pltpu.HBM) for t in (tile_row, tile_col, tile_bits)]
    at, degree = build(*fixed, top, empty)

    give = forward(theirs, planes, at, degree, BF)
    taken = send_core(give)
    keep = forward(mine, planes, at, degree, F32)
    own, *sent = mix(keep, taken)
    far = send_y(sent[1], 2)
    got = [far, send_y(sent[0], 1), send_y(sent[2], 3)]
    layer_out, pre_grad, mean_t, mean_grad = middle(
        own, got, node_feats, w_self, w_neigh, bias.reshape(1, -1), cotangent
    )
    same_core = [mean_grad] + [send_y(mean_grad, k) for k in FAR_FIRST[1:]]

    part, self_part = weights(node_feats, pre_grad, mean_t, w_self)
    part = pair_sum(part, send_x_flip(part, 1)).astype(BF)
    other_core = [send_core(g) for g in same_core]
    flipped = send_x_flip(part, 2)

    src = backward(mine, same_core + other_core, at)
    src, part, flipped = lax.optimization_barrier((src, part, flipped))
    parts = swap(src.reshape(nodes, rows_dev, width), "nodes")

    part = pair_sum(part, flipped)
    halves = (part[:width], part[width : 2 * width])
    kept = jnp.concatenate([jnp.where(zero, *halves), part[2 * width :]])
    given = jnp.concatenate([jnp.where(zero, *halves[::-1]), part[2 * width :]])
    part = (kept + send_core(given)).astype(BF)
    part = add_terms([part] + [send_y(part, k) for k in (1, 2, 3)]).astype(BF)
    terms = [part] + [send_z(part, k) for k in (1, 2, 3)]

    feat_grad = finish(parts, self_part)
    feat_grad, terms = lax.optimization_barrier((feat_grad, terms))
    part = add_terms(terms)
    other = send_core(part)
    bias_grad = part[width]
    self_grad = jnp.where(zero, part[:width], other[:width])
    neigh_grad = jnp.where(zero, other[:width], part[:width])
    return (layer_out, feat_grad, self_grad, neigh_grad, bias_grad)


def solution(mesh):
    return jax.shard_map(
        shards,
        mesh=mesh,
        in_specs=(
            P(("nodes", "cols"), None),
            P("nodes", "cols"),
            P("nodes", "cols"),
            P("nodes", "cols", None, None),
            P(),
            P(),
            P(),
            P(("nodes", "cols"), None),
        ),
        out_specs=(P(("nodes", "cols"), None), P(("nodes", "cols"), None), P(), P(), P()),
        check_vma=False,
    )
```
